256 devices in a mesh: seq: 32 (over x, z_hi, y), tp: 8 (over z_lo, core).
Axes of the slice: x: 4, y: 4, z: 8 (z_hi: 2, z_lo: 4; z = z_hi * 4 + z_lo), core: 2. Of those that a mesh axis runs over, the one named last changes fastest.
Arguments:
- residual: bfloat16 [4096, 1024], P(('seq', 'tp')), may hold values from -6 to 6
- queries: bfloat16 [2, 4096, 1024], P(None, 'seq', 'tp'), may hold values from -41 to 41
- keys: bfloat16 [2, 4096, 1024], P(None, 'seq', 'tp'), may hold values from -5.1 to 5.1
- values: bfloat16 [2, 4096, 1024], P(None, 'seq', 'tp'), may hold values from -6 to 6
- slopes: float32 [16], P('tp'), may hold values from 0.002 to 0.1
- out_weight: bfloat16 [1024, 1024], P('tp'), may hold values from -0.1875 to 0.1875
- cotangent: bfloat16 [4096, 1024], P(('seq', 'tp')), may hold values from -6 to 6
- far_blocks: int32 [32, 24], replicated, may hold values from -1 to 63, as said below
- far_count: int32 [32], replicated, may hold values from 8 to 24, as said below
Outputs:
- mixed: bfloat16 [4096, 1024], P(('seq', 'tp'))
- grad_queries: bfloat16 [2, 4096, 1024], P(None, 'seq', 'tp')
- grad_keys: bfloat16 [2, 4096, 1024], P(None, 'seq', 'tp')
- grad_values: bfloat16 [2, 4096, 1024], P(None, 'seq', 'tp')
The draws below stay inside these ranges and needn't reach their ends.
Inputs may be any that keep to these rules, and one draw needn't show every extreme that they name: `far_blocks`: row s holds, in its first far_count[s] entries, global key blocks of 64 positions on distinct shards, none of them on shard s - 1, s or s + 1; the remaining entries are -1. `far_count`: some shard lists exactly 24 blocks.
All inputs are finite; a program needn't handle non-finite values.
Results may differ from the reference program's by a relative error of at most 0.01.
Values may be sent and summed in bfloat16 or wider, within the bound.
No kernel may reach another device: no remote copies, remote signals or barrier semaphores. Data moves between devices by JAX's collectives and lax.ppermute only.
A program may use at most 128 MiB of HBM per device.

```python
import math
import jax
import jax.numpy as jnp
from jax import lax

HEADS = 16
HD = 64
BLK = 64
BAND = 2
S_DEV = 128
WIDTH = 1024
TOKENS = 4096
BPS = 2
NFAR = 24
N_SEQ = 32


def paired_fields(key):
    key_query, key_key = jax.random.split(jax.random.fold_in(key, 7), 2)
    shape = (2, TOKENS, WIDTH)
    query_field = jnp.clip(jax.random.normal(key_query, shape, jnp.float32), -5.0, 5.0)
    key_field = jnp.clip(jax.random.normal(key_key, shape, jnp.float32), -5.0, 5.0)
    return (query_field, key_field)


def draw_queries(key, part):
    return paired_fields(key)[0].astype(jnp.bfloat16)


def draw_keys(key, part):
    return paired_fields(key)[1].astype(jnp.bfloat16)


def contact_lists(key):
    key_order, key_block, key_count, key_top = jax.random.split(jax.random.fold_in(key, 11), 4)
    shard_ids = jnp.arange(N_SEQ, dtype=jnp.int32)
    ranks = jax.vmap(lambda one: jax.random.permutation(one, N_SEQ))(jax.random.split(key_order, N_SEQ)).astype(jnp.int32)
    near = (jnp.abs(shard_ids[None, :] - shard_ids[:, None]) <= 1).astype(jnp.int32)
    ranks = ranks + N_SEQ * near
    owners = jnp.argsort(ranks, axis=1, stable=True)[:, :NFAR].astype(jnp.int32)
    inner = jax.random.randint(key_block, (N_SEQ, NFAR), 0, BPS, dtype=jnp.int32)
    counts = jax.random.randint(key_count, (N_SEQ,), NFAR // 3, NFAR + 1, dtype=jnp.int32)
    busiest = jax.random.randint(key_top, (), 0, N_SEQ, dtype=jnp.int32)
    counts = jnp.where(shard_ids == busiest, NFAR, counts).astype(jnp.int32)
    live = jnp.arange(NFAR, dtype=jnp.int32)[None, :] < counts[:, None]
    lists = jnp.where(live, owners * BPS + inner, -1).astype(jnp.int32)
    return (lists, counts)


def draw_far_blocks(key, part):
    return contact_lists(key)[0]


def draw_far_count(key, part):
    return contact_lists(key)[1]


def levels(stream_key, dims, cuts, smallest, top_value):
    factor_of, own = 1.0, jax.random.fold_in(stream_key, 6)
    for axis_at, shards_of in cuts:
        heights = jnp.exp(jax.random.uniform(jax.random.fold_in(own, axis_at), (shards_of,), jnp.float32, smallest / len(cuts), top_value / len(cuts)))
        factor_of = factor_of * jnp.repeat(heights, dims[axis_at] // shards_of).reshape([-1 if axis == axis_at else 1 for axis in range(len(dims))])
    return factor_of


def centred(own_key, extent, width, bound, cuts=(), kind=jnp.bfloat16):
    factor_of = levels(own_key, extent, cuts, -0.22, 0.18) if cuts else 1.0
    drawn = jax.random.normal(own_key, extent, jnp.float32) * width * factor_of
    return jnp.minimum(jnp.maximum(drawn, -bound), bound).astype(kind)


def setup_inputs(seed: int = 0) -> dict:
    seeds = jax.random.split(jax.random.key(seed), 10)
    return {
        "residual": centred(seeds[0], (TOKENS, WIDTH), 1.0, 6.0, ((0, 256),)),
        "queries": draw_queries(jax.random.fold_in(seeds[9], 71), 0),
        "keys": draw_keys(jax.random.fold_in(seeds[9], 71), 0),
        "values": centred(seeds[3], (2, TOKENS, WIDTH), 1.0, 6.0, ((1, 32), (2, 8))),
        "slopes": jnp.clip(jnp.exp(math.log(0.1) - 3.912023 * jax.random.uniform(seeds[4], (HEADS,), jnp.float32) ** levels(seeds[4], (HEADS,), ((0, 8),), -0.2, 0.2)), 0.002, 0.1),
        "out_weight": centred(seeds[5], (WIDTH, WIDTH), WIDTH ** -0.5, 0.1875, ((0, 8),)),
        "cotangent": centred(seeds[6], (TOKENS, WIDTH), 1.0, 6.0, ((0, 256),)),
        "far_blocks": draw_far_blocks(jax.random.fold_in(seeds[9], 71), 0),
        "far_count": draw_far_count(jax.random.fold_in(seeds[9], 71), 0),
    }


masked_value = -1.0e30


def attend_shard(query_rows, key_rows, value_rows, grad_rows, allowed, distance, slopes):
    scale = HD ** -0.5
    query_three = query_rows.reshape(query_rows.shape[0], HEADS, HD).astype(jnp.float32)
    key_three = key_rows.reshape(key_rows.shape[0], HEADS, HD).astype(jnp.float32)
    value_three = value_rows.reshape(value_rows.shape[0], HEADS, HD).astype(jnp.float32)
    grad_three = grad_rows.reshape(grad_rows.shape[0], HEADS, HD).astype(jnp.float32)
    scores = jnp.einsum("shd,khd->hsk", query_three, key_three) * scale
    scores = scores - slopes[:, None, None] * distance[None]
    scores = jnp.where(allowed[None], scores, masked_value)
    row_max = jnp.max(scores, axis=-1, keepdims=True)
    weights_exp = jnp.exp(scores - row_max)
    probs = weights_exp / jnp.sum(weights_exp, axis=-1, keepdims=True)
    probs_low = lax.optimization_barrier(probs.astype(jnp.bfloat16)).astype(jnp.float32)
    context = jnp.einsum("hsk,khd->shd", probs_low, value_three)
    context = context.reshape(query_rows.shape[0], WIDTH).astype(jnp.bfloat16)
    grad_probs = jnp.einsum("shd,khd->hsk", grad_three, value_three)
    row_dot = jnp.sum(probs * grad_probs, axis=-1, keepdims=True)
    grad_score = (probs * (grad_probs - row_dot) * scale).astype(jnp.bfloat16)
    grad_score = lax.optimization_barrier(grad_score).astype(jnp.float32)
    grad_query = jnp.einsum("hsk,khd->shd", grad_score, key_three).reshape(query_rows.shape[0], WIDTH)
    grad_key = jnp.einsum("hsk,shd->khd", grad_score, query_three).reshape(key_rows.shape[0], WIDTH)
    grad_value = jnp.einsum("hsk,shd->khd", probs_low, grad_three).reshape(key_rows.shape[0], WIDTH)
    return context, grad_query, grad_key, grad_value


def reference(residual, queries, keys, values, slopes, out_weight, cotangent, far_blocks, far_count):
    halo_rows = BAND * BLK
    window_rows = S_DEV + 2 * halo_rows
    total_blocks = BPS * N_SEQ
    far_rows = NFAR * BLK
    block_lists = [far_blocks, (total_blocks - 1 - far_blocks[::-1]).astype(jnp.int32)]
    list_counts = [far_count, far_count[::-1]]
    grad_context = jnp.dot(cotangent, out_weight.T, preferred_element_type=jnp.float32).astype(jnp.bfloat16)
    grad_strands = [grad_context, jnp.flip(grad_context, 0)]
    contexts = []
    grads_q = []
    grads_k = []
    grads_v = []
    for strand in range(2):
        query_all = queries[strand]
        key_pad = jnp.pad(keys[strand], ((halo_rows, halo_rows), (0, 0)))
        value_pad = jnp.pad(values[strand], ((halo_rows, halo_rows), (0, 0)))
        key_blocks = keys[strand].reshape(total_blocks, BLK, WIDTH)
        value_blocks = values[strand].reshape(total_blocks, BLK, WIDTH)
        grad_full = grad_strands[strand]
        list_here = block_lists[strand]
        count_here = list_counts[strand]

        def shard_step(carry, shard):
            key_acc, value_acc = carry
            start = (shard * S_DEV).astype(jnp.int32)
            query_rows = lax.dynamic_slice_in_dim(query_all, start, S_DEV, 0)
            grad_rows = lax.dynamic_slice_in_dim(grad_full, start, S_DEV, 0)
            key_band = lax.dynamic_slice_in_dim(key_pad, start, window_rows, 0)
            value_band = lax.dynamic_slice_in_dim(value_pad, start, window_rows, 0)
            entries = list_here[shard]
            live = jnp.arange(NFAR, dtype=jnp.int32) < count_here[shard]
            clipped = jnp.where(live, entries, 0).astype(jnp.int32)
            key_far = jnp.take(key_blocks, clipped, axis=0).reshape(far_rows, WIDTH)
            value_far = jnp.take(value_blocks, clipped, axis=0).reshape(far_rows, WIDTH)
            key_rows = jnp.concatenate([key_band, key_far], axis=0)
            value_rows = jnp.concatenate([value_band, value_far], axis=0)
            query_pos = start + jnp.arange(S_DEV, dtype=jnp.int32)
            key_pos = start - halo_rows + jnp.arange(window_rows, dtype=jnp.int32)
            band_ok = (key_pos[None, :] >= 0) & (key_pos[None, :] < TOKENS)
            band_ok = band_ok & (jnp.abs(key_pos[None, :] // BLK - query_pos[:, None] // BLK) <= BAND)
            far_live = jnp.repeat(live, BLK)
            allowed = jnp.concatenate([band_ok, jnp.broadcast_to(far_live[None, :], (S_DEV, far_rows))], axis=1)
            band_dist = jnp.abs(query_pos[:, None] - key_pos[None, :]).astype(jnp.float32)
            far_dist = jnp.full((S_DEV, far_rows), float((BAND + 1) * BLK), jnp.float32)
            distance = jnp.concatenate([band_dist, far_dist], axis=1)
            context, grad_query, grad_key, grad_value = attend_shard(query_rows, key_rows, value_rows, grad_rows, allowed, distance, slopes)
            zero_index = jnp.zeros((), jnp.int32)
            key_acc = lax.dynamic_update_slice(key_acc, lax.dynamic_slice_in_dim(key_acc, start, window_rows, 0) + grad_key[:window_rows], (start, zero_index))
            value_acc = lax.dynamic_update_slice(value_acc, lax.dynamic_slice_in_dim(value_acc, start, window_rows, 0) + grad_value[:window_rows], (start, zero_index))
            far_index = (halo_rows + clipped[:, None] * BLK + jnp.arange(BLK, dtype=jnp.int32)[None, :]).reshape(-1)
            key_acc = key_acc.at[far_index].add(jnp.where(far_live[:, None], grad_key[window_rows:], 0.0))
            value_acc = value_acc.at[far_index].add(jnp.where(far_live[:, None], grad_value[window_rows:], 0.0))
            return (key_acc, value_acc), (context, grad_query)

        start_acc = (jnp.zeros((TOKENS + 2 * halo_rows, WIDTH), jnp.float32), jnp.zeros((TOKENS + 2 * halo_rows, WIDTH), jnp.float32))
        (key_acc, value_acc), (context_all, grad_query_all) = lax.scan(shard_step, start_acc, jnp.arange(N_SEQ, dtype=jnp.int32))
        contexts.append(context_all.reshape(TOKENS, WIDTH))
        grads_q.append(grad_query_all.reshape(TOKENS, WIDTH).astype(jnp.bfloat16))
        grads_k.append(key_acc[halo_rows:halo_rows + TOKENS].astype(jnp.bfloat16))
        grads_v.append(value_acc[halo_rows:halo_rows + TOKENS].astype(jnp.bfloat16))
    context_sum = (contexts[0].astype(jnp.float32) + jnp.flip(contexts[1], 0).astype(jnp.float32)).astype(jnp.bfloat16)
    mixed = (residual.astype(jnp.float32) + jnp.dot(context_sum, out_weight, preferred_element_type=jnp.float32)).astype(jnp.bfloat16)
    return mixed, jnp.stack(grads_q), jnp.stack(grads_k), jnp.stack(grads_v)
```

```python
import functools

import jax
import jax.numpy as jnp
from jax import lax
from jax.experimental import pallas as pl
from jax.experimental.pallas import tpu as pltpu
from jax.sharding import PartitionSpec as P

HD = 64
BLK = 64
BAND = 2

masked_value = -1e30
f32 = jnp.float32
bf16 = jnp.bfloat16

NT = (((1,), (1,)), ((), ()))
NN = (((1,), (0,)), ((), ()))


def dot(a, b, dims):
    return lax.dot_general(a, b, dims, preferred_element_type=f32)


def two_heads(x):
    first = lax.broadcasted_iota(jnp.int32, x.shape, 1) < HD
    zero = jnp.zeros_like(x)
    return jnp.concatenate([jnp.where(first, x, zero), jnp.where(first, zero, x)], axis=0)


def pick_heads(xt):
    rows = xt.shape[1] // 2
    own = jnp.concatenate([xt[:HD, :rows], xt[HD:, rows:]], axis=0)
    return own.T


def flipped(x):
    n = x.shape[0]
    there = lax.broadcasted_iota(jnp.int32, (n, n), 0) + lax.broadcasted_iota(jnp.int32, (n, n), 1)
    return dot((there == n - 1).astype(bf16), x, NN).astype(bf16)


def stage(meta, slot_ref, own_ref, prev_ref, next_ref, far_ref, kbuf, vbuf):
    for which, buf in ((0, kbuf), (1, vbuf)):
        buf[0:128] = prev_ref[which]
        buf[128:256] = own_ref[which]
        buf[256:384] = next_ref[which]
        for f in range(slot_ref.shape[0]):
            buf[384 + f * BLK : 384 + (f + 1) * BLK] = far_ref[slot_ref[f], which]


def biased(meta, slopes_ref, q2, kbuf, put):
    shard, shards, count = meta[0], meta[1], meta[2]
    cols = q2.shape[0]
    half = cols // 2
    head_col = lax.broadcasted_iota(jnp.int32, (1, cols), 1)
    slope = jnp.where(head_col < half, slopes_ref[0], slopes_ref[1])
    r = lax.broadcasted_iota(jnp.int32, (384, cols), 0)
    c = lax.broadcasted_iota(jnp.int32, (384, cols), 1)
    c = jnp.where(c < half, c, c - half)
    delta = r - 128 - c
    low = jnp.where(shard > 0, 0, 128)
    high = jnp.where(shard < shards - 1, 384, 256)
    edge = jnp.where(c < BLK, 0, BLK)
    ok = (r >= jnp.maximum(edge, low)) & (r < jnp.minimum(edge + 320, high))
    scores = dot(kbuf[0:384], q2, NT) - slope * jnp.abs(delta).astype(f32)
    scores = jnp.where(ok, scores, masked_value)
    put(0, 384, scores)
    top = jnp.max(scores, axis=0, keepdims=True)
    far_bias = slope * (-float((BAND + 1) * BLK))
    total = kbuf.shape[0]
    step = 384
    for lo in range(384, total, step):
        scores = dot(kbuf[lo : lo + step], q2, NT)
        parts = []
        for i in range(step // BLK):
            f = (lo - 384) // BLK + i
            row = jnp.where(f < count, far_bias, masked_value)
            parts.append(scores[i * BLK : (i + 1) * BLK] + row)
        scores = jnp.concatenate(parts, axis=0)
        put(lo, lo + step, scores)
        top = jnp.maximum(top, jnp.max(scores, axis=0, keepdims=True))
    return top


def forward_kernel(flip, meta, slot_ref, slopes_ref, q_ref, own_ref, prev_ref, next_ref, far_ref, ctx_ref, stat_ref, kbuf, vbuf, sbuf):
    stage(meta, slot_ref, own_ref, prev_ref, next_ref, far_ref, kbuf, vbuf)
    q2 = two_heads(q_ref[...] * HD ** (-0.5))

    def put(lo, hi, scores):
        sbuf[lo:hi] = scores

    top = biased(meta, slopes_ref, q2, kbuf, put)
    total = kbuf.shape[0]
    norm = jnp.zeros_like(top)
    for lo in range(0, total, 384):
        w = jnp.exp(sbuf[lo : lo + 384] - top)
        sbuf[lo : lo + 384] = w
        norm = norm + jnp.sum(w, axis=0, keepdims=True)
    inv = 1.0 / norm
    stat_ref[0:1] = top
    stat_ref[1:2] = inv
    n = 2 * HD
    eye = (lax.broadcasted_iota(jnp.int32, (n, n), 0) == lax.broadcasted_iota(jnp.int32, (n, n), 1)).astype(bf16)
    acc = jnp.zeros((n, q2.shape[0]), f32)
    for lo in range(0, total, 384):
        low = (sbuf[lo : lo + 384] * inv).astype(bf16)
        vt = dot(eye, vbuf[lo : lo + 384], NT).astype(bf16)
        acc = acc + dot(vt, low, NN)
    ctx = pick_heads(acc).astype(bf16)
    ctx_ref[...] = flipped(ctx) if flip else ctx


def backward_kernel(
    flip, meta, slot_ref, slopes_ref, q_ref, own_ref, prev_ref, next_ref, far_ref, stat_ref, grad_ref,
    gq_ref, own_out, prev_out, next_out, far_out, kbuf, vbuf, pbuf, gbuf,
):
    stage(meta, slot_ref, own_ref, prev_ref, next_ref, far_ref, kbuf, vbuf)
    q2 = two_heads(q_ref[...] * HD ** (-0.5))
    grad = grad_ref[...]
    g2 = two_heads(flipped(grad) if flip else grad)
    total = kbuf.shape[0]
    cols = q2.shape[0]
    top = stat_ref[0:1]
    inv = stat_ref[1:2]

    def put(lo, hi, scores):
        pbuf[lo:hi] = jnp.exp(scores - top) * inv

    biased(meta, slopes_ref, q2, kbuf, put)
    row_dot = jnp.zeros((1, cols), f32)
    for lo in range(0, total, 384):
        gp = dot(vbuf[lo : lo + 384], g2, NT)
        gbuf[lo : lo + 384] = gp
        row_dot = row_dot + jnp.sum(pbuf[lo : lo + 384] * gp, axis=0, keepdims=True)
    n = 2 * HD
    eye = (lax.broadcasted_iota(jnp.int32, (n, n), 0) == lax.broadcasted_iota(jnp.int32, (n, n), 1)).astype(bf16)
    acc = jnp.zeros((n, cols), f32)
    for lo in range(0, total, 384):
        p = pbuf[lo : lo + 384]
        ds = (p * (gbuf[lo : lo + 384] - row_dot)).astype(bf16)
        kt = dot(eye, kbuf[lo : lo + 384], NT).astype(bf16)
        acc = acc + dot(kt, ds, NN)
        for which, x in ((0, dot(ds, q2, NN)), (1, dot(p.astype(bf16), g2, NN))):
            if lo == 0:
                prev_out[which] = x[0:128].astype(bf16)
                own_out[which] = x[128:256]
                next_out[which] = x[256:384].astype(bf16)
            else:
                low = x.astype(bf16)
                for i in range(384 // BLK):
                    f = (lo - 384) // BLK + i

                    @pl.when(f < meta[2])
                    def _():
                        far_out[slot_ref[f], which] = low[i * BLK : (i + 1) * BLK]

    gq_ref[...] = (pick_heads(acc) * HD ** (-0.5)).astype(bf16)


def combine_kernel(blk_ref, own_ref, prev_ref, next_ref, far_ref, out_ref):
    for t in range(2):
        for which in range(2):
            for lo in range(0, BLK, 32):
                first = jnp.zeros((32, 2 * HD), f32)
                second = jnp.zeros((32, 2 * HD), f32)
                for d in range(far_ref[0].shape[0]):
                    x = far_ref[t][d, which, lo : lo + 32].astype(f32)
                    first = first + jnp.where(blk_ref[t, d] == 0, x, 0.0)
                    second = second + jnp.where(blk_ref[t, d] == 1, x, 0.0)
                for at, far in ((lo, first), (BLK + lo, second)):
                    rows = slice(at, at + 32)
                    total = own_ref[t][which, rows] + prev_ref[t, which, rows].astype(f32)
                    total = total + next_ref[t, which, rows].astype(f32)
                    out_ref[which, t, rows] = (total + far).astype(bf16)


def smem():
    return pl.BlockSpec(memory_space=pltpu.SMEM)


def vmem():
    return pl.BlockSpec(memory_space=pltpu.VMEM)


def per_device(
    residual, queries, keys, values, slopes, out_weight, cotangent, far_blocks, far_count
):
    seq_count = lax.axis_size("seq")
    tp_count = lax.axis_size("tp")
    seq_index = lax.axis_index("seq")
    tok_rows = queries.shape[1]
    width_here = queries.shape[2]
    per_shard = tok_rows // BLK
    total_blocks = per_shard * seq_count
    nfar = far_blocks.shape[1]
    total_keys = 3 * tok_rows + nfar * BLK
    model = out_weight.shape[1]

    block_lists = jnp.stack([far_blocks, total_blocks - 1 - far_blocks[::-1]])
    list_counts = jnp.stack([far_count, far_count[::-1]])
    listed_ok = jnp.arange(nfar)[None, None, :] < list_counts[:, :, None]
    owners = jnp.where(listed_ok, block_lists // per_shard, -1)
    asked_me = owners == seq_index
    asked_block = jnp.sum(jnp.where(asked_me, block_lists % per_shard + 1, 0), axis=2) - 1
    mine = jnp.maximum(jnp.take(owners, seq_index, axis=1), 0).astype(jnp.int32)
    counts = jnp.take(list_counts, seq_index, axis=1).astype(jnp.int32)

    key_value = jnp.stack([keys, values], axis=1)
    blocks = key_value.reshape(2, 2, per_shard, BLK, width_here)

    def far_of(t):
        second = (asked_block[t] == 1)[:, None, None, None]
        outgoing = jnp.where(second, blocks[t, :, 1][None], blocks[t, :, 0][None])
        return lax.all_to_all(outgoing, "seq", split_axis=0, concat_axis=0, tiled=True)

    far = [far_of(0), far_of(1)]
    up = [(i, i + 1) for i in range(seq_count - 1)]
    down = [(j, i) for i, j in up]
    from_prev = lax.ppermute(key_value, "seq", up)
    from_next = lax.ppermute(key_value, "seq", down)

    mirror = [(i, seq_count - 1 - i) for i in range(seq_count)]
    copies = jnp.broadcast_to(cotangent[None], (tp_count,) + cotangent.shape)
    cot_rows = lax.all_to_all(copies, "tp", split_axis=0, concat_axis=0, tiled=True)
    grad_context = lax.dot_general(
        cot_rows.reshape(tok_rows, model), out_weight, NT, preferred_element_type=f32
    ).astype(bf16)
    grads = [grad_context, lax.ppermute(grad_context, "seq", mirror)]

    metas = [
        jnp.stack([seq_index, seq_count, counts[t]]).astype(jnp.int32) for t in range(2)
    ]
    square = jax.ShapeDtypeStruct((tok_rows, width_here), bf16)
    pair = (2, tok_rows, width_here)
    cols = 2 * tok_rows

    def forward(t):
        return pl.pallas_call(
            functools.partial(forward_kernel, t == 1),
            out_shape=(square, jax.ShapeDtypeStruct((2, cols), f32)),
            in_specs=[smem()] * 3 + [vmem()] * 5,
            out_specs=(vmem(), vmem()),
            scratch_shapes=[
                pltpu.VMEM((total_keys, width_here), bf16),
                pltpu.VMEM((total_keys, width_here), bf16),
                pltpu.VMEM((total_keys, cols), f32),
            ],
            cost_estimate=pl.CostEstimate(flops=800_000_000, bytes_accessed=2_000_000, transcendentals=500_000),
            name="attend_forward",
        )(metas[t], mine[t], slopes, queries[t], key_value[t], from_prev[t], from_next[t], far[t])

    def backward(t, stats):
        return pl.pallas_call(
            functools.partial(backward_kernel, t == 1),
            out_shape=(
                square,
                jax.ShapeDtypeStruct(pair, f32),
                jax.ShapeDtypeStruct(pair, bf16),
                jax.ShapeDtypeStruct(pair, bf16),
                jax.ShapeDtypeStruct((seq_count, 2, BLK, width_here), bf16),
            ),
            in_specs=[smem()] * 3 + [vmem()] * 7,
            out_specs=(vmem(),) * 5,
            scratch_shapes=[
                pltpu.VMEM((total_keys, width_here), bf16),
                pltpu.VMEM((total_keys, width_here), bf16),
                pltpu.VMEM((total_keys, cols), f32),
                pltpu.VMEM((total_keys, cols), f32),
            ],
            cost_estimate=pl.CostEstimate(flops=1_600_000_000, bytes_accessed=4_000_000, transcendentals=500_000),
            name="attend_backward",
        )(metas[t], mine[t], slopes, queries[t], key_value[t], from_prev[t], from_next[t], far[t], stats, grads[t])

    context_fwd, stats_fwd = forward(0)
    context_rev, stats_rev = forward(1)
    context_back = lax.ppermute(context_rev, "seq", mirror)

    gq0, own0, prev0, next0, far0 = backward(0, stats_fwd)
    back0 = lax.all_to_all(far0, "seq", split_axis=0, concat_axis=0, tiled=True)
    gq1, own1, prev1, next1, far1 = backward(1, stats_rev)
    back1 = lax.all_to_all(far1, "seq", split_axis=0, concat_axis=0, tiled=True)

    context_sum = (context_fwd.astype(f32) + context_back.astype(f32)).astype(bf16)
    partial = jnp.dot(context_sum, out_weight, preferred_element_type=f32).astype(bf16)
    pieces = lax.all_to_all(
        partial.reshape(tp_count, tok_rows // tp_count, model), "tp", split_axis=0, concat_axis=0, tiled=True
    )
    mixed = (residual.astype(f32) + jnp.sum(pieces.astype(f32), axis=0)).astype(bf16)

    to_owner_next = lax.ppermute(jnp.stack([next0, next1]), "seq", up)
    to_owner_prev = lax.ppermute(jnp.stack([prev0, prev1]), "seq", down)
    totals = pl.pallas_call(
        lambda b, o0, o1, p, n, f0, f1, out: combine_kernel(b, (o0, o1), p, n, (f0, f1), out),
        out_shape=jax.ShapeDtypeStruct((2,) + pair, bf16),
        in_specs=[smem()] + [vmem()] * 6,
        out_specs=vmem(),
        cost_estimate=pl.CostEstimate(flops=4_000_000, bytes_accessed=3_000_000, transcendentals=0),
        name="combine",
    )(asked_block, own0, own1, to_owner_next, to_owner_prev, back0, back1)
    return (mixed, jnp.stack([gq0, gq1]), totals[0], totals[1])


def solution(mesh):
    return jax.shard_map(
        per_device,
        mesh=mesh,
        in_specs=(
            P(("seq", "tp"), None),
            P(None, "seq", "tp"),
            P(None, "seq", "tp"),
            P(None, "seq", "tp"),
            P("tp"),
            P("tp", None),
            P(("seq", "tp"), None),
            P(),
            P(),
        ),
        out_specs=(
            P(("seq", "tp"), None),
            P(None, "seq", "tp"),
            P(None, "seq", "tp"),
            P(None, "seq", "tp"),
        ),
        check_vma=False,
    )
```

```python
import jax
import jax.numpy as jnp
from jax import lax
from jax.experimental import pallas as pl
from jax.experimental.pallas import tpu as pltpu
from jax.sharding import PartitionSpec as P

HD = 64
BLK = 64
BAND = 2
STEP = 384
LIMIT = 24 << 20

masked_value = -1e30
f32 = jnp.float32
bf16 = jnp.bfloat16

NT = (((1,), (1,)), ((), ()))
NN = (((1,), (0,)), ((), ()))


def dot(a, b, dims):
    return lax.dot_general(a, b, dims, preferred_element_type=f32)


def two_heads(x):
    first = lax.broadcasted_iota(jnp.int32, x.shape, 1) < HD
    zero = jnp.zeros_like(x)
    return jnp.concatenate([jnp.where(first, x, zero), jnp.where(first, zero, x)], axis=0)


def pick_heads(xt):
    rows = xt.shape[1] // 2
    own = jnp.concatenate([xt[:HD, :rows], xt[HD:, rows:]], axis=0)
    return own.T


def one_hot(n, at):
    r = lax.broadcasted_iota(jnp.int32, (n, n), 0)
    c = lax.broadcasted_iota(jnp.int32, (n, n), 1)
    return (c == at(r)).astype(bf16)


def flipped(x):
    n = x.shape[0]
    return dot(one_hot(n, lambda r: n - 1 - r), x, NN).astype(bf16)


def place():
    return lax.axis_index("seq"), lax.axis_size("seq")


def listed(fb_ref, t, shard, shards, f):
    entry = fb_ref[shard if t == 0 else shards - 1 - shard, f]
    owner = lax.shift_right_arithmetic(entry, 1)
    owner = owner if t == 0 else shards - 1 - owner
    return entry >= 0, jnp.where(entry >= 0, owner, 0)


def asked_of(fb, t, shard, shards):
    mine = shard if t == 0 else shards - 1 - shard
    inner = fb & 1
    inner = inner + 1 if t == 0 else 2 - inner
    hit = jnp.where(lax.shift_right_arithmetic(fb, 1) == mine, inner, 0)
    return jnp.sum(hit, axis=1, keepdims=True)


def pack_kernel(fb_ref, key_ref, value_ref, out_ref, kv_ref):
    shard, shards = place()
    fb = fb_ref[...]
    for which, ref in ((0, key_ref), (1, value_ref)):
        kv_ref[:, which] = ref[...]
    for t in range(2):
        asked = jnp.broadcast_to(asked_of(fb, t, shard, shards), (shards, 2 * HD))
        for d in range(shards):
            row = d if t == 0 else shards - 1 - d
            second = jnp.broadcast_to(asked[row : row + 1] == 2, (BLK, 2 * HD))
            for which, ref in ((0, key_ref), (1, value_ref)):
                out_ref[d, t, which] = jnp.where(second, ref[t, BLK:], ref[t, :BLK])


def stage(fb_ref, t, kv_ref, prev_ref, next_ref, far_ref, kbuf, vbuf):
    shard, shards = place()
    for which, buf in ((0, kbuf), (1, vbuf)):
        buf[0:128] = prev_ref[t, which]
        buf[128:256] = kv_ref[t, which]
        buf[256:384] = next_ref[t, which]
    for f in range(fb_ref.shape[1]):
        _, slot = listed(fb_ref, t, shard, shards, f)
        rows = slice(STEP + f * BLK, STEP + (f + 1) * BLK)
        kbuf[rows] = far_ref[slot, t, 0]
        vbuf[rows] = far_ref[slot, t, 1]


def biased(fb_ref, t, slopes_ref, q2, kbuf, put):
    shard, shards = place()
    cols = q2.shape[0]
    half = cols // 2
    head_col = lax.broadcasted_iota(jnp.int32, (1, cols), 1)
    slope = jnp.where(head_col < half, slopes_ref[0], slopes_ref[1])
    r = lax.broadcasted_iota(jnp.int32, (STEP, cols), 0)
    c = lax.broadcasted_iota(jnp.int32, (STEP, cols), 1)
    c = jnp.where(c < half, c, c - half)
    delta = r - 128 - c
    low = jnp.where(shard > 0, 0, 128)
    high = jnp.where(shard < shards - 1, STEP, 256)
    edge = jnp.where(c < BLK, 0, BLK)
    ok = (r >= jnp.maximum(edge, low)) & (r < jnp.minimum(edge + 320, high))
    scores = dot(kbuf[0:STEP], q2, NT) - slope * jnp.abs(delta).astype(f32)
    scores = jnp.where(ok, scores, masked_value)
    put(0, STEP, scores)
    top = jnp.max(scores, axis=0, keepdims=True)
    far_bias = slope * (-float((BAND + 1) * BLK))
    for lo in range(STEP, kbuf.shape[0], STEP):
        scores = dot(kbuf[lo : lo + STEP], q2, NT)
        parts = []
        for i in range(STEP // BLK):
            there, _ = listed(fb_ref, t, shard, shards, (lo - STEP) // BLK + i)
            row = jnp.where(there, far_bias, masked_value)
            parts.append(scores[i * BLK : (i + 1) * BLK] + row)
        scores = jnp.concatenate(parts, axis=0)
        put(lo, lo + STEP, scores)
        top = jnp.maximum(top, jnp.max(scores, axis=0, keepdims=True))
    return top


def forward_kernel(fb_ref, slopes_ref, q_ref, kv_ref, prev_ref, next_ref, far_ref, ctx_ref, rev_ref, stat_ref, kbuf, vbuf, sbuf):
    n = 2 * HD
    eye = one_hot(n, lambda r: r)
    total = kbuf.shape[0]
    for t in (1, 0):
        stage(fb_ref, t, kv_ref, prev_ref, next_ref, far_ref, kbuf, vbuf)
        q2 = two_heads(q_ref[t] * HD ** (-0.5))

        def put(lo, hi, scores):
            sbuf[lo:hi] = scores

        top = biased(fb_ref, t, slopes_ref, q2, kbuf, put)
        norm = jnp.zeros_like(top)
        for lo in range(0, total, STEP):
            w = jnp.exp(sbuf[lo : lo + STEP] - top)
            sbuf[lo : lo + STEP] = w
            norm = norm + jnp.sum(w, axis=0, keepdims=True)
        inv = 1.0 / norm
        stat_ref[t, 0:1] = top
        stat_ref[t, 1:2] = inv
        acc = jnp.zeros((n, q2.shape[0]), f32)
        for lo in range(0, total, STEP):
            low = (sbuf[lo : lo + STEP] * inv).astype(bf16)
            vt = dot(eye, vbuf[lo : lo + STEP], NT).astype(bf16)
            acc = acc + dot(vt, low, NN)
        ctx = pick_heads(acc).astype(bf16)
        if t == 1:
            rev_ref[...] = flipped(ctx)
        else:
            ctx_ref[...] = ctx


def reorder(x_ref, out_ref):
    at = lax.axis_index("tp")
    count = lax.axis_size("tp")
    rows = out_ref.shape[0] // count
    for k in range(count):
        out_ref[k * rows : (k + 1) * rows] = x_ref[lax.bitwise_xor(at, k)]


def backward_kernel(
    fb_ref, slopes_ref, q_ref, kv_ref, prev_ref, next_ref, far_ref, stat_ref, grad_ref, mirrored_ref,
    gq_ref, own_out, prev_out, next_out, far_out, kbuf, vbuf, pbuf, dbuf, rows_buf,
):
    shard, shards = place()
    n = 2 * HD
    eye = one_hot(n, lambda r: r)
    total = kbuf.shape[0]
    for t in range(2):
        stage(fb_ref, t, kv_ref, prev_ref, next_ref, far_ref, kbuf, vbuf)
        q2 = two_heads(q_ref[t] * HD ** (-0.5))
        reorder((grad_ref, mirrored_ref)[t], rows_buf)
        grad = rows_buf[...]
        g2 = two_heads(flipped(grad) if t == 1 else grad)
        cols = q2.shape[0]
        top = stat_ref[t, 0:1]
        inv = stat_ref[t, 1:2]

        def put(lo, hi, scores):
            pbuf[lo:hi] = jnp.exp(scores - top) * inv

        biased(fb_ref, t, slopes_ref, q2, kbuf, put)
        row_dot = jnp.zeros((1, cols), f32)
        for lo in range(0, total, STEP):
            gp = dot(vbuf[lo : lo + STEP], g2, NT)
            dbuf[lo : lo + STEP] = gp
            row_dot = row_dot + jnp.sum(pbuf[lo : lo + STEP] * gp, axis=0, keepdims=True)
        acc = jnp.zeros((n, cols), f32)
        for lo in range(0, total, STEP):
            p = pbuf[lo : lo + STEP]
            ds = (p * (dbuf[lo : lo + STEP] - row_dot)).astype(bf16)
            kt = dot(eye, kbuf[lo : lo + STEP], NT).astype(bf16)
            acc = acc + dot(kt, ds, NN)
            for which, x in ((0, dot(ds, q2, NN)), (1, dot(p.astype(bf16), g2, NN))):
                if lo == 0:
                    prev_out[t, which] = x[0:128].astype(bf16)
                    own_out[t, which] = x[128:256]
                    next_out[t, which] = x[256:384].astype(bf16)
                else:
                    low = x.astype(bf16)
                    for i in range(STEP // BLK):
                        there, slot = listed(fb_ref, t, shard, shards, (lo - STEP) // BLK + i)

                        @pl.when(there)
                        def _():
                            far_out[slot, t, which] = low[i * BLK : (i + 1) * BLK]

        gq_ref[t] = (pick_heads(acc) * HD ** (-0.5)).astype(bf16)


def combine_kernel(fb_ref, own_ref, prev_ref, next_ref, far_ref, gk_ref, gv_ref):
    shard, shards = place()
    fb = fb_ref[...]
    rows = 32
    for t in range(2):
        asked = jnp.broadcast_to(asked_of(fb, t, shard, shards), (shards, 2 * HD))
        for which, out_ref in ((0, gk_ref), (1, gv_ref)):
            for lo in range(0, BLK, rows):
                first = jnp.zeros((rows, 2 * HD), f32)
                second = jnp.zeros((rows, 2 * HD), f32)
                for d in range(shards):
                    row = d if t == 0 else shards - 1 - d
                    block = jnp.broadcast_to(asked[row : row + 1], (rows, 2 * HD))
                    x = far_ref[d, t, which, lo : lo + rows].astype(f32)
                    first = first + jnp.where(block == 1, x, 0.0)
                    second = second + jnp.where(block == 2, x, 0.0)
                for at, far in ((lo, first), (BLK + lo, second)):
                    here = slice(at, at + rows)
                    total = own_ref[t, which, here] + prev_ref[t, which, here].astype(f32)
                    total = total + next_ref[t, which, here].astype(f32)
                    out_ref[t, here] = (total + far).astype(bf16)


def project_kernel(ctx_ref, back_ref, weight_ref, out_ref, sum_buf):
    total = (ctx_ref[...].astype(f32) + back_ref[...].astype(f32)).astype(bf16)
    count, rows, _ = out_ref.shape
    for k in range(count):
        sum_buf[k] = total[k * rows : (k + 1) * rows]
    at = lax.axis_index("tp")
    for j in range(count):
        out_ref[j] = dot(sum_buf[lax.bitwise_xor(at, j)], weight_ref[...], NN)


def smem():
    return pl.BlockSpec(memory_space=pltpu.SMEM)


def vmem():
    return pl.BlockSpec(memory_space=pltpu.VMEM)


def shape(dims, dtype=bf16):
    return jax.ShapeDtypeStruct(dims, dtype)


def cost(flops, nbytes, exps=0):
    return pl.CostEstimate(flops=flops, bytes_accessed=nbytes, transcendentals=exps)


def swap(x, bit):
    count = lax.axis_size("tp")
    return lax.ppermute(x, "tp", [(i, i ^ bit) for i in range(count)])


def per_device(
    residual, queries, keys, values, slopes, out_weight, cotangent, far_blocks, far_count
):
    seq_count = lax.axis_size("seq")
    tp_count = lax.axis_size("tp")
    tok_rows, width = queries.shape[1:]
    total_keys = 3 * tok_rows + far_blocks.shape[1] * BLK
    model = out_weight.shape[1]
    cols = 2 * tok_rows
    both = (2, 2, tok_rows, width)
    slots = (seq_count, 2, 2, BLK, width)

    outgoing, key_value = pl.pallas_call(
        pack_kernel,
        out_shape=(shape(slots), shape(both)),
        in_specs=[vmem()] * 3,
        out_specs=(vmem(), vmem()),
        cost_estimate=cost(1_000_000, 2_500_000),
        compiler_params=pltpu.CompilerParams(vmem_limit_bytes=LIMIT),
        name="pack",
    )(far_blocks, keys, values)
    far = lax.all_to_all(outgoing, "seq", split_axis=0, concat_axis=0, tiled=True)

    up = [(i, i + 1) for i in range(seq_count - 1)]
    down = [(j, i) for i, j in up]
    mirror = [(i, seq_count - 1 - i) for i in range(seq_count)]
    from_prev = lax.ppermute(key_value, "seq", up)
    from_next = lax.ppermute(key_value, "seq", down)

    gathered = cotangent[None]
    for bit in (1, 2, 4):
        gathered = jnp.concatenate([gathered, swap(gathered, bit)], axis=0)
    grad_context = dot(gathered.reshape(tok_rows, model), out_weight, NT).astype(bf16)
    mirrored = lax.ppermute(grad_context, "seq", mirror)
    pieces = (tp_count, tok_rows // tp_count, width)

    keyed = [pltpu.VMEM((total_keys, width), bf16), pltpu.VMEM((total_keys, width), bf16)]
    context_fwd, context_rev, stats = pl.pallas_call(
        forward_kernel,
        out_shape=(shape((tok_rows, width)), shape((tok_rows, width)), shape((2, 2, cols), f32)),
        in_specs=[smem()] * 2 + [vmem()] * 5,
        out_specs=(vmem(),) * 3,
        scratch_shapes=keyed + [pltpu.VMEM((total_keys, cols), f32)],
        cost_estimate=cost(1_600_000_000, 4_000_000, 1_000_000),
        compiler_params=pltpu.CompilerParams(vmem_limit_bytes=LIMIT),
        name="attend_forward",
    )(far_blocks, slopes, queries, key_value, from_prev, from_next, far)
    context_back = lax.ppermute(context_rev, "seq", mirror)

    grad_queries, own, before, after, far_grads = pl.pallas_call(
        backward_kernel,
        out_shape=(shape((2, tok_rows, width)), shape(both, f32), shape(both), shape(both), shape(slots)),
        in_specs=[smem()] * 2 + [vmem()] * 8,
        out_specs=(vmem(),) * 5,
        scratch_shapes=keyed
        + [pltpu.VMEM((total_keys, cols), f32)] * 2
        + [pltpu.VMEM((tok_rows, width), bf16)],
        cost_estimate=cost(3_200_000_000, 8_000_000, 1_000_000),
        compiler_params=pltpu.CompilerParams(vmem_limit_bytes=LIMIT),
        name="attend_backward",
    )(
        far_blocks, slopes, queries, key_value, from_prev, from_next, far, stats,
        grad_context.reshape(pieces), mirrored.reshape(pieces),
    )
    returned = lax.all_to_all(far_grads, "seq", split_axis=0, concat_axis=0, tiled=True)
    from_prev_grad = lax.ppermute(after, "seq", up)
    from_next_grad = lax.ppermute(before, "seq", down)

    partial = pl.pallas_call(
        project_kernel,
        out_shape=shape((tp_count, tok_rows // tp_count, model), f32),
        in_specs=[vmem()] * 3,
        out_specs=vmem(),
        scratch_shapes=[pltpu.VMEM(pieces, bf16)],
        cost_estimate=cost(34_000_000, 1_000_000),
        compiler_params=pltpu.CompilerParams(vmem_limit_bytes=LIMIT),
        name="project",
    )(context_fwd, context_back, out_weight)
    held = partial
    for bit in (4, 2, 1):
        held = held[:bit] + swap(held[bit:].astype(bf16), bit).astype(f32)
    mixed = (residual.astype(f32) + held[0]).astype(bf16)

    grad_keys, grad_values = pl.pallas_call(
        combine_kernel,
        out_shape=(shape((2, tok_rows, width)),) * 2,
        in_specs=[vmem()] * 5,
        out_specs=(vmem(),) * 2,
        cost_estimate=cost(4_000_000, 3_000_000),
        compiler_params=pltpu.CompilerParams(vmem_limit_bytes=LIMIT),
        name="combine",
    )(far_blocks, own, from_prev_grad, from_next_grad, returned)
    return (mixed, grad_queries, grad_keys, grad_values)


def solution(mesh):
    return jax.shard_map(
        per_device,
        mesh=mesh,
        in_specs=(
            P(("seq", "tp"), None),
            P(None, "seq", "tp"),
            P(None, "seq", "tp"),
            P(None, "seq", "tp"),
            P("tp"),
            P("tp", None),
            P(("seq", "tp"), None),
            P(),
            P(),
        ),
        out_specs=(
            P(("seq", "tp"), None),
            P(None, "seq", "tp"),
            P(None, "seq", "tp"),
            P(None, "seq", "tp"),
        ),
        check_vma=False,
    )
```

```python
import jax
import jax.numpy as jnp
from jax import lax
from jax.experimental import pallas as pl
from jax.experimental.pallas import tpu as pltpu
from jax.sharding import PartitionSpec as P

HD = 64
BLK = 64
BAND = 2
STEP = 384
LIMIT = 24 << 20

masked_value = -1e30
f32 = jnp.float32
bf16 = jnp.bfloat16

NT = (((1,), (1,)), ((), ()))
NN = (((1,), (0,)), ((), ()))


def dot(a, b, dims):
    return lax.dot_general(a, b, dims, preferred_element_type=f32)


def two_heads(x):
    first = lax.broadcasted_iota(jnp.int32, x.shape, 1) < HD
    zero = jnp.zeros_like(x)
    return jnp.concatenate([jnp.where(first, x, zero), jnp.where(first, zero, x)], axis=0)


def pick_heads(xt):
    rows = xt.shape[1] // 2
    own = jnp.concatenate([xt[:HD, :rows], xt[HD:, rows:]], axis=0)
    return own.T


def one_hot(n, at):
    r = lax.broadcasted_iota(jnp.int32, (n, n), 0)
    c = lax.broadcasted_iota(jnp.int32, (n, n), 1)
    return (c == at(r)).astype(bf16)


def flipped(x):
    n = x.shape[0]
    return dot(one_hot(n, lambda r: n - 1 - r), x, NN).astype(bf16)


def place():
    return lax.axis_index("seq"), lax.axis_size("seq")


def part(t, which):
    return slice((2 * t + which) * BLK, (2 * t + which + 1) * BLK)


def listed(fb_ref, t, shard, shards, f):
    entry = fb_ref[shard if t == 0 else shards - 1 - shard, f]
    owner = lax.shift_right_arithmetic(entry, 1)
    owner = owner if t == 0 else shards - 1 - owner
    return entry >= 0, jnp.where(entry >= 0, owner, 0)


def asked_of(fb, t, shard, shards):
    mine = shard if t == 0 else shards - 1 - shard
    inner = fb & 1
    inner = inner + 1 if t == 0 else 2 - inner
    hit = jnp.where(lax.shift_right_arithmetic(fb, 1) == mine, inner, 0)
    return jnp.sum(hit, axis=1, keepdims=True)


def pack_kernel(fb_ref, key_ref, value_ref, out_ref, kv_ref):
    shard, shards = place()
    fb = fb_ref[...]
    for which, ref in ((0, key_ref), (1, value_ref)):
        kv_ref[:, which] = ref[...]
    for t in range(2):
        asked = jnp.broadcast_to(asked_of(fb, t, shard, shards), (shards, 2 * HD))
        for d in range(shards):
            row = d if t == 0 else shards - 1 - d
            second = jnp.broadcast_to(asked[row : row + 1] == 2, (BLK, 2 * HD))
            for which, ref in ((0, key_ref), (1, value_ref)):
                out_ref[d, part(t, which)] = jnp.where(second, ref[t, BLK:], ref[t, :BLK])


def stage(fb_ref, t, kv_ref, prev_ref, next_ref, far_ref, kbuf, vbuf):
    shard, shards = place()
    for which, buf in ((0, kbuf), (1, vbuf)):
        buf[0:128] = prev_ref[t, which]
        buf[128:256] = kv_ref[t, which]
        buf[256:384] = next_ref[t, which]
    for f in range(fb_ref.shape[1]):
        _, slot = listed(fb_ref, t, shard, shards, f)
        rows = slice(STEP + f * BLK, STEP + (f + 1) * BLK)
        kbuf[rows] = far_ref[slot, part(t, 0)]
        vbuf[rows] = far_ref[slot, part(t, 1)]


def biased(fb_ref, t, slopes_ref, q2, kbuf, put):
    shard, shards = place()
    cols = q2.shape[0]
    half = cols // 2
    head_col = lax.broadcasted_iota(jnp.int32, (1, cols), 1)
    slope = jnp.where(head_col < half, slopes_ref[0], slopes_ref[1])
    r = lax.broadcasted_iota(jnp.int32, (STEP, cols), 0)
    c = lax.broadcasted_iota(jnp.int32, (STEP, cols), 1)
    c = jnp.where(c < half, c, c - half)
    delta = r - 128 - c
    low = jnp.where(shard > 0, 0, 128)
    high = jnp.where(shard < shards - 1, STEP, 256)
    edge = jnp.where(c < BLK, 0, BLK)
    ok = (r >= jnp.maximum(edge, low)) & (r < jnp.minimum(edge + 320, high))
    scores = dot(kbuf[0:STEP], q2, NT) - slope * jnp.abs(delta).astype(f32)
    scores = jnp.where(ok, scores, masked_value)
    put(0, STEP, scores)
    top = jnp.max(scores, axis=0, keepdims=True)
    far_bias = slope * (-float((BAND + 1) * BLK))
    for lo in range(STEP, kbuf.shape[0], STEP):
        scores = dot(kbuf[lo : lo + STEP], q2, NT)
        parts = []
        for i in range(STEP // BLK):
            there, _ = listed(fb_ref, t, shard, shards, (lo - STEP) // BLK + i)
            row = jnp.where(there, far_bias, masked_value)
            parts.append(scores[i * BLK : (i + 1) * BLK] + row)
        scores = jnp.concatenate(parts, axis=0)
        put(lo, lo + STEP, scores)
        top = jnp.maximum(top, jnp.max(scores, axis=0, keepdims=True))
    return top


def forward_kernel(fb_ref, slopes_ref, q_ref, kv_ref, prev_ref, next_ref, far_ref, ctx_ref, rev_ref, stat_ref, kbuf, vbuf, sbuf):
    n = 2 * HD
    eye = one_hot(n, lambda r: r)
    total = kbuf.shape[0]
    for t in (1, 0):
        stage(fb_ref, t, kv_ref, prev_ref, next_ref, far_ref, kbuf, vbuf)
        q2 = two_heads(q_ref[t] * HD ** (-0.5))

        def put(lo, hi, scores):
            sbuf[lo:hi] = scores

        top = biased(fb_ref, t, slopes_ref, q2, kbuf, put)
        norm = jnp.zeros_like(top)
        for lo in range(0, total, STEP):
            w = jnp.exp(sbuf[lo : lo + STEP] - top)
            sbuf[lo : lo + STEP] = w
            norm = norm + jnp.sum(w, axis=0, keepdims=True)
        inv = 1.0 / norm
        stat_ref[t, 0:1] = top
        stat_ref[t, 1:2] = inv
        acc = jnp.zeros((n, q2.shape[0]), f32)
        for lo in range(0, total, STEP):
            low = (sbuf[lo : lo + STEP] * inv).astype(bf16)
            vt = dot(eye, vbuf[lo : lo + STEP], NT).astype(bf16)
            acc = acc + dot(vt, low, NN)
        ctx = pick_heads(acc).astype(bf16)
        if t == 1:
            rev_ref[...] = flipped(ctx)
        else:
            ctx_ref[...] = ctx


def context_grad_kernel(own_ref, ref2, ref4, ref6, weight_ref, out_ref, buf):
    count, rows, _ = buf.shape
    got = jnp.concatenate([ref[k] for ref in (own_ref, ref2, ref4, ref6) for k in range(2)], axis=0)
    out = dot(got, weight_ref[...], NT).astype(bf16)
    for k in range(count):
        buf[k] = out[k * rows : (k + 1) * rows]
    at = lax.axis_index("tp")
    for k in range(count):
        out_ref[k * rows : (k + 1) * rows] = buf[lax.bitwise_xor(at, k)]


def backward_kernel(
    fb_ref, slopes_ref, q_ref, kv_ref, prev_ref, next_ref, far_ref, stat_ref, grad_ref, mirrored_ref,
    gq_ref, own_out, prev_out, next_out, far_out, kbuf, vbuf, pbuf, dbuf,
):
    shard, shards = place()
    n = 2 * HD
    eye = one_hot(n, lambda r: r)
    total = kbuf.shape[0]
    for t in range(2):
        stage(fb_ref, t, kv_ref, prev_ref, next_ref, far_ref, kbuf, vbuf)
        q2 = two_heads(q_ref[t] * HD ** (-0.5))
        g2 = two_heads(flipped(mirrored_ref[...]) if t == 1 else grad_ref[...])
        cols = q2.shape[0]
        top = stat_ref[t, 0:1]
        inv = stat_ref[t, 1:2]

        def put(lo, hi, scores):
            pbuf[lo:hi] = jnp.exp(scores - top) * inv

        biased(fb_ref, t, slopes_ref, q2, kbuf, put)
        row_dot = jnp.zeros((1, cols), f32)
        for lo in range(0, total, STEP):
            gp = dot(vbuf[lo : lo + STEP], g2, NT)
            dbuf[lo : lo + STEP] = gp
            row_dot = row_dot + jnp.sum(pbuf[lo : lo + STEP] * gp, axis=0, keepdims=True)
        acc = jnp.zeros((n, cols), f32)
        for lo in range(0, total, STEP):
            p = pbuf[lo : lo + STEP]
            ds = (p * (dbuf[lo : lo + STEP] - row_dot)).astype(bf16)
            kt = dot(eye, kbuf[lo : lo + STEP], NT).astype(bf16)
            acc = acc + dot(kt, ds, NN)
            for which, x in ((0, dot(ds, q2, NN)), (1, dot(p.astype(bf16), g2, NN))):
                if lo == 0:
                    prev_out[t, which] = x[0:128].astype(bf16)
                    own_out[t, which] = x[128:256]
                    next_out[t, which] = x[256:384].astype(bf16)
                else:
                    low = x.astype(bf16)
                    for i in range(STEP // BLK):
                        there, slot = listed(fb_ref, t, shard, shards, (lo - STEP) // BLK + i)

                        @pl.when(there)
                        def _():
                            far_out[slot, part(t, which)] = low[i * BLK : (i + 1) * BLK]

        gq_ref[t] = (pick_heads(acc) * HD ** (-0.5)).astype(bf16)


def combine_kernel(fb_ref, own_ref, prev_ref, next_ref, far_ref, gk_ref, gv_ref):
    shard, shards = place()
    fb = fb_ref[...]
    rows = 32
    for t in range(2):
        asked = jnp.broadcast_to(asked_of(fb, t, shard, shards), (shards, 2 * HD))
        for which, out_ref in ((0, gk_ref), (1, gv_ref)):
            for lo in range(0, BLK, rows):
                first = jnp.zeros((rows, 2 * HD), f32)
                second = jnp.zeros((rows, 2 * HD), f32)
                for d in range(shards):
                    row = d if t == 0 else shards - 1 - d
                    block = jnp.broadcast_to(asked[row : row + 1], (rows, 2 * HD))
                    at = part(t, which).start + lo
                    x = far_ref[d, at : at + rows].astype(f32)
                    first = first + jnp.where(block == 1, x, 0.0)
                    second = second + jnp.where(block == 2, x, 0.0)
                for at, far in ((lo, first), (BLK + lo, second)):
                    here = slice(at, at + rows)
                    total = own_ref[t, which, here] + prev_ref[t, which, here].astype(f32)
                    total = total + next_ref[t, which, here].astype(f32)
                    out_ref[t, here] = (total + far).astype(bf16)


def project_kernel(ctx_ref, back_ref, weight_ref, own_ref, ref2, ref4, ref6, sum_buf):
    total = (ctx_ref[...].astype(f32) + back_ref[...].astype(f32)).astype(bf16)
    count, rows, _ = sum_buf.shape
    for k in range(count):
        sum_buf[k] = total[k * rows : (k + 1) * rows]
    at = lax.axis_index("tp")
    blocks = jnp.concatenate([sum_buf[lax.bitwise_xor(at, j)] for j in range(count)], axis=0)
    out = dot(blocks, weight_ref[...], NN)
    for j in range(count):
        ref = (own_ref, ref2, ref4, ref6)[j // 2]
        ref[j % 2] = out[j * rows : (j + 1) * rows].astype(ref.dtype)


def smem():
    return pl.BlockSpec(memory_space=pltpu.SMEM)


def vmem():
    return pl.BlockSpec(memory_space=pltpu.VMEM)


def shape(dims, dtype=bf16):
    return jax.ShapeDtypeStruct(dims, dtype)


def cost(flops, nbytes, exps=0):
    return pl.CostEstimate(flops=flops, bytes_accessed=nbytes, transcendentals=exps)


def swap(x, bit):
    count = lax.axis_size("tp")
    return lax.ppermute(x, "tp", [(i, i ^ bit) for i in range(count)])


def per_device(
    residual, queries, keys, values, slopes, out_weight, cotangent, far_blocks, far_count
):
    seq_count = lax.axis_size("seq")
    tp_count = lax.axis_size("tp")
    tok_rows, width = queries.shape[1:]
    total_keys = 3 * tok_rows + far_blocks.shape[1] * BLK
    model = out_weight.shape[1]
    cols = 2 * tok_rows
    both = (2, 2, tok_rows, width)
    pieces = (tp_count, tok_rows // tp_count, width)
    slots = (seq_count, 4 * BLK, width)

    outgoing, key_value = pl.pallas_call(
        pack_kernel,
        out_shape=(shape(slots), shape(both)),
        in_specs=[vmem()] * 3,
        out_specs=(vmem(), vmem()),
        cost_estimate=cost(1_000_000, 2_500_000),
        compiler_params=pltpu.CompilerParams(vmem_limit_bytes=LIMIT),
        name="pack",
    )(far_blocks, keys, values)
    own_pair = jnp.stack([cotangent, swap(cotangent, 1)])
    others = [swap(own_pair, bit) for bit in (2, 4, 6)]
    outgoing, *others = lax.optimization_barrier((outgoing, *others))
    far = lax.all_to_all(outgoing, "seq", split_axis=0, concat_axis=0, tiled=True)

    up = [(i, i + 1) for i in range(seq_count - 1)]
    down = [(j, i) for i, j in up]
    mirror = [(i, seq_count - 1 - i) for i in range(seq_count)]
    from_prev = lax.ppermute(key_value, "seq", up)
    from_next = lax.ppermute(key_value, "seq", down)

    grad_context = pl.pallas_call(
        context_grad_kernel,
        out_shape=shape((tok_rows, width)),
        in_specs=[vmem()] * 5,
        out_specs=vmem(),
        scratch_shapes=[pltpu.VMEM(pieces, bf16)],
        cost_estimate=cost(34_000_000, 600_000),
        compiler_params=pltpu.CompilerParams(vmem_limit_bytes=LIMIT),
        name="context_grad",
    )(own_pair, *others, out_weight)
    mirrored = lax.ppermute(grad_context, "seq", mirror)

    keyed = [pltpu.VMEM((total_keys, width), bf16), pltpu.VMEM((total_keys, width), bf16)]
    context_fwd, context_rev, stats = pl.pallas_call(
        forward_kernel,
        out_shape=(shape((tok_rows, width)), shape((tok_rows, width)), shape((2, 2, cols), f32)),
        in_specs=[smem()] * 2 + [vmem()] * 5,
        out_specs=(vmem(),) * 3,
        scratch_shapes=keyed + [pltpu.VMEM((total_keys, cols), f32)],
        cost_estimate=cost(1_600_000_000, 4_000_000, 1_000_000),
        compiler_params=pltpu.CompilerParams(vmem_limit_bytes=LIMIT),
        name="attend_forward",
    )(far_blocks, slopes, queries, key_value, from_prev, from_next, far)
    context_back = lax.ppermute(context_rev, "seq", mirror)

    grad_queries, own, before, after, far_grads = pl.pallas_call(
        backward_kernel,
        out_shape=(shape((2, tok_rows, width)), shape(both, f32), shape(both), shape(both), shape(slots)),
        in_specs=[smem()] * 2 + [vmem()] * 8,
        out_specs=(vmem(),) * 5,
        scratch_shapes=keyed
        + [pltpu.VMEM((total_keys, cols), f32)] * 2,
        cost_estimate=cost(3_200_000_000, 8_000_000, 1_000_000),
        compiler_params=pltpu.CompilerParams(vmem_limit_bytes=LIMIT),
        name="attend_backward",
    )(
        far_blocks, slopes, queries, key_value, from_prev, from_next, far, stats,
        grad_context, mirrored,
    )
    own_rows, *other_rows = pl.pallas_call(
        project_kernel,
        out_shape=(shape((2, tok_rows // tp_count, model), f32),)
        + (shape((2, tok_rows // tp_count, model)),) * 3,
        in_specs=[vmem()] * 3,
        out_specs=(vmem(),) * 4,
        scratch_shapes=[pltpu.VMEM(pieces, bf16)],
        cost_estimate=cost(34_000_000, 1_000_000),
        compiler_params=pltpu.CompilerParams(vmem_limit_bytes=LIMIT),
        name="project",
    )(context_fwd, context_back, out_weight)
    far_grads, *other_rows = lax.optimization_barrier((far_grads, *other_rows))
    returned = lax.all_to_all(far_grads, "seq", split_axis=0, concat_axis=0, tiled=True)
    from_prev_grad = lax.ppermute(after, "seq", up)
    from_next_grad = lax.ppermute(before, "seq", down)

    held = own_rows
    for bit, rows in zip((2, 4, 6), other_rows):
        held = held + swap(rows, bit).astype(f32)
    held, from_prev_grad, from_next_grad = lax.optimization_barrier((held, from_prev_grad, from_next_grad))
    mixed = (residual.astype(f32) + held[0] + swap(held[1].astype(bf16), 1).astype(f32)).astype(bf16)

    grad_keys, grad_values = pl.pallas_call(
        combine_kernel,
        out_shape=(shape((2, tok_rows, width)),) * 2,
        in_specs=[vmem()] * 5,
        out_specs=(vmem(),) * 2,
        cost_estimate=cost(4_000_000, 3_000_000),
        compiler_params=pltpu.CompilerParams(vmem_limit_bytes=LIMIT),
        name="combine",
    )(far_blocks, own, from_prev_grad, from_next_grad, returned)
    return (mixed, grad_queries, grad_keys, grad_values)


def solution(mesh):
    return jax.shard_map(
        per_device,
        mesh=mesh,
        in_specs=(
            P(("seq", "tp"), None),
            P(None, "seq", "tp"),
            P(None, "seq", "tp"),
            P(None, "seq", "tp"),
            P("tp"),
            P("tp", None),
            P(("seq", "tp"), None),
            P(),
            P(),
        ),
        out_specs=(
            P(("seq", "tp"), None),
            P(None, "seq", "tp"),
            P(None, "seq", "tp"),
            P(None, "seq", "tp"),
        ),
        check_vma=False,
    )
```

```python
import jax
import jax.numpy as jnp
from jax import lax
from jax.experimental import pallas as pl
from jax.experimental.pallas import tpu as pltpu
from jax.sharding import PartitionSpec as P

HD = 64
BLK = 64
BAND = 2
STEP = 384
LIMIT = 24 << 20

masked_value = -1e30
f32 = jnp.float32
bf16 = jnp.bfloat16

NT = (((1,), (1,)), ((), ()))
NN = (((1,), (0,)), ((), ()))


def dot(a, b, dims):
    return lax.dot_general(a, b, dims, preferred_element_type=f32)


def two_heads(x):
    first = lax.broadcasted_iota(jnp.int32, x.shape, 1) < HD
    zero = jnp.zeros_like(x)
    return jnp.concatenate([jnp.where(first, x, zero), jnp.where(first, zero, x)], axis=0)


def pick_heads(xt):
    rows = xt.shape[1] // 2
    own = jnp.concatenate([xt[:HD, :rows], xt[HD:, rows:]], axis=0)
    return own.T


def one_hot(n, at):
    r = lax.broadcasted_iota(jnp.int32, (n, n), 0)
    c = lax.broadcasted_iota(jnp.int32, (n, n), 1)
    return (c == at(r)).astype(bf16)


def flipped(x):
    n = x.shape[0]
    return dot(one_hot(n, lambda r: n - 1 - r), x, NN).astype(bf16)


SEQ = ("x", "zh", "y")


def place():
    x, zh, y = (lax.axis_index(a) for a in SEQ)
    nx, nz, ny = (lax.axis_size(a) for a in SEQ)
    return (x * nz + zh) * ny + y, nx * nz * ny, zh, y


def slot_of(owner):
    nz, ny = lax.axis_size("zh"), lax.axis_size("y")
    xz, y = lax.div(owner, ny), lax.rem(owner, ny)
    return (lax.div(xz, nz) * ny + y) * nz + lax.rem(xz, nz)


def plane_readers(zh):
    nx, nz, ny = (lax.axis_size(a) for a in SEQ)
    return [(x * nz + zh) * ny + y for x in range(nx) for y in range(ny)]


def part(t, which):
    return slice((2 * t + which) * BLK, (2 * t + which + 1) * BLK)


def listed(fb_ref, t, shard, shards, f):
    entry = fb_ref[shard if t == 0 else shards - 1 - shard, f]
    owner = lax.shift_right_arithmetic(entry, 1)
    owner = owner if t == 0 else shards - 1 - owner
    return entry >= 0, jnp.where(entry >= 0, slot_of(owner), 0)


def asked_of(fb, t, shard, shards):
    mine = shard if t == 0 else shards - 1 - shard
    inner = fb & 1
    inner = inner + 1 if t == 0 else 2 - inner
    hit = jnp.where(lax.shift_right_arithmetic(fb, 1) == mine, inner, 0)
    return jnp.sum(hit, axis=1, keepdims=True)


def asked_rows(fb_ref, asked_buf):
    shard, shards, zh, y = place()
    fb = fb_ref[...]
    ny = lax.axis_size("y")
    for z in range(lax.axis_size("zh")):
        for t in range(2):
            asked = asked_of(fb, t, shard + (z - zh) * ny, shards)
            asked_buf[z, t] = jnp.broadcast_to(asked, asked_buf.shape[2:])


def asked_by(asked_buf, z, t, reader, rows):
    row = reader if t == 0 else asked_buf.shape[2] - 1 - reader
    return jnp.broadcast_to(asked_buf[z, t, pl.ds(row, 1)], (rows, 2 * HD))


def pack_kernel(fb_ref, own_ref, partner_ref, out_ref, up_ref, down_ref, asked_buf, kv_buf):
    shard, shards, zh, y = place()
    ny = lax.axis_size("y")
    asked_rows(fb_ref, asked_buf)
    kv_buf[zh] = own_ref[...]
    kv_buf[1 - zh] = partner_ref[...]
    up_ref[...] = kv_buf[jnp.where(y == ny - 1, 1 - zh, zh)]
    down_ref[...] = kv_buf[jnp.where(y == 0, 1 - zh, zh)]
    for p, reader in enumerate(plane_readers(zh)):
        for z in range(2):
            for t in range(2):
                second = asked_by(asked_buf, z, t, reader, BLK) == 2
                for which in range(2):
                    out_ref[2 * p + z, part(t, which)] = jnp.where(
                        second, kv_buf[z, t, which, BLK:], kv_buf[z, t, which, :BLK]
                    )


def stage(fb_ref, t, kv_ref, prev_ref, next_ref, far_ref, kbuf, vbuf):
    shard, shards, zh, y = place()
    for which, buf in ((0, kbuf), (1, vbuf)):
        buf[0:128] = prev_ref[t, which]
        buf[128:256] = kv_ref[t, which]
        buf[256:384] = next_ref[t, which]
    for f in range(fb_ref.shape[1]):
        _, slot = listed(fb_ref, t, shard, shards, f)
        rows = slice(STEP + f * BLK, STEP + (f + 1) * BLK)
        kbuf[rows] = far_ref[slot, part(t, 0)]
        vbuf[rows] = far_ref[slot, part(t, 1)]


def biased(fb_ref, t, slopes_ref, q2, kbuf, put):
    shard, shards, zh, y = place()
    cols = q2.shape[0]
    half = cols // 2
    head_col = lax.broadcasted_iota(jnp.int32, (1, cols), 1)
    slope = jnp.where(head_col < half, slopes_ref[0], slopes_ref[1])
    r = lax.broadcasted_iota(jnp.int32, (STEP, cols), 0)
    c = lax.broadcasted_iota(jnp.int32, (STEP, cols), 1)
    c = jnp.where(c < half, c, c - half)
    delta = r - 128 - c
    low = jnp.where(shard > 0, 0, 128)
    high = jnp.where(shard < shards - 1, STEP, 256)
    edge = jnp.where(c < BLK, 0, BLK)
    ok = (r >= jnp.maximum(edge, low)) & (r < jnp.minimum(edge + 320, high))
    scores = dot(kbuf[0:STEP], q2, NT) - slope * jnp.abs(delta).astype(f32)
    scores = jnp.where(ok, scores, masked_value)
    put(0, STEP, scores)
    top = jnp.max(scores, axis=0, keepdims=True)
    far_bias = slope * (-float((BAND + 1) * BLK))
    for lo in range(STEP, kbuf.shape[0], STEP):
        scores = dot(kbuf[lo : lo + STEP], q2, NT)
        parts = []
        for i in range(STEP // BLK):
            there, _ = listed(fb_ref, t, shard, shards, (lo - STEP) // BLK + i)
            row = jnp.where(there, far_bias, masked_value)
            parts.append(scores[i * BLK : (i + 1) * BLK] + row)
        scores = jnp.concatenate(parts, axis=0)
        put(lo, lo + STEP, scores)
        top = jnp.maximum(top, jnp.max(scores, axis=0, keepdims=True))
    return top


def forward_kernel(fb_ref, slopes_ref, q_ref, kv_ref, prev_ref, next_ref, far_ref, ctx_ref, rev_ref, stat_ref, kbuf, vbuf, sbuf):
    n = 2 * HD
    eye = one_hot(n, lambda r: r)
    total = kbuf.shape[0]
    for t in (1, 0):
        stage(fb_ref, t, kv_ref, prev_ref, next_ref, far_ref, kbuf, vbuf)
        q2 = two_heads(q_ref[t] * HD ** (-0.5))

        def put(lo, hi, scores):
            sbuf[lo:hi] = scores

        top = biased(fb_ref, t, slopes_ref, q2, kbuf, put)
        norm = jnp.zeros_like(top)
        for lo in range(0, total, STEP):
            w = jnp.exp(sbuf[lo : lo + STEP] - top)
            sbuf[lo : lo + STEP] = w
            norm = norm + jnp.sum(w, axis=0, keepdims=True)
        inv = 1.0 / norm
        stat_ref[t, 0:1] = top
        stat_ref[t, 1:2] = inv
        acc = jnp.zeros((n, q2.shape[0]), f32)
        for lo in range(0, total, STEP):
            low = (sbuf[lo : lo + STEP] * inv).astype(bf16)
            vt = dot(eye, vbuf[lo : lo + STEP], NT).astype(bf16)
            acc = acc + dot(vt, low, NN)
        ctx = pick_heads(acc).astype(bf16)
        if t == 1:
            rev_ref[...] = flipped(ctx)
        else:
            ctx_ref[...] = ctx


def context_grad_kernel(own_ref, ref2, ref4, ref6, weight_ref, out_ref, buf):
    count, rows, _ = buf.shape
    got = jnp.concatenate([ref[k] for ref in (own_ref, ref2, ref4, ref6) for k in range(2)], axis=0)
    out = dot(got, weight_ref[...], NT).astype(bf16)
    for k in range(count):
        buf[k] = out[k * rows : (k + 1) * rows]
    at = lax.axis_index("tp")
    for k in range(count):
        out_ref[k * rows : (k + 1) * rows] = buf[lax.bitwise_xor(at, k)]


def backward_kernel(
    fb_ref, slopes_ref, q_ref, kv_ref, prev_ref, next_ref, far_ref, stat_ref, grad_ref, mirrored_ref,
    gq_ref, own_out, prev_out, next_out, far_out, kbuf, vbuf, pbuf, dbuf,
):
    shard, shards, zh, y = place()
    n = 2 * HD
    eye = one_hot(n, lambda r: r)
    total = kbuf.shape[0]
    for t in range(2):
        stage(fb_ref, t, kv_ref, prev_ref, next_ref, far_ref, kbuf, vbuf)
        q2 = two_heads(q_ref[t] * HD ** (-0.5))
        g2 = two_heads(flipped(mirrored_ref[...]) if t == 1 else grad_ref[...])
        cols = q2.shape[0]
        top = stat_ref[t, 0:1]
        inv = stat_ref[t, 1:2]

        def put(lo, hi, scores):
            pbuf[lo:hi] = jnp.exp(scores - top) * inv

        biased(fb_ref, t, slopes_ref, q2, kbuf, put)
        row_dot = jnp.zeros((1, cols), f32)
        for lo in range(0, total, STEP):
            gp = dot(vbuf[lo : lo + STEP], g2, NT)
            dbuf[lo : lo + STEP] = gp
            row_dot = row_dot + jnp.sum(pbuf[lo : lo + STEP] * gp, axis=0, keepdims=True)
        acc = jnp.zeros((n, cols), f32)
        for lo in range(0, total, STEP):
            p = pbuf[lo : lo + STEP]
            ds = (p * (dbuf[lo : lo + STEP] - row_dot)).astype(bf16)
            kt = dot(eye, kbuf[lo : lo + STEP], NT).astype(bf16)
            acc = acc + dot(kt, ds, NN)
            for which, x in ((0, dot(ds, q2, NN)), (1, dot(p.astype(bf16), g2, NN))):
                if lo == 0:
                    prev_out[t, which] = x[0:128].astype(bf16)
                    own_out[t, which] = x[128:256]
                    next_out[t, which] = x[256:384].astype(bf16)
                else:
                    low = x.astype(bf16)
                    for i in range(STEP // BLK):
                        there, slot = listed(fb_ref, t, shard, shards, (lo - STEP) // BLK + i)

                        @pl.when(there)
                        def _():
                            far_out[slot, part(t, which)] = low[i * BLK : (i + 1) * BLK]

        gq_ref[t] = (pick_heads(acc) * HD ** (-0.5)).astype(bf16)


def combine_kernel(fb_ref, own_ref, prev_ref, next_ref, far_ref, mine_ref, other_ref, asked_buf, sum_buf):
    shard, shards, zh, y = place()
    last = lax.axis_size("y") - 1
    asked_rows(fb_ref, asked_buf)
    rows = 32
    for z in range(2):
        for t in range(2):
            for which in range(2):
                for lo in range(0, BLK, rows):
                    first = jnp.zeros((rows, 2 * HD), f32)
                    second = jnp.zeros((rows, 2 * HD), f32)
                    at = part(t, which).start + lo
                    for p, reader in enumerate(plane_readers(zh)):
                        block = asked_by(asked_buf, z, t, reader, rows)
                        x = far_ref[2 * p + z, at : at + rows].astype(f32)
                        first = first + jnp.where(block == 1, x, 0.0)
                        second = second + jnp.where(block == 2, x, 0.0)
                    sum_buf[z, t, which, lo : lo + rows] = first
                    sum_buf[z, t, which, BLK + lo : BLK + lo + rows] = second
    sum_buf[zh] = sum_buf[zh] + own_ref[...]
    to = jnp.where(y == 0, 1 - zh, zh)
    sum_buf[to] = sum_buf[to] + prev_ref[...].astype(f32)
    to = jnp.where(y == last, 1 - zh, zh)
    sum_buf[to] = sum_buf[to] + next_ref[...].astype(f32)
    mine_ref[...] = sum_buf[zh]
    other_ref[...] = sum_buf[1 - zh].astype(bf16)


def finish_kernel(mine_ref, other_ref, gk_ref, gv_ref):
    for which, ref in ((0, gk_ref), (1, gv_ref)):
        ref[...] = (mine_ref[:, which] + other_ref[:, which].astype(f32)).astype(bf16)


def project_kernel(ctx_ref, back_ref, weight_ref, own_ref, ref2, ref4, ref6, sum_buf):
    total = (ctx_ref[...].astype(f32) + back_ref[...].astype(f32)).astype(bf16)
    count, rows, _ = sum_buf.shape
    for k in range(count):
        sum_buf[k] = total[k * rows : (k + 1) * rows]
    at = lax.axis_index("tp")
    blocks = jnp.concatenate([sum_buf[lax.bitwise_xor(at, j)] for j in range(count)], axis=0)
    out = dot(blocks, weight_ref[...], NN)
    for j in range(count):
        ref = (own_ref, ref2, ref4, ref6)[j // 2]
        ref[j % 2] = out[j * rows : (j + 1) * rows].astype(ref.dtype)


def smem():
    return pl.BlockSpec(memory_space=pltpu.SMEM)


def vmem():
    return pl.BlockSpec(memory_space=pltpu.VMEM)


def shape(dims, dtype=bf16):
    return jax.ShapeDtypeStruct(dims, dtype)


def cost(flops, nbytes, exps=0):
    return pl.CostEstimate(flops=flops, bytes_accessed=nbytes, transcendentals=exps)


def swap(x, bit):
    count = lax.axis_size("tp")
    return lax.ppermute(x, "tp", [(i, i ^ bit) for i in range(count)])


def per_device(
    residual, queries, keys, values, slopes, out_weight, cotangent, far_blocks, far_count
):
    nx, nz, ny = (lax.axis_size(a) for a in SEQ)
    seq_count = nx * nz * ny
    tp_count = lax.axis_size("tp")
    tok_rows, width = queries.shape[1:]
    total_keys = 3 * tok_rows + far_blocks.shape[1] * BLK
    model = out_weight.shape[1]
    cols = 2 * tok_rows
    both = (2, 2, tok_rows, width)
    pieces = (tp_count, tok_rows // tp_count, width)
    slots = (seq_count, 4 * BLK, width)

    def plane_a2a(x):
        x = x.reshape(nx * ny, nz * slots[1], width)
        return lax.all_to_all(x, ("x", "y"), split_axis=0, concat_axis=0, tiled=True).reshape(slots)

    def z_swap(x):
        return lax.ppermute(x, "zh", [(i, nz - 1 - i) for i in range(nz)])

    key_value = jnp.stack([keys, values], axis=1)
    partner = z_swap(key_value)
    asked = pltpu.VMEM((nz, 2, seq_count, 2 * HD), jnp.int32)
    outgoing, to_up, to_down = pl.pallas_call(
        pack_kernel,
        out_shape=(shape(slots), shape(both), shape(both)),
        in_specs=[vmem()] * 3,
        out_specs=(vmem(),) * 3,
        scratch_shapes=[asked, pltpu.VMEM((nz,) + both, bf16)],
        cost_estimate=cost(1_000_000, 2_500_000),
        compiler_params=pltpu.CompilerParams(vmem_limit_bytes=LIMIT),
        name="pack",
    )(far_blocks, key_value, partner)
    own_pair = jnp.stack([cotangent, swap(cotangent, 1)])
    others = [swap(own_pair, bit) for bit in (2, 4, 6)]
    outgoing, *others = lax.optimization_barrier((outgoing, *others))
    far = plane_a2a(outgoing)

    def flat(x, zh, y):
        return (x * nz + zh) * ny + y

    places = [(x, zh, y) for x in range(nx) for zh in range(nz) for y in range(ny)]
    up, down = [], []
    for x, zh, y in places:
        if y < ny - 1:
            up.append((flat(x, zh, y), flat(x, zh, y + 1)))
        elif zh == nz - 1:
            up.append((flat(x, zh, y), flat(x, zh, 0)))
        elif x < nx - 1:
            up.append((flat(x, zh, y), flat(x + 1, zh, 0)))
        if y > 0:
            down.append((flat(x, zh, y), flat(x, zh, y - 1)))
        elif zh == 0:
            down.append((flat(x, zh, y), flat(x, zh, ny - 1)))
        elif x > 0:
            down.append((flat(x, zh, y), flat(x - 1, zh, ny - 1)))
    mirror = [(i, seq_count - 1 - i) for i in range(seq_count)]
    from_prev = lax.ppermute(to_up, SEQ, up)
    from_next = lax.ppermute(to_down, SEQ, down)

    grad_context = pl.pallas_call(
        context_grad_kernel,
        out_shape=shape((tok_rows, width)),
        in_specs=[vmem()] * 5,
        out_specs=vmem(),
        scratch_shapes=[pltpu.VMEM(pieces, bf16)],
        cost_estimate=cost(34_000_000, 600_000),
        compiler_params=pltpu.CompilerParams(vmem_limit_bytes=LIMIT),
        name="context_grad",
    )(own_pair, *others, out_weight)
    mirrored = lax.ppermute(grad_context, SEQ, mirror)

    keyed = [pltpu.VMEM((total_keys, width), bf16), pltpu.VMEM((total_keys, width), bf16)]
    context_fwd, context_rev, stats = pl.pallas_call(
        forward_kernel,
        out_shape=(shape((tok_rows, width)), shape((tok_rows, width)), shape((2, 2, cols), f32)),
        in_specs=[smem()] * 2 + [vmem()] * 5,
        out_specs=(vmem(),) * 3,
        scratch_shapes=keyed + [pltpu.VMEM((total_keys, cols), f32)],
        cost_estimate=cost(1_600_000_000, 4_000_000, 1_000_000),
        compiler_params=pltpu.CompilerParams(vmem_limit_bytes=LIMIT),
        name="attend_forward",
    )(far_blocks, slopes, queries, key_value, from_prev, from_next, far)
    context_back = lax.ppermute(context_rev, SEQ, mirror)

    grad_queries, own, before, after, far_grads = pl.pallas_call(
        backward_kernel,
        out_shape=(shape((2, tok_rows, width)), shape(both, f32), shape(both), shape(both), shape(slots)),
        in_specs=[smem()] * 2 + [vmem()] * 8,
        out_specs=(vmem(),) * 5,
        scratch_shapes=keyed
        + [pltpu.VMEM((total_keys, cols), f32)] * 2,
        cost_estimate=cost(3_200_000_000, 8_000_000, 1_000_000),
        compiler_params=pltpu.CompilerParams(vmem_limit_bytes=LIMIT),
        name="attend_backward",
    )(
        far_blocks, slopes, queries, key_value, from_prev, from_next, far, stats,
        grad_context, mirrored,
    )
    own_rows, *other_rows = pl.pallas_call(
        project_kernel,
        out_shape=(shape((2, tok_rows // tp_count, model), f32),)
        + (shape((2, tok_rows // tp_count, model)),) * 3,
        in_specs=[vmem()] * 3,
        out_specs=(vmem(),) * 4,
        scratch_shapes=[pltpu.VMEM(pieces, bf16)],
        cost_estimate=cost(34_000_000, 1_000_000),
        compiler_params=pltpu.CompilerParams(vmem_limit_bytes=LIMIT),
        name="project",
    )(context_fwd, context_back, out_weight)
    far_grads, *other_rows = lax.optimization_barrier((far_grads, *other_rows))
    returned = plane_a2a(far_grads)
    from_prev_grad = lax.ppermute(after, SEQ, [(b, a) for a, b in down])
    from_next_grad = lax.ppermute(before, SEQ, [(b, a) for a, b in up])

    held = own_rows
    for bit, rows in zip((2, 4, 6), other_rows):
        held = held + swap(rows, bit).astype(f32)
    held, from_prev_grad, from_next_grad = lax.optimization_barrier((held, from_prev_grad, from_next_grad))
    mixed = (residual.astype(f32) + held[0] + swap(held[1].astype(bf16), 1).astype(f32)).astype(bf16)

    mine, other = pl.pallas_call(
        combine_kernel,
        out_shape=(shape(both, f32), shape(both)),
        in_specs=[vmem()] * 5,
        out_specs=(vmem(),) * 2,
        scratch_shapes=[asked, pltpu.VMEM((nz,) + both, f32)],
        cost_estimate=cost(4_000_000, 3_000_000),
        compiler_params=pltpu.CompilerParams(vmem_limit_bytes=LIMIT),
        name="combine",
    )(far_blocks, own, from_prev_grad, from_next_grad, returned)
    grad_keys, grad_values = pl.pallas_call(
        finish_kernel,
        out_shape=(shape((2, tok_rows, width)),) * 2,
        in_specs=[vmem()] * 2,
        out_specs=(vmem(),) * 2,
        cost_estimate=cost(100_000, 500_000),
        compiler_params=pltpu.CompilerParams(vmem_limit_bytes=LIMIT),
        name="finish",
    )(mine, z_swap(other))
    return (mixed, grad_queries, grad_keys, grad_values)


def solution(mesh):
    split = jax.sharding.Mesh(mesh.devices.reshape(4, 2, 4, -1), SEQ + ("tp",))
    rows = P(SEQ + ("tp",), None)
    strands = P(None, SEQ, "tp")
    return jax.shard_map(
        per_device,
        mesh=split,
        in_specs=(rows, strands, strands, strands, P("tp"), P("tp", None), rows, P(), P()),
        out_specs=(rows, strands, strands, strands),
        check_vma=False,
    )
```

```python
import jax
import jax.numpy as jnp
from jax import lax
from jax.experimental import pallas as pl
from jax.experimental.pallas import tpu as pltpu
from jax.sharding import PartitionSpec as P

HD = 64
BLK = 64
BAND = 2
STEP = 384
LIMIT = 24 << 20

masked_value = -1e30
f32 = jnp.float32
bf16 = jnp.bfloat16

NT = (((1,), (1,)), ((), ()))
NN = (((1,), (0,)), ((), ()))


def dot(a, b, dims):
    return lax.dot_general(a, b, dims, preferred_element_type=f32)


def two_heads(x):
    first = lax.broadcasted_iota(jnp.int32, x.shape, 1) < HD
    zero = jnp.zeros_like(x)
    return jnp.concatenate([jnp.where(first, x, zero), jnp.where(first, zero, x)], axis=0)


def pick_heads(xt):
    rows = xt.shape[1] // 2
    own = jnp.concatenate([xt[:HD, :rows], xt[HD:, rows:]], axis=0)
    return own.T


def one_hot(n, at):
    r = lax.broadcasted_iota(jnp.int32, (n, n), 0)
    c = lax.broadcasted_iota(jnp.int32, (n, n), 1)
    return (c == at(r)).astype(bf16)


def flipped(x):
    n = x.shape[0]
    return dot(one_hot(n, lambda r: n - 1 - r), x, NN).astype(bf16)


SEQ = ("x", "zh", "y")


def place():
    x, zh, y = (lax.axis_index(a) for a in SEQ)
    nx, nz, ny = (lax.axis_size(a) for a in SEQ)
    return (x * nz + zh) * ny + y, nx * nz * ny, zh, y


def slot_of(owner):
    nz, ny = lax.axis_size("zh"), lax.axis_size("y")
    xz, y = lax.div(owner, ny), lax.rem(owner, ny)
    return (lax.div(xz, nz) * ny + y) * nz + lax.rem(xz, nz)


def plane_readers(zh):
    nx, nz, ny = (lax.axis_size(a) for a in SEQ)
    return [(x * nz + zh) * ny + y for x in range(nx) for y in range(ny)]


def part(t, which):
    return slice((2 * t + which) * BLK, (2 * t + which + 1) * BLK)


def listed(fb_ref, t, shard, shards, f):
    entry = fb_ref[shard if t == 0 else shards - 1 - shard, f]
    owner = lax.shift_right_arithmetic(entry, 1)
    owner = owner if t == 0 else shards - 1 - owner
    return entry >= 0, jnp.where(entry >= 0, slot_of(owner), 0)


def asked_of(fb, t, shard, shards):
    mine = shard if t == 0 else shards - 1 - shard
    inner = fb & 1
    inner = inner + 1 if t == 0 else 2 - inner
    hit = jnp.where(lax.shift_right_arithmetic(fb, 1) == mine, inner, 0)
    return jnp.sum(hit, axis=1, keepdims=True)


def asked_rows(fb_ref, asked_buf):
    shard, shards, zh, y = place()
    fb = fb_ref[...]
    ny = lax.axis_size("y")
    for z in range(lax.axis_size("zh")):
        for t in range(2):
            asked = asked_of(fb, t, shard + (z - zh) * ny, shards)
            asked_buf[z, t] = jnp.broadcast_to(asked, asked_buf.shape[2:])


def asked_by(asked_buf, z, t, reader, rows):
    row = reader if t == 0 else asked_buf.shape[2] - 1 - reader
    return jnp.broadcast_to(asked_buf[z, t, pl.ds(row, 1)], (rows, 2 * HD))


def pack_kernel(fb_ref, own_ref, partner_ref, out_ref, up_ref, down_ref, asked_buf, kv_buf, out_buf, sems):
    shard, shards, zh, y = place()
    ny = lax.axis_size("y")
    asked_rows(fb_ref, asked_buf)
    kv_buf[zh] = own_ref[...]
    kv_buf[1 - zh] = partner_ref[...]
    up_ref[...] = kv_buf[jnp.where(y == ny - 1, 1 - zh, zh)]
    down_ref[...] = kv_buf[jnp.where(y == 0, 1 - zh, zh)]
    copies = []
    for p, reader in enumerate(plane_readers(zh)):
        for z in range(2):
            for t in range(2):
                second = asked_by(asked_buf, z, t, reader, BLK) == 2
                for which in range(2):
                    out_buf[2 * p + z, part(t, which)] = jnp.where(
                        second, kv_buf[z, t, which, BLK:], kv_buf[z, t, which, :BLK]
                    )
        if p % 4 == 3:
            done = pl.ds(2 * p - 6, 8)
            copies.append(pltpu.make_async_copy(out_buf.at[done], out_ref.at[done], sems.at[p // 4]))
            copies[-1].start()
    for copy in copies:
        copy.wait()


def stage(fb_ref, t, kv_ref, prev_ref, next_ref, far_ref, kbuf, vbuf):
    shard, shards, zh, y = place()
    for which, buf in ((0, kbuf), (1, vbuf)):
        buf[0:128] = prev_ref[t, which]
        buf[128:256] = kv_ref[t, which]
        buf[256:384] = next_ref[t, which]
    for f in range(fb_ref.shape[1]):
        _, slot = listed(fb_ref, t, shard, shards, f)
        rows = slice(STEP + f * BLK, STEP + (f + 1) * BLK)
        kbuf[rows] = far_ref[slot, part(t, 0)]
        vbuf[rows] = far_ref[slot, part(t, 1)]


def biased(fb_ref, t, slopes_ref, q2, kbuf, put):
    shard, shards, zh, y = place()
    cols = q2.shape[0]
    half = cols // 2
    head_col = lax.broadcasted_iota(jnp.int32, (1, cols), 1)
    slope = jnp.where(head_col < half, slopes_ref[0], slopes_ref[1])
    r = lax.broadcasted_iota(jnp.int32, (STEP, cols), 0)
    c = lax.broadcasted_iota(jnp.int32, (STEP, cols), 1)
    c = jnp.where(c < half, c, c - half)
    delta = r - 128 - c
    low = jnp.where(shard > 0, 0, 128)
    high = jnp.where(shard < shards - 1, STEP, 256)
    edge = jnp.where(c < BLK, 0, BLK)
    ok = (r >= jnp.maximum(edge, low)) & (r < jnp.minimum(edge + 320, high))
    scores = dot(kbuf[0:STEP], q2, NT) - slope * jnp.abs(delta).astype(f32)
    scores = jnp.where(ok, scores, masked_value)
    put(0, STEP, scores)
    top = jnp.max(scores, axis=0, keepdims=True)
    far_bias = slope * (-float((BAND + 1) * BLK))
    for lo in range(STEP, kbuf.shape[0], STEP):
        scores = dot(kbuf[lo : lo + STEP], q2, NT)
        parts = []
        for i in range(STEP // BLK):
            there, _ = listed(fb_ref, t, shard, shards, (lo - STEP) // BLK + i)
            row = jnp.where(there, far_bias, masked_value)
            parts.append(scores[i * BLK : (i + 1) * BLK] + row)
        scores = jnp.concatenate(parts, axis=0)
        put(lo, lo + STEP, scores)
        top = jnp.maximum(top, jnp.max(scores, axis=0, keepdims=True))
    return top


def context_grad_kernel(ref0, ref2, ref4, ref6, odd_ref, weight_ref, out_ref, buf):
    count, rows, _ = buf.shape
    got = [x for k, ref in enumerate((ref0, ref2, ref4, ref6)) for x in (ref[...], odd_ref[k])]
    got = jnp.concatenate(got, axis=0)
    out = dot(got, weight_ref[...], NT).astype(bf16)
    for k in range(count):
        buf[k] = out[k * rows : (k + 1) * rows]
    at = lax.axis_index("tp")
    for k in range(count):
        out_ref[k * rows : (k + 1) * rows] = buf[lax.bitwise_xor(at, k)]


def attend_kernel(
    fb_ref, slopes_ref, q_ref, kv_ref, prev_ref, next_ref, far_ref, grad_ref, mirrored_ref,
    ctx_ref, rev_ref, gq_ref, own_out, prev_out, next_out, far_out,
    kbuf, vbuf, pbuf, dbuf, far_buf0, far_buf1, sems,
):
    shard, shards, zh, y = place()
    n = 2 * HD
    eye = one_hot(n, lambda r: r)
    total = kbuf.shape[0]
    copies = []
    for t in range(2):
        far_buf = (far_buf0, far_buf1)[t]
        stage(fb_ref, t, kv_ref, prev_ref, next_ref, far_ref, kbuf, vbuf)
        q2 = two_heads(q_ref[t] * HD ** (-0.5))
        g2 = two_heads(flipped(mirrored_ref[...]) if t == 1 else grad_ref[...])
        cols = q2.shape[0]

        def put(lo, hi, scores):
            pbuf[lo:hi] = scores

        top = biased(fb_ref, t, slopes_ref, q2, kbuf, put)
        norm = jnp.zeros((1, cols), f32)
        row_dot = jnp.zeros((1, cols), f32)
        for lo in range(0, total, STEP):
            w = jnp.exp(pbuf[lo : lo + STEP] - top)
            gp = dot(vbuf[lo : lo + STEP], g2, NT)
            pbuf[lo : lo + STEP] = w
            dbuf[lo : lo + STEP] = gp
            norm = norm + jnp.sum(w, axis=0, keepdims=True)
            row_dot = row_dot + jnp.sum(w * gp, axis=0, keepdims=True)
        inv = 1.0 / norm
        row_dot = row_dot * inv
        gq_acc = jnp.zeros((n, cols), f32)
        ctx_acc = jnp.zeros((n, cols), f32)
        for lo in range(0, total, STEP):
            p = pbuf[lo : lo + STEP] * inv
            low = p.astype(bf16)
            ds = (p * (dbuf[lo : lo + STEP] - row_dot)).astype(bf16)
            vt = dot(eye, vbuf[lo : lo + STEP], NT).astype(bf16)
            ctx_acc = ctx_acc + dot(vt, low, NN)
            kt = dot(eye, kbuf[lo : lo + STEP], NT).astype(bf16)
            gq_acc = gq_acc + dot(kt, ds, NN)
            for which, x in ((0, dot(ds, q2, NN)), (1, dot(low, g2, NN))):
                if lo == 0:
                    prev_out[t, which] = x[0:128].astype(bf16)
                    own_out[t, which] = x[128:256]
                    next_out[t, which] = x[256:384].astype(bf16)
                else:
                    x = x.astype(bf16)
                    for i in range(STEP // BLK):
                        there, slot = listed(fb_ref, t, shard, shards, (lo - STEP) // BLK + i)

                        @pl.when(there)
                        def _():
                            far_buf[slot, which * BLK : (which + 1) * BLK] = x[i * BLK : (i + 1) * BLK]

        copies.append(pltpu.make_async_copy(far_buf, far_out.at[:, 2 * t * BLK : 2 * (t + 1) * BLK], sems.at[t]))
        copies[-1].start()
        gq_ref[t] = (pick_heads(gq_acc) * HD ** (-0.5)).astype(bf16)
        ctx = pick_heads(ctx_acc).astype(bf16)
        if t == 1:
            rev_ref[...] = flipped(ctx)
        else:
            ctx_ref[...] = ctx
    for copy in copies:
        copy.wait()


def combine_kernel(fb_ref, own_ref, prev_ref, next_ref, far_ref, mine_ref, other_ref, asked_buf, sum_buf):
    shard, shards, zh, y = place()
    last = lax.axis_size("y") - 1
    asked_rows(fb_ref, asked_buf)
    rows = 32
    for z in range(2):
        for t in range(2):
            for which in range(2):
                for lo in range(0, BLK, rows):
                    first = jnp.zeros((rows, 2 * HD), f32)
                    second = jnp.zeros((rows, 2 * HD), f32)
                    at = part(t, which).start + lo
                    for p, reader in enumerate(plane_readers(zh)):
                        block = asked_by(asked_buf, z, t, reader, rows)
                        x = far_ref[2 * p + z, at : at + rows].astype(f32)
                        first = first + jnp.where(block == 1, x, 0.0)
                        second = second + jnp.where(block == 2, x, 0.0)
                    sum_buf[z, t, which, lo : lo + rows] = first
                    sum_buf[z, t, which, BLK + lo : BLK + lo + rows] = second
    sum_buf[zh] = sum_buf[zh] + own_ref[...]
    to = jnp.where(y == 0, 1 - zh, zh)
    sum_buf[to] = sum_buf[to] + prev_ref[...].astype(f32)
    to = jnp.where(y == last, 1 - zh, zh)
    sum_buf[to] = sum_buf[to] + next_ref[...].astype(f32)
    mine_ref[...] = sum_buf[zh]
    other_ref[...] = sum_buf[1 - zh].astype(bf16)


def finish_kernel(mine_ref, other_ref, gk_ref, gv_ref):
    for which, ref in ((0, gk_ref), (1, gv_ref)):
        ref[...] = (mine_ref[:, which] + other_ref[:, which].astype(f32)).astype(bf16)


def project_kernel(ctx_ref, back_ref, weight_ref, even_ref, odd_ref, sum_buf):
    total = (ctx_ref[...].astype(f32) + back_ref[...].astype(f32)).astype(bf16)
    count, rows, _ = sum_buf.shape
    for k in range(count):
        sum_buf[k] = total[k * rows : (k + 1) * rows]
    at = lax.axis_index("tp")
    blocks = jnp.concatenate([sum_buf[lax.bitwise_xor(at, j)] for j in range(count)], axis=0)
    out = dot(blocks, weight_ref[...], NN)
    for j in range(count):
        ref = (even_ref, odd_ref)[j % 2]
        ref[j // 2] = out[j * rows : (j + 1) * rows].astype(ref.dtype)


def smem():
    return pl.BlockSpec(memory_space=pltpu.SMEM)


def vmem():
    return pl.BlockSpec(memory_space=pltpu.VMEM)


def hbm():
    return pl.BlockSpec(memory_space=pltpu.HBM)


def shape(dims, dtype=bf16):
    return jax.ShapeDtypeStruct(dims, dtype)


def cost(flops, nbytes, exps=0):
    return pl.CostEstimate(flops=flops, bytes_accessed=nbytes, transcendentals=exps)


def swap(x, bit):
    count = lax.axis_size("tp")
    return lax.ppermute(x, "tp", [(i, i ^ bit) for i in range(count)])


def per_device(
    residual, queries, keys, values, slopes, out_weight, cotangent, far_blocks, far_count
):
    nx, nz, ny = (lax.axis_size(a) for a in SEQ)
    seq_count = nx * nz * ny
    tp_count = lax.axis_size("tp")
    tok_rows, width = queries.shape[1:]
    total_keys = 3 * tok_rows + far_blocks.shape[1] * BLK
    model = out_weight.shape[1]
    cols = 2 * tok_rows
    both = (2, 2, tok_rows, width)
    pieces = (tp_count, tok_rows // tp_count, width)
    slots = (seq_count, 4 * BLK, width)

    def plane_a2a(x):
        x = x.reshape(nx * ny, nz * slots[1], width)
        return lax.all_to_all(x, ("x", "y"), split_axis=0, concat_axis=0, tiled=True).reshape(slots)

    def z_swap(x):
        return lax.ppermute(x, "zh", [(i, nz - 1 - i) for i in range(nz)])

    key_value = jnp.stack([keys, values], axis=1)
    partner = z_swap(key_value)
    asked = pltpu.VMEM((nz, 2, seq_count, 2 * HD), jnp.int32)
    outgoing, to_up, to_down = pl.pallas_call(
        pack_kernel,
        out_shape=(pltpu.HBM(slots, bf16), shape(both), shape(both)),
        in_specs=[vmem()] * 3,
        out_specs=(hbm(), vmem(), vmem()),
        scratch_shapes=[
            asked, pltpu.VMEM((nz,) + both, bf16), pltpu.VMEM(slots, bf16),
            pltpu.SemaphoreType.DMA((nx * ny // 4,)),
        ],
        cost_estimate=cost(1_000_000, 2_500_000),
        compiler_params=pltpu.CompilerParams(vmem_limit_bytes=LIMIT),
        name="pack",
    )(far_blocks, key_value, partner)
    same_core = [cotangent] + [swap(cotangent, bit) for bit in (2, 4, 6)]
    other_core = swap(jnp.stack(same_core), 1)
    outgoing, other_core = lax.optimization_barrier((outgoing, other_core))
    far = plane_a2a(outgoing)

    def flat(x, zh, y):
        return (x * nz + zh) * ny + y

    places = [(x, zh, y) for x in range(nx) for zh in range(nz) for y in range(ny)]
    up, down = [], []
    for x, zh, y in places:
        if y < ny - 1:
            up.append((flat(x, zh, y), flat(x, zh, y + 1)))
        elif zh == nz - 1:
            up.append((flat(x, zh, y), flat(x, zh, 0)))
        elif x < nx - 1:
            up.append((flat(x, zh, y), flat(x + 1, zh, 0)))
        if y > 0:
            down.append((flat(x, zh, y), flat(x, zh, y - 1)))
        elif zh == 0:
            down.append((flat(x, zh, y), flat(x, zh, ny - 1)))
        elif x > 0:
            down.append((flat(x, zh, y), flat(x - 1, zh, ny - 1)))
    mirror = [(i, seq_count - 1 - i) for i in range(seq_count)]
    from_prev = lax.ppermute(to_up, SEQ, up)
    from_next = lax.ppermute(to_down, SEQ, down)

    grad_context = pl.pallas_call(
        context_grad_kernel,
        out_shape=shape((tok_rows, width)),
        in_specs=[vmem()] * 6,
        out_specs=vmem(),
        scratch_shapes=[pltpu.VMEM(pieces, bf16)],
        cost_estimate=cost(34_000_000, 600_000),
        compiler_params=pltpu.CompilerParams(vmem_limit_bytes=LIMIT),
        name="context_grad",
    )(*same_core, other_core, out_weight)
    mirrored = lax.ppermute(grad_context, SEQ, mirror)

    square = shape((tok_rows, width))
    half = pltpu.VMEM((seq_count, 2 * BLK, width), bf16)
    context_fwd, context_rev, grad_queries, own, before, after, far_grads = pl.pallas_call(
        attend_kernel,
        out_shape=(square, square, shape((2, tok_rows, width)), shape(both, f32), shape(both), shape(both), pltpu.HBM(slots, bf16)),
        in_specs=[smem()] * 2 + [vmem()] * 7,
        out_specs=(vmem(),) * 6 + (hbm(),),
        scratch_shapes=[pltpu.VMEM((total_keys, width), bf16)] * 2
        + [pltpu.VMEM((total_keys, cols), f32)] * 2
        + [half, half, pltpu.SemaphoreType.DMA((2,))],
        cost_estimate=cost(4_000_000_000, 8_000_000, 1_000_000),
        compiler_params=pltpu.CompilerParams(vmem_limit_bytes=LIMIT),
        name="attend",
    )(far_blocks, slopes, queries, key_value, from_prev, from_next, far, grad_context, mirrored)
    context_back = lax.ppermute(context_rev, SEQ, mirror)

    returned = plane_a2a(far_grads)
    from_prev_grad = lax.ppermute(after, SEQ, [(b, a) for a, b in down])
    from_next_grad = lax.ppermute(before, SEQ, [(b, a) for a, b in up])
    context_back, from_prev_grad, from_next_grad = lax.optimization_barrier(
        (context_back, from_prev_grad, from_next_grad)
    )

    even, odd = pl.pallas_call(
        project_kernel,
        out_shape=(
            shape((tp_count // 2, tok_rows // tp_count, model), f32),
            shape((tp_count // 2, tok_rows // tp_count, model)),
        ),
        in_specs=[vmem()] * 3,
        out_specs=(vmem(),) * 2,
        scratch_shapes=[pltpu.VMEM(pieces, bf16)],
        cost_estimate=cost(34_000_000, 1_000_000),
        compiler_params=pltpu.CompilerParams(vmem_limit_bytes=LIMIT),
        name="project",
    )(context_fwd, context_back, out_weight)
    held = even + swap(odd, 1).astype(f32)
    parts = [swap(held[k].astype(bf16), 2 * k) for k in range(1, tp_count // 2)]
    total = residual.astype(f32) + held[0]
    for part_here in parts:
        total = total + part_here.astype(f32)
    mixed = total.astype(bf16)

    mine, other = pl.pallas_call(
        combine_kernel,
        out_shape=(shape(both, f32), shape(both)),
        in_specs=[vmem()] * 5,
        out_specs=(vmem(),) * 2,
        scratch_shapes=[asked, pltpu.VMEM((nz,) + both, f32)],
        cost_estimate=cost(4_000_000, 3_000_000),
        compiler_params=pltpu.CompilerParams(vmem_limit_bytes=LIMIT),
        name="combine",
    )(far_blocks, own, from_prev_grad, from_next_grad, returned)
    grad_keys, grad_values = pl.pallas_call(
        finish_kernel,
        out_shape=(shape((2, tok_rows, width)),) * 2,
        in_specs=[vmem()] * 2,
        out_specs=(vmem(),) * 2,
        cost_estimate=cost(100_000, 500_000),
        compiler_params=pltpu.CompilerParams(vmem_limit_bytes=LIMIT),
        name="finish",
    )(mine, z_swap(other))
    return (mixed, grad_queries, grad_keys, grad_values)


def solution(mesh):
    split = jax.sharding.Mesh(mesh.devices.reshape(4, 2, 4, -1), SEQ + ("tp",))
    rows = P(SEQ + ("tp",), None)
    strands = P(None, SEQ, "tp")
    return jax.shard_map(
        per_device,
        mesh=split,
        in_specs=(rows, strands, strands, strands, P("tp"), P("tp", None), rows, P(), P()),
        out_specs=(rows, strands, strands, strands),
        check_vma=False,
    )
```

```python
import jax
import jax.numpy as jnp
from jax import lax
from jax.experimental import pallas as pl
from jax.experimental.pallas import tpu as pltpu
from jax.sharding import PartitionSpec as P

HD = 64
BLK = 64
BAND = 2
STEP = 384
LIMIT = 24 << 20

masked_value = -1e30
f32 = jnp.float32
bf16 = jnp.bfloat16

NT = (((1,), (1,)), ((), ()))
NN = (((1,), (0,)), ((), ()))


def dot(a, b, dims):
    return lax.dot_general(a, b, dims, preferred_element_type=f32)


def two_heads(x):
    first = lax.broadcasted_iota(jnp.int32, x.shape, 1) < HD
    zero = jnp.zeros_like(x)
    return jnp.concatenate([jnp.where(first, x, zero), jnp.where(first, zero, x)], axis=0)


def pick_heads(xt):
    rows = xt.shape[1] // 2
    own = jnp.concatenate([xt[:HD, :rows], xt[HD:, rows:]], axis=0)
    return own.T


def one_hot(n, at):
    r = lax.broadcasted_iota(jnp.int32, (n, n), 0)
    c = lax.broadcasted_iota(jnp.int32, (n, n), 1)
    return (c == at(r)).astype(bf16)


def flipped(x):
    n = x.shape[0]
    return dot(one_hot(n, lambda r: n - 1 - r), x, NN).astype(bf16)


SEQ = ("x", "zh", "y")


def place():
    x, zh, y = (lax.axis_index(a) for a in SEQ)
    nx, nz, ny = (lax.axis_size(a) for a in SEQ)
    return (x * nz + zh) * ny + y, nx * nz * ny, zh, y


def slot_of(owner, zh):
    nx, nz, ny = (lax.axis_size(a) for a in SEQ)
    xz, y = lax.div(owner, ny), lax.rem(owner, ny)
    x, z = lax.div(xz, nz), lax.rem(xz, nz)
    return jnp.where(z == zh, 0, nx * ny) + x * ny + y


def plane_readers(zh):
    nx, nz, ny = (lax.axis_size(a) for a in SEQ)
    return [(x * nz + zh) * ny + y for x in range(nx) for y in range(ny)]


def part(t, which):
    return slice((2 * t + which) * BLK, (2 * t + which + 1) * BLK)


def listed(fb_ref, t, shard, shards, zh, f):
    entry = fb_ref[shard if t == 0 else shards - 1 - shard, f]
    owner = lax.shift_right_arithmetic(entry, 1)
    owner = owner if t == 0 else shards - 1 - owner
    return entry >= 0, jnp.where(entry >= 0, slot_of(owner, zh), 0)


def asked_of(fb, t, shard, shards):
    mine = shard if t == 0 else shards - 1 - shard
    inner = fb & 1
    inner = inner + 1 if t == 0 else 2 - inner
    hit = jnp.where(lax.shift_right_arithmetic(fb, 1) == mine, inner, 0)
    return jnp.sum(hit, axis=1, keepdims=True)


def asked_rows(fb_ref, asked_buf, rel):
    shard, shards, zh, y = place()
    target = shard + rel * (1 - 2 * zh) * lax.axis_size("y")
    fb = fb_ref[...]
    for t in range(2):
        asked_buf[t] = jnp.broadcast_to(asked_of(fb, t, target, shards), asked_buf.shape[1:])


def asked_by(asked_buf, t, reader, rows):
    row = reader if t == 0 else asked_buf.shape[1] - 1 - reader
    return jnp.broadcast_to(asked_buf[t, pl.ds(row, 1)], (rows, 2 * HD))


def pack(fb_ref, kv_ref, out_ref, asked_buf, out_buf, sems, rel):
    shard, shards, zh, y = place()
    asked_rows(fb_ref, asked_buf, rel)
    copies = []
    for p, reader in enumerate(plane_readers(zh)):
        for t in range(2):
            second = asked_by(asked_buf, t, reader, BLK) == 2
            for which in range(2):
                out_buf[p, part(t, which)] = jnp.where(second, kv_ref[t, which, BLK:], kv_ref[t, which, :BLK])
        if p % 4 == 3:
            done = pl.ds(p - 3, 4)
            copies.append(pltpu.make_async_copy(out_buf.at[done], out_ref.at[done], sems.at[p // 4]))
            copies[-1].start()
    return copies


def pack_own_kernel(fb_ref, key_ref, value_ref, out_ref, kv_ref, asked_buf, out_buf, sems):
    kv_ref[:, 0] = key_ref[...]
    kv_ref[:, 1] = value_ref[...]
    for copy in pack(fb_ref, kv_ref, out_ref, asked_buf, out_buf, sems, 0):
        copy.wait()


def pack_partner_kernel(fb_ref, own_ref, partner_ref, out_ref, up_ref, down_ref, asked_buf, out_buf, sems):
    shard, shards, zh, y = place()
    copies = pack(fb_ref, partner_ref, out_ref, asked_buf, out_buf, sems, 1)
    up_ref[...] = jnp.where(y == lax.axis_size("y") - 1, partner_ref[...], own_ref[...])
    down_ref[...] = jnp.where(y == 0, partner_ref[...], own_ref[...])
    for copy in copies:
        copy.wait()


def stage(fb_ref, t, kv_ref, prev_ref, next_ref, far_refs, kbuf, vbuf):
    shard, shards, zh, y = place()
    plane = far_refs[0].shape[0]
    for which, buf in ((0, kbuf), (1, vbuf)):
        buf[0:128] = prev_ref[t, which]
        buf[128:256] = kv_ref[t, which]
        buf[256:384] = next_ref[t, which]
    for f in range(fb_ref.shape[1]):
        _, slot = listed(fb_ref, t, shard, shards, zh, f)
        rows = slice(STEP + f * BLK, STEP + (f + 1) * BLK)
        here = slot < plane
        at = jnp.where(here, slot, slot - plane)
        for which, buf in ((0, kbuf), (1, vbuf)):
            buf[rows] = jnp.where(here, *(ref[at, part(t, which)] for ref in far_refs))


def biased(fb_ref, t, slopes_ref, q2, kbuf, put):
    shard, shards, zh, y = place()
    cols = q2.shape[0]
    half = cols // 2
    head_col = lax.broadcasted_iota(jnp.int32, (1, cols), 1)
    slope = jnp.where(head_col < half, slopes_ref[0], slopes_ref[1])
    r = lax.broadcasted_iota(jnp.int32, (STEP, cols), 0)
    c = lax.broadcasted_iota(jnp.int32, (STEP, cols), 1)
    c = jnp.where(c < half, c, c - half)
    delta = r - 128 - c
    low = jnp.where(shard > 0, 0, 128)
    high = jnp.where(shard < shards - 1, STEP, 256)
    edge = jnp.where(c < BLK, 0, BLK)
    ok = (r >= jnp.maximum(edge, low)) & (r < jnp.minimum(edge + 320, high))
    scores = dot(kbuf[0:STEP], q2, NT) - slope * jnp.abs(delta).astype(f32)
    scores = jnp.where(ok, scores, masked_value)
    put(0, STEP, scores)
    top = jnp.max(scores, axis=0, keepdims=True)
    far_bias = slope * (-float((BAND + 1) * BLK))
    for lo in range(STEP, kbuf.shape[0], STEP):
        scores = dot(kbuf[lo : lo + STEP], q2, NT)
        parts = []
        for i in range(STEP // BLK):
            there, _ = listed(fb_ref, t, shard, shards, zh, (lo - STEP) // BLK + i)
            row = jnp.where(there, far_bias, masked_value)
            parts.append(scores[i * BLK : (i + 1) * BLK] + row)
        scores = jnp.concatenate(parts, axis=0)
        put(lo, lo + STEP, scores)
        top = jnp.maximum(top, jnp.max(scores, axis=0, keepdims=True))
    return top


def context_grad_kernel(ref0, ref2, ref4, ref6, odd_ref, weight_ref, out_ref, buf):
    count, rows, _ = buf.shape
    got = [x for k, ref in enumerate((ref0, ref2, ref4, ref6)) for x in (ref[...], odd_ref[k])]
    got = jnp.concatenate(got, axis=0)
    out = dot(got, weight_ref[...], NT).astype(bf16)
    for k in range(count):
        buf[k] = out[k * rows : (k + 1) * rows]
    at = lax.axis_index("tp")
    for k in range(count):
        out_ref[k * rows : (k + 1) * rows] = buf[lax.bitwise_xor(at, k)]


def attend_kernel(
    fb_ref, slopes_ref, q_ref, kv_ref, prev_ref, next_ref, far_own, far_partner, grad_ref, mirrored_ref,
    ctx_ref, rev_ref, gq_ref, own_out, prev_out, next_out, partner_out, here_out,
    kbuf, vbuf, pbuf, dbuf, far_buf0, far_buf1, sems,
):
    shard, shards, zh, y = place()
    n = 2 * HD
    eye = one_hot(n, lambda r: r)
    total = kbuf.shape[0]
    copies = []
    for t in range(2):
        far_buf = (far_buf0, far_buf1)[t]
        stage(fb_ref, t, kv_ref, prev_ref, next_ref, (far_own, far_partner), kbuf, vbuf)
        q2 = two_heads(q_ref[t] * HD ** (-0.5))
        g2 = two_heads(flipped(mirrored_ref[...]) if t == 1 else grad_ref[...])
        cols = q2.shape[0]

        def put(lo, hi, scores):
            pbuf[lo:hi] = scores

        top = biased(fb_ref, t, slopes_ref, q2, kbuf, put)
        norm = jnp.zeros((1, cols), f32)
        row_dot = jnp.zeros((1, cols), f32)
        for lo in range(0, total, STEP):
            w = jnp.exp(pbuf[lo : lo + STEP] - top)
            gp = dot(vbuf[lo : lo + STEP], g2, NT)
            pbuf[lo : lo + STEP] = w
            dbuf[lo : lo + STEP] = gp
            norm = norm + jnp.sum(w, axis=0, keepdims=True)
            row_dot = row_dot + jnp.sum(w * gp, axis=0, keepdims=True)
        inv = 1.0 / norm
        row_dot = row_dot * inv
        gq_acc = jnp.zeros((n, cols), f32)
        ctx_acc = jnp.zeros((n, cols), f32)
        for lo in range(0, total, STEP):
            p = pbuf[lo : lo + STEP] * inv
            low = p.astype(bf16)
            ds = (p * (dbuf[lo : lo + STEP] - row_dot)).astype(bf16)
            vt = dot(eye, vbuf[lo : lo + STEP], NT).astype(bf16)
            ctx_acc = ctx_acc + dot(vt, low, NN)
            kt = dot(eye, kbuf[lo : lo + STEP], NT).astype(bf16)
            gq_acc = gq_acc + dot(kt, ds, NN)
            for which, x in ((0, dot(ds, q2, NN)), (1, dot(low, g2, NN))):
                if lo == 0:
                    prev_out[t, which] = x[0:128].astype(bf16)
                    own_out[t, which] = x[128:256]
                    next_out[t, which] = x[256:384].astype(bf16)
                else:
                    x = x.astype(bf16)
                    for i in range(STEP // BLK):
                        there, slot = listed(fb_ref, t, shard, shards, zh, (lo - STEP) // BLK + i)

                        @pl.when(there)
                        def _():
                            far_buf[slot, which * BLK : (which + 1) * BLK] = x[i * BLK : (i + 1) * BLK]

        plane = far_own.shape[0]
        for k, (out, rows) in enumerate(((here_out, pl.ds(0, plane)), (partner_out, pl.ds(plane, plane)))):
            to = out.at[:, 2 * t * BLK : 2 * (t + 1) * BLK]
            copies.append(pltpu.make_async_copy(far_buf.at[rows], to, sems.at[t, k]))
            copies[-1].start()
        gq_ref[t] = (pick_heads(gq_acc) * HD ** (-0.5)).astype(bf16)
        ctx = pick_heads(ctx_acc).astype(bf16)
        if t == 1:
            rev_ref[...] = flipped(ctx)
        else:
            ctx_ref[...] = ctx
    for copy in copies:
        copy.wait()


def combine(fb_ref, far_ref, asked_buf, rel, put):
    shard, shards, zh, y = place()
    asked_rows(fb_ref, asked_buf, rel)
    rows = 32
    for t in range(2):
        for which in range(2):
            for lo in range(0, BLK, rows):
                first = jnp.zeros((rows, 2 * HD), f32)
                second = jnp.zeros((rows, 2 * HD), f32)
                at = part(t, which).start + lo
                for p, reader in enumerate(plane_readers(zh)):
                    block = asked_by(asked_buf, t, reader, rows)
                    x = far_ref[p, at : at + rows].astype(f32)
                    first = first + jnp.where(block == 1, x, 0.0)
                    second = second + jnp.where(block == 2, x, 0.0)
                put(t, which, slice(lo, lo + rows), first)
                put(t, which, slice(BLK + lo, BLK + lo + rows), second)


def combine_partner_kernel(fb_ref, prev_ref, next_ref, far_ref, out_ref, asked_buf):
    shard, shards, zh, y = place()
    last = lax.axis_size("y") - 1

    def put(t, which, rows, far):
        far = far + jnp.where(y == 0, prev_ref[t, which, rows].astype(f32), 0.0)
        far = far + jnp.where(y == last, next_ref[t, which, rows].astype(f32), 0.0)
        out_ref[t, which, rows] = far.astype(bf16)

    combine(fb_ref, far_ref, asked_buf, 1, put)


def combine_own_kernel(fb_ref, own_ref, prev_ref, next_ref, other_ref, far_ref, gk_ref, gv_ref, asked_buf):
    shard, shards, zh, y = place()
    last = lax.axis_size("y") - 1

    def put(t, which, rows, far):
        total = own_ref[t, which, rows] + jnp.where(y == 0, 0.0, prev_ref[t, which, rows].astype(f32))
        total = total + jnp.where(y == last, 0.0, next_ref[t, which, rows].astype(f32))
        total = total + other_ref[t, which, rows].astype(f32) + far
        (gk_ref, gv_ref)[which][t, rows] = total.astype(bf16)

    combine(fb_ref, far_ref, asked_buf, 0, put)


def project_kernel(ctx_ref, back_ref, weight_ref, even_ref, odd_ref, sum_buf):
    total = (ctx_ref[...].astype(f32) + back_ref[...].astype(f32)).astype(bf16)
    count, rows, _ = sum_buf.shape
    for k in range(count):
        sum_buf[k] = total[k * rows : (k + 1) * rows]
    at = lax.axis_index("tp")
    blocks = jnp.concatenate([sum_buf[lax.bitwise_xor(at, j)] for j in range(count)], axis=0)
    out = dot(blocks, weight_ref[...], NN)
    for j in range(count):
        ref = (even_ref, odd_ref)[j % 2]
        ref[j // 2] = out[j * rows : (j + 1) * rows].astype(ref.dtype)


def smem():
    return pl.BlockSpec(memory_space=pltpu.SMEM)


def vmem():
    return pl.BlockSpec(memory_space=pltpu.VMEM)


def hbm():
    return pl.BlockSpec(memory_space=pltpu.HBM)


def shape(dims, dtype=bf16):
    return jax.ShapeDtypeStruct(dims, dtype)


def cost(flops, nbytes, exps=0):
    return pl.CostEstimate(flops=flops, bytes_accessed=nbytes, transcendentals=exps)


def swap(x, bit):
    count = lax.axis_size("tp")
    return lax.ppermute(x, "tp", [(i, i ^ bit) for i in range(count)])


def per_device(
    residual, queries, keys, values, slopes, out_weight, cotangent, far_blocks, far_count
):
    nx, nz, ny = (lax.axis_size(a) for a in SEQ)
    seq_count = nx * nz * ny
    tp_count = lax.axis_size("tp")
    tok_rows, width = queries.shape[1:]
    total_keys = 3 * tok_rows + far_blocks.shape[1] * BLK
    model = out_weight.shape[1]
    cols = 2 * tok_rows
    both = (2, 2, tok_rows, width)
    pieces = (tp_count, tok_rows // tp_count, width)
    slots = (nx * ny, 4 * BLK, width)

    def plane_a2a(x):
        return lax.all_to_all(x, ("x", "y"), split_axis=0, concat_axis=0, tiled=True)

    def z_swap(x):
        return lax.ppermute(x, "zh", [(i, nz - 1 - i) for i in range(nz)])

    asked = pltpu.VMEM((2, seq_count, 2 * HD), jnp.int32)
    packed = [asked, pltpu.VMEM(slots, bf16), pltpu.SemaphoreType.DMA((nx * ny // 4,))]
    outgoing, key_value = pl.pallas_call(
        pack_own_kernel,
        out_shape=(pltpu.HBM(slots, bf16), shape(both)),
        in_specs=[vmem()] * 3,
        out_specs=(hbm(), vmem()),
        scratch_shapes=packed,
        cost_estimate=cost(500_000, 1_500_000),
        compiler_params=pltpu.CompilerParams(vmem_limit_bytes=LIMIT),
        name="pack_own",
    )(far_blocks, keys, values)
    far_own = plane_a2a(outgoing)
    partner = z_swap(key_value)
    outgoing, to_up, to_down = pl.pallas_call(
        pack_partner_kernel,
        out_shape=(pltpu.HBM(slots, bf16), shape(both), shape(both)),
        in_specs=[vmem()] * 3,
        out_specs=(hbm(), vmem(), vmem()),
        scratch_shapes=packed,
        cost_estimate=cost(500_000, 1_500_000),
        compiler_params=pltpu.CompilerParams(vmem_limit_bytes=LIMIT),
        name="pack_partner",
    )(far_blocks, key_value, partner)
    same_core = [cotangent] + [swap(cotangent, bit) for bit in (2, 4, 6)]
    other_core = swap(jnp.stack(same_core), 1)
    outgoing, other_core = lax.optimization_barrier((outgoing, other_core))
    far_partner = plane_a2a(outgoing)

    def flat(x, zh, y):
        return (x * nz + zh) * ny + y

    places = [(x, zh, y) for x in range(nx) for zh in range(nz) for y in range(ny)]
    up, down = [], []
    for x, zh, y in places:
        if y < ny - 1:
            up.append((flat(x, zh, y), flat(x, zh, y + 1)))
        elif zh == nz - 1:
            up.append((flat(x, zh, y), flat(x, zh, 0)))
        elif x < nx - 1:
            up.append((flat(x, zh, y), flat(x + 1, zh, 0)))
        if y > 0:
            down.append((flat(x, zh, y), flat(x, zh, y - 1)))
        elif zh == 0:
            down.append((flat(x, zh, y), flat(x, zh, ny - 1)))
        elif x > 0:
            down.append((flat(x, zh, y), flat(x - 1, zh, ny - 1)))
    mirror = [(i, seq_count - 1 - i) for i in range(seq_count)]
    from_prev = lax.ppermute(to_up, SEQ, up)
    from_next = lax.ppermute(to_down, SEQ, down)

    grad_context = pl.pallas_call(
        context_grad_kernel,
        out_shape=shape((tok_rows, width)),
        in_specs=[vmem()] * 6,
        out_specs=vmem(),
        scratch_shapes=[pltpu.VMEM(pieces, bf16)],
        cost_estimate=cost(34_000_000, 600_000),
        compiler_params=pltpu.CompilerParams(vmem_limit_bytes=LIMIT),
        name="context_grad",
    )(*same_core, other_core, out_weight)
    mirrored = lax.ppermute(grad_context, SEQ, mirror)

    square = shape((tok_rows, width))
    half = pltpu.VMEM((seq_count, 2 * BLK, width), bf16)
    context_fwd, context_rev, grad_queries, own, before, after, partner_grads, here_grads = pl.pallas_call(
        attend_kernel,
        out_shape=(square, square, shape((2, tok_rows, width)), shape(both, f32), shape(both), shape(both))
        + (pltpu.HBM(slots, bf16),) * 2,
        in_specs=[smem()] * 2 + [vmem()] * 8,
        out_specs=(vmem(),) * 6 + (hbm(),) * 2,
        scratch_shapes=[pltpu.VMEM((total_keys, width), bf16)] * 2
        + [pltpu.VMEM((total_keys, cols), f32)] * 2
        + [half, half, pltpu.SemaphoreType.DMA((2, 2))],
        cost_estimate=cost(4_000_000_000, 8_000_000, 1_000_000),
        compiler_params=pltpu.CompilerParams(vmem_limit_bytes=LIMIT),
        name="attend",
    )(far_blocks, slopes, queries, key_value, from_prev, from_next, far_own, far_partner, grad_context, mirrored)
    context_back = lax.ppermute(context_rev, SEQ, mirror)

    returned_partner = plane_a2a(partner_grads)
    from_prev_grad = lax.ppermute(after, SEQ, [(b, a) for a, b in down])
    from_next_grad = lax.ppermute(before, SEQ, [(b, a) for a, b in up])
    here_grads, returned_partner, context_back = lax.optimization_barrier(
        (here_grads, returned_partner, context_back)
    )
    returned_own = plane_a2a(here_grads)
    other = pl.pallas_call(
        combine_partner_kernel,
        out_shape=shape(both),
        in_specs=[vmem()] * 4,
        out_specs=vmem(),
        scratch_shapes=[asked],
        cost_estimate=cost(2_000_000, 1_500_000),
        compiler_params=pltpu.CompilerParams(vmem_limit_bytes=LIMIT),
        name="combine_partner",
    )(far_blocks, from_prev_grad, from_next_grad, returned_partner)
    other, context_back = lax.optimization_barrier((other, context_back))
    other = z_swap(other)

    even, odd = pl.pallas_call(
        project_kernel,
        out_shape=(
            shape((tp_count // 2, tok_rows // tp_count, model), f32),
            shape((tp_count // 2, tok_rows // tp_count, model)),
        ),
        in_specs=[vmem()] * 3,
        out_specs=(vmem(),) * 2,
        scratch_shapes=[pltpu.VMEM(pieces, bf16)],
        cost_estimate=cost(34_000_000, 1_000_000),
        compiler_params=pltpu.CompilerParams(vmem_limit_bytes=LIMIT),
        name="project",
    )(context_fwd, context_back, out_weight)
    held = even + swap(odd, 1).astype(f32)
    parts = [swap(held[k].astype(bf16), 2 * k) for k in range(1, tp_count // 2)]
    total = residual.astype(f32) + held[0]
    for part_here in parts:
        total = total + part_here.astype(f32)
    mixed = total.astype(bf16)

    grad_keys, grad_values = pl.pallas_call(
        combine_own_kernel,
        out_shape=(shape((2, tok_rows, width)),) * 2,
        in_specs=[vmem()] * 6,
        out_specs=(vmem(),) * 2,
        scratch_shapes=[asked],
        cost_estimate=cost(2_000_000, 1_500_000),
        compiler_params=pltpu.CompilerParams(vmem_limit_bytes=LIMIT),
        name="combine_own",
    )(far_blocks, own, from_prev_grad, from_next_grad, other, returned_own)
    return (mixed, grad_queries, grad_keys, grad_values)


def solution(mesh):
    split = jax.sharding.Mesh(mesh.devices.reshape(4, 2, 4, -1), SEQ + ("tp",))
    rows = P(SEQ + ("tp",), None)
    strands = P(None, SEQ, "tp")
    return jax.shard_map(
        per_device,
        mesh=split,
        in_specs=(rows, strands, strands, strands, P("tp"), P("tp", None), rows, P(), P()),
        out_specs=(rows, strands, strands, strands),
        check_vma=False,
    )
```

```python
import jax
import jax.numpy as jnp
from jax import lax
from jax.experimental import pallas as pl
from jax.experimental.pallas import tpu as pltpu
from jax.sharding import PartitionSpec as P

HD = 64
BLK = 64
BAND = 2
STEP = 384
LIMIT = 24 << 20

masked_value = -1e30
f32 = jnp.float32
bf16 = jnp.bfloat16

NT = (((1,), (1,)), ((), ()))
NN = (((1,), (0,)), ((), ()))


def dot(a, b, dims):
    return lax.dot_general(a, b, dims, preferred_element_type=f32)


def two_heads(x):
    first = lax.broadcasted_iota(jnp.int32, x.shape, 1) < HD
    zero = jnp.zeros_like(x)
    return jnp.concatenate([jnp.where(first, x, zero), jnp.where(first, zero, x)], axis=0)


def pick_heads(xt):
    rows = xt.shape[1] // 2
    own = jnp.concatenate([xt[:HD, :rows], xt[HD:, rows:]], axis=0)
    return own.T


def one_hot(n, at):
    r = lax.broadcasted_iota(jnp.int32, (n, n), 0)
    c = lax.broadcasted_iota(jnp.int32, (n, n), 1)
    return (c == at(r)).astype(bf16)


def flipped(x):
    n = x.shape[0]
    return dot(one_hot(n, lambda r: n - 1 - r), x, NN).astype(bf16)


SEQ = ("x", "zh", "y")


def place():
    x, zh, y = (lax.axis_index(a) for a in SEQ)
    nx, nz, ny = (lax.axis_size(a) for a in SEQ)
    return (x * nz + zh) * ny + y, nx * nz * ny, zh, y


def slot_of(owner, zh):
    nz, ny = lax.axis_size("zh"), lax.axis_size("y")
    xz, y = lax.div(owner, ny), lax.rem(owner, ny)
    x, z = lax.div(xz, nz), lax.rem(xz, nz)
    return 2 * (x * ny + y) + jnp.where(z == zh, 0, 1)


def plane_readers(zh):
    nx, nz, ny = (lax.axis_size(a) for a in SEQ)
    return [(x * nz + zh) * ny + y for x in range(nx) for y in range(ny)]


def part(t, which):
    return slice((2 * t + which) * BLK, (2 * t + which + 1) * BLK)


def listed(fb_ref, t, shard, shards, zh, f):
    entry = fb_ref[shard if t == 0 else shards - 1 - shard, f]
    owner = lax.shift_right_arithmetic(entry, 1)
    owner = owner if t == 0 else shards - 1 - owner
    return entry >= 0, jnp.where(entry >= 0, slot_of(owner, zh), 0)


def asked_of(fb, t, shard, shards):
    mine = shard if t == 0 else shards - 1 - shard
    inner = fb & 1
    inner = inner + 1 if t == 0 else 2 - inner
    hit = jnp.where(lax.shift_right_arithmetic(fb, 1) == mine, inner, 0)
    return jnp.sum(hit, axis=1, keepdims=True)


def asked_rows(fb_ref, asked_buf, rel):
    shard, shards, zh, y = place()
    target = shard + rel * (1 - 2 * zh) * lax.axis_size("y")
    fb = fb_ref[...]
    for t in range(2):
        asked_buf[t] = jnp.broadcast_to(asked_of(fb, t, target, shards), asked_buf.shape[1:])


def asked_by(asked_buf, t, reader, rows):
    row = reader if t == 0 else asked_buf.shape[1] - 1 - reader
    return jnp.broadcast_to(asked_buf[t, pl.ds(row, 1)], (rows, 2 * HD))


def load_kernel(key_ref, value_ref, cot_ref, out_ref, sems):
    rows, lanes = cot_ref.shape[0], out_ref.shape[2]
    copies = []
    for t in range(2):
        for which, ref in ((0, key_ref), (1, value_ref)):
            copies.append((ref.at[t], out_ref.at[2 * t + which]))
    for k in range(cot_ref.shape[1] // lanes):
        copies.append((cot_ref.at[:, pl.ds(k * lanes, lanes)], out_ref.at[4, pl.ds(k * rows, rows)]))
    copies = [pltpu.make_async_copy(a, b, sems.at[n]) for n, (a, b) in enumerate(copies)]
    for copy in copies:
        copy.start()
    for copy in copies:
        copy.wait()


def pack_kernel(fb_ref, own_ref, partner_ref, out_ref, up_ref, down_ref, asked_buf, out_buf, sems):
    shard, shards, zh, y = place()
    readers = plane_readers(zh)
    copies = []
    for rel, kv_ref in ((0, own_ref), (1, partner_ref)):
        asked_rows(fb_ref, asked_buf, rel)
        for p, reader in enumerate(readers):
            for t in range(2):
                second = asked_by(asked_buf, t, reader, BLK) == 2
                for which in range(2):
                    kv = kv_ref.at[2 * t + which]
                    out_buf[2 * p + rel, part(t, which)] = jnp.where(second, kv[BLK:], kv[:BLK])
            if rel == 1 and p % 4 == 3:
                done = pl.ds(2 * p - 6, 8)
                copies.append(pltpu.make_async_copy(out_buf.at[done], out_ref.at[done], sems.at[p // 4]))
                copies[-1].start()
    for k in range(4):
        up_ref[k] = jnp.where(y == lax.axis_size("y") - 1, partner_ref[k], own_ref[k])
        down_ref[k] = jnp.where(y == 0, partner_ref[k], own_ref[k])
    for copy in copies:
        copy.wait()


def stage(fb_ref, t, kv_ref, prev_ref, next_ref, far_ref, kbuf, vbuf):
    shard, shards, zh, y = place()
    for which, buf in ((0, kbuf), (1, vbuf)):
        buf[0:128] = prev_ref[2 * t + which]
        buf[128:256] = kv_ref[2 * t + which]
        buf[256:384] = next_ref[2 * t + which]
    for f in range(fb_ref.shape[1]):
        _, slot = listed(fb_ref, t, shard, shards, zh, f)
        rows = slice(STEP + f * BLK, STEP + (f + 1) * BLK)
        for which, buf in ((0, kbuf), (1, vbuf)):
            buf[rows] = far_ref[slot, part(t, which)]


def biased(fb_ref, t, slopes_ref, q2, kbuf, put):
    shard, shards, zh, y = place()
    cols = q2.shape[0]
    half = cols // 2
    head_col = lax.broadcasted_iota(jnp.int32, (1, cols), 1)
    slope = jnp.where(head_col < half, slopes_ref[0], slopes_ref[1])
    r = lax.broadcasted_iota(jnp.int32, (STEP, cols), 0)
    c = lax.broadcasted_iota(jnp.int32, (STEP, cols), 1)
    c = jnp.where(c < half, c, c - half)
    delta = r - 128 - c
    low = jnp.where(shard > 0, 0, 128)
    high = jnp.where(shard < shards - 1, STEP, 256)
    edge = jnp.where(c < BLK, 0, BLK)
    ok = (r >= jnp.maximum(edge, low)) & (r < jnp.minimum(edge + 320, high))
    scores = dot(kbuf[0:STEP], q2, NT) - slope * jnp.abs(delta).astype(f32)
    scores = jnp.where(ok, scores, masked_value)
    put(0, STEP, scores)
    top = jnp.max(scores, axis=0, keepdims=True)
    far_bias = slope * (-float((BAND + 1) * BLK))
    for lo in range(STEP, kbuf.shape[0], STEP):
        scores = dot(kbuf[lo : lo + STEP], q2, NT)
        parts = []
        for i in range(STEP // BLK):
            there, _ = listed(fb_ref, t, shard, shards, zh, (lo - STEP) // BLK + i)
            row = jnp.where(there, far_bias, masked_value)
            parts.append(scores[i * BLK : (i + 1) * BLK] + row)
        scores = jnp.concatenate(parts, axis=0)
        put(lo, lo + STEP, scores)
        top = jnp.maximum(top, jnp.max(scores, axis=0, keepdims=True))
    return top


def context_grad_kernel(ref0, ref2, ref4, ref6, odd_ref, weight_ref, own_ref, mirrored_ref, buf):
    _, count, rows, lanes = buf.shape
    pieces = [x for k, ref in enumerate((ref0, ref2, ref4, ref6)) for x in (ref, odd_ref.at[k])]
    out = jnp.zeros((2 * count * rows, lanes), f32)
    for k in range(pieces[0].shape[1] // rows):
        here = [piece[which, k * rows : (k + 1) * rows] for which in range(2) for piece in pieces]
        out = out + dot(jnp.concatenate(here, axis=0), weight_ref[:, k * lanes : (k + 1) * lanes], NT)
    out = out.astype(bf16)
    for which in range(2):
        for j in range(count):
            at = (which * count + j) * rows
            buf[which, j] = out[at : at + rows]
    at = lax.axis_index("tp")
    for which, ref in ((0, own_ref), (1, mirrored_ref)):
        for k in range(count):
            ref[k * rows : (k + 1) * rows] = buf[which, lax.bitwise_xor(at, k)]


def attend_kernel(
    fb_ref, slopes_ref, q_ref, kv_ref, prev_ref, next_ref, far_ref, grad_ref, mirrored_ref,
    ctx_ref, rev_ref, gq_ref, own_out, prev_out, next_out, far_out,
    kbuf, vbuf, pbuf, dbuf, far_buf0, far_buf1, sems,
):
    shard, shards, zh, y = place()
    n = 2 * HD
    eye = one_hot(n, lambda r: r)
    total = kbuf.shape[0]
    copies = []
    for t in range(2):
        far_buf = (far_buf0, far_buf1)[t]
        stage(fb_ref, t, kv_ref, prev_ref, next_ref, far_ref, kbuf, vbuf)
        q2 = two_heads(q_ref[t] * HD ** (-0.5))
        g2 = two_heads(flipped(mirrored_ref[...]) if t == 1 else grad_ref[...])
        cols = q2.shape[0]

        def put(lo, hi, scores):
            pbuf[lo:hi] = scores

        top = biased(fb_ref, t, slopes_ref, q2, kbuf, put)
        norm = jnp.zeros((1, cols), f32)
        row_dot = jnp.zeros((1, cols), f32)
        for lo in range(0, total, STEP):
            w = jnp.exp(pbuf[lo : lo + STEP] - top)
            gp = dot(vbuf[lo : lo + STEP], g2, NT)
            pbuf[lo : lo + STEP] = w
            dbuf[lo : lo + STEP] = gp
            norm = norm + jnp.sum(w, axis=0, keepdims=True)
            row_dot = row_dot + jnp.sum(w * gp, axis=0, keepdims=True)
        inv = 1.0 / norm
        row_dot = row_dot * inv
        gq_acc = jnp.zeros((n, cols), f32)
        ctx_acc = jnp.zeros((n, cols), f32)
        for lo in range(0, total, STEP):
            p = pbuf[lo : lo + STEP] * inv
            low = p.astype(bf16)
            ds = (p * (dbuf[lo : lo + STEP] - row_dot)).astype(bf16)
            vt = dot(eye, vbuf[lo : lo + STEP], NT).astype(bf16)
            ctx_acc = ctx_acc + dot(vt, low, NN)
            kt = dot(eye, kbuf[lo : lo + STEP], NT).astype(bf16)
            gq_acc = gq_acc + dot(kt, ds, NN)
            for which, x in ((0, dot(ds, q2, NN)), (1, dot(low, g2, NN))):
                if lo == 0:
                    prev_out[t, which] = x[0:128].astype(bf16)
                    own_out[t, which] = x[128:256]
                    next_out[t, which] = x[256:384].astype(bf16)
                else:
                    x = x.astype(bf16)
                    for i in range(STEP // BLK):
                        there, slot = listed(fb_ref, t, shard, shards, zh, (lo - STEP) // BLK + i)

                        @pl.when(there)
                        def _():
                            far_buf[slot, which * BLK : (which + 1) * BLK] = x[i * BLK : (i + 1) * BLK]

        copies.append(pltpu.make_async_copy(far_buf, far_out.at[:, 2 * t * BLK : 2 * (t + 1) * BLK], sems.at[t]))
        copies[-1].start()
        gq_ref[t] = (pick_heads(gq_acc) * HD ** (-0.5)).astype(bf16)
        ctx = pick_heads(ctx_acc).astype(bf16)
        if t == 1:
            rev_ref[...] = flipped(ctx)
        else:
            ctx_ref[...] = ctx
    for copy in copies:
        copy.wait()


def combine(fb_ref, far_ref, asked_buf, rel, put):
    shard, shards, zh, y = place()
    asked_rows(fb_ref, asked_buf, rel)
    rows = 32
    for t in range(2):
        for which in range(2):
            for lo in range(0, BLK, rows):
                first = jnp.zeros((rows, 2 * HD), f32)
                second = jnp.zeros((rows, 2 * HD), f32)
                at = part(t, which).start + lo
                for p, reader in enumerate(plane_readers(zh)):
                    block = asked_by(asked_buf, t, reader, rows)
                    x = far_ref[2 * p + rel, at : at + rows].astype(f32)
                    first = first + jnp.where(block == 1, x, 0.0)
                    second = second + jnp.where(block == 2, x, 0.0)
                put(t, which, slice(lo, lo + rows), first)
                put(t, which, slice(BLK + lo, BLK + lo + rows), second)


def combine_partner_kernel(fb_ref, prev_ref, next_ref, far_ref, rows_ref, out_ref, asked_buf):
    shard, shards, zh, y = place()
    last = lax.axis_size("y") - 1

    def put(t, which, rows, far):
        far = far + jnp.where(y == 0, prev_ref[t, which, rows].astype(f32), 0.0)
        far = far + jnp.where(y == last, next_ref[t, which, rows].astype(f32), 0.0)
        out_ref[2 * t + which, rows] = far.astype(bf16)

    combine(fb_ref, far_ref, asked_buf, 1, put)
    rows, lanes = rows_ref.shape[0], out_ref.shape[2]
    for k in range(rows_ref.shape[1] // lanes):
        out_ref[4, k * rows : (k + 1) * rows] = rows_ref[:, k * lanes : (k + 1) * lanes]


def combine_own_kernel(fb_ref, own_ref, prev_ref, next_ref, far_ref, out_ref, asked_buf):
    shard, shards, zh, y = place()
    last = lax.axis_size("y") - 1

    def put(t, which, rows, far):
        total = own_ref[t, which, rows] + jnp.where(y == 0, 0.0, prev_ref[t, which, rows].astype(f32))
        total = total + jnp.where(y == last, 0.0, next_ref[t, which, rows].astype(f32))
        out_ref[t, which, rows] = total + far

    combine(fb_ref, far_ref, asked_buf, 0, put)


def finish_kernel(mine_ref, other_ref, residual_ref, rows_ref, gk_ref, gv_ref, mixed_ref):
    for t in range(2):
        for which, ref in ((0, gk_ref), (1, gv_ref)):
            ref[t] = (mine_ref[t, which] + other_ref[2 * t + which].astype(f32)).astype(bf16)
    rows, lanes = residual_ref.shape[0], other_ref.shape[2]
    for k in range(residual_ref.shape[1] // lanes):
        cols = slice(k * lanes, (k + 1) * lanes)
        total = residual_ref[:, cols].astype(f32) + rows_ref[:, cols]
        total = total + other_ref[4, k * rows : (k + 1) * rows].astype(f32)
        mixed_ref[:, cols] = total.astype(bf16)


def project_kernel(ctx_ref, rev_ref, weight_ref, even_ref, odd_ref, buf):
    _, count, rows, _ = buf.shape
    for which, ref in ((0, ctx_ref), (1, rev_ref)):
        for k in range(count):
            buf[which, k] = ref[k * rows : (k + 1) * rows]
    at = lax.axis_index("tp")
    blocks = [buf[which, lax.bitwise_xor(at, j)] for which in range(2) for j in range(count)]
    out = dot(jnp.concatenate(blocks, axis=0), weight_ref[...], NN)
    for which in range(2):
        for j in range(count):
            ref = (even_ref, odd_ref)[j % 2]
            row = (which * count + j) * rows
            ref[j // 2, which] = out[row : row + rows].astype(ref.dtype)


def smem():
    return pl.BlockSpec(memory_space=pltpu.SMEM)


def vmem():
    return pl.BlockSpec(memory_space=pltpu.VMEM)


def hbm():
    return pl.BlockSpec(memory_space=pltpu.HBM)


def shape(dims, dtype=bf16):
    return jax.ShapeDtypeStruct(dims, dtype)


def cost(flops, nbytes, exps=0):
    return pl.CostEstimate(flops=flops, bytes_accessed=nbytes, transcendentals=exps)


def swap(x, bit):
    count = lax.axis_size("tp")
    return lax.ppermute(x, "tp", [(i, i ^ bit) for i in range(count)])


def per_device(
    residual, queries, keys, values, slopes, out_weight, cotangent, far_blocks, far_count
):
    nx, nz, ny = (lax.axis_size(a) for a in SEQ)
    seq_count = nx * nz * ny
    tp_count = lax.axis_size("tp")
    tok_rows, width = queries.shape[1:]
    total_keys = 3 * tok_rows + far_blocks.shape[1] * BLK
    model = out_weight.shape[1]
    cols = 2 * tok_rows
    both = (2, 2, tok_rows, width)
    pieces = (tp_count, tok_rows // tp_count, width)
    slots = (nx * ny, 4 * BLK, width)

    def plane_a2a(x):
        halves = x.reshape(slots[0], 2 * slots[1], width)
        return lax.all_to_all(halves, ("x", "y"), split_axis=0, concat_axis=0, tiled=True).reshape(x.shape)

    def z_swap(x):
        return lax.ppermute(x, "zh", [(i, nz - 1 - i) for i in range(nz)])

    asked = pltpu.VMEM((2, seq_count, 2 * HD), jnp.int32)
    tile = (tok_rows, width)
    loaded = pl.pallas_call(
        load_kernel,
        out_shape=shape((5,) + tile),
        in_specs=[hbm()] * 3,
        out_specs=vmem(),
        scratch_shapes=[pltpu.SemaphoreType.DMA((4 + model // width,))],
        cost_estimate=cost(1_000, 320_000),
        compiler_params=pltpu.CompilerParams(vmem_limit_bytes=LIMIT),
        name="load",
    )(*(pltpu.with_memory_space_constraint(x, pltpu.HBM) for x in (keys, values, cotangent)))
    partner = z_swap(loaded)
    outgoing, to_up, to_down = pl.pallas_call(
        pack_kernel,
        out_shape=(pltpu.HBM((2 * slots[0],) + slots[1:], bf16), shape((4,) + tile), shape((4,) + tile)),
        in_specs=[vmem()] * 3,
        out_specs=(hbm(), vmem(), vmem()),
        scratch_shapes=[
            asked, pltpu.VMEM((2 * slots[0],) + slots[1:], bf16), pltpu.SemaphoreType.DMA((slots[0] // 4,)),
        ],
        cost_estimate=cost(1_000_000, 2_500_000),
        compiler_params=pltpu.CompilerParams(vmem_limit_bytes=LIMIT),
        name="pack",
    )(far_blocks, loaded, partner)
    far = plane_a2a(outgoing)

    turn = [
        ((x * nz + zh) * ny + y, ((nx - 1 - x) * nz + zh) * ny + ny - 1 - y)
        for x in range(nx)
        for zh in range(nz)
        for y in range(ny)
    ]
    both_cot = jnp.stack([loaded[4], lax.ppermute(partner[4], SEQ, turn)])
    same_core = [both_cot] + [swap(both_cot, bit) for bit in (2, 4, 6)]
    other_core = swap(jnp.stack(same_core), 1)

    def flat(x, zh, y):
        return (x * nz + zh) * ny + y

    places = [(x, zh, y) for x in range(nx) for zh in range(nz) for y in range(ny)]
    up, down = [], []
    for x, zh, y in places:
        if y < ny - 1:
            up.append((flat(x, zh, y), flat(x, zh, y + 1)))
        elif zh == nz - 1:
            up.append((flat(x, zh, y), flat(x, zh, 0)))
        elif x < nx - 1:
            up.append((flat(x, zh, y), flat(x + 1, zh, 0)))
        if y > 0:
            down.append((flat(x, zh, y), flat(x, zh, y - 1)))
        elif zh == 0:
            down.append((flat(x, zh, y), flat(x, zh, ny - 1)))
        elif x > 0:
            down.append((flat(x, zh, y), flat(x - 1, zh, ny - 1)))
    from_prev = lax.ppermute(to_up, SEQ, up)
    from_next = lax.ppermute(to_down, SEQ, down)

    grad_context, mirrored = pl.pallas_call(
        context_grad_kernel,
        out_shape=(shape(tile), shape(tile)),
        in_specs=[vmem()] * 6,
        out_specs=(vmem(), vmem()),
        scratch_shapes=[pltpu.VMEM((2,) + pieces, bf16)],
        cost_estimate=cost(68_000_000, 900_000),
        compiler_params=pltpu.CompilerParams(vmem_limit_bytes=LIMIT),
        name="context_grad",
    )(*same_core, other_core, out_weight)

    square = shape((tok_rows, width))
    half = pltpu.VMEM((seq_count, 2 * BLK, width), bf16)
    context_fwd, context_rev, grad_queries, own, before, after, far_grads = pl.pallas_call(
        attend_kernel,
        out_shape=(square, square, shape((2, tok_rows, width)), shape(both, f32), shape(both), shape(both))
        + (pltpu.HBM(outgoing.shape, bf16),),
        in_specs=[smem()] * 2 + [vmem()] * 7,
        out_specs=(vmem(),) * 6 + (hbm(),),
        scratch_shapes=[pltpu.VMEM((total_keys, width), bf16)] * 2
        + [pltpu.VMEM((total_keys, cols), f32)] * 2
        + [half, half, pltpu.SemaphoreType.DMA((2,))],
        cost_estimate=cost(4_000_000_000, 8_000_000, 1_000_000),
        compiler_params=pltpu.CompilerParams(vmem_limit_bytes=LIMIT),
        name="attend",
    )(far_blocks, slopes, queries, loaded, from_prev, from_next, far, grad_context, mirrored)
    returned = plane_a2a(far_grads)
    from_prev_grad = lax.ppermute(after, SEQ, [(b, a) for a, b in down])
    from_next_grad = lax.ppermute(before, SEQ, [(b, a) for a, b in up])
    rows = (tp_count // 2, 2, tok_rows // tp_count, model)
    even, odd = pl.pallas_call(
        project_kernel,
        out_shape=(shape(rows, f32), shape(rows)),
        in_specs=[vmem()] * 3,
        out_specs=(vmem(),) * 2,
        scratch_shapes=[pltpu.VMEM((2,) + pieces, bf16)],
        cost_estimate=cost(68_000_000, 1_500_000),
        compiler_params=pltpu.CompilerParams(vmem_limit_bytes=LIMIT),
        name="project",
    )(context_fwd, context_rev, out_weight)
    held = even + swap(odd, 1).astype(f32)
    parts = [swap(held[k].astype(bf16), 2 * k) for k in range(1, tp_count // 2)]
    summed = held[0] + sum(here.astype(f32) for here in parts)
    turned = lax.ppermute(summed[1].astype(bf16), SEQ, turn)

    other = pl.pallas_call(
        combine_partner_kernel,
        out_shape=shape((5,) + tile),
        in_specs=[vmem()] * 5,
        out_specs=vmem(),
        scratch_shapes=[asked],
        cost_estimate=cost(2_000_000, 1_500_000),
        compiler_params=pltpu.CompilerParams(vmem_limit_bytes=LIMIT),
        name="combine_partner",
    )(far_blocks, from_prev_grad, from_next_grad, returned, turned)
    mine = pl.pallas_call(
        combine_own_kernel,
        out_shape=shape(both, f32),
        in_specs=[vmem()] * 5,
        out_specs=vmem(),
        scratch_shapes=[asked],
        cost_estimate=cost(2_000_000, 1_500_000),
        compiler_params=pltpu.CompilerParams(vmem_limit_bytes=LIMIT),
        name="combine_own",
    )(far_blocks, own, from_prev_grad, from_next_grad, returned)
    grad_keys, grad_values, mixed = pl.pallas_call(
        finish_kernel,
        out_shape=(shape((2,) + tile),) * 2 + (shape(residual.shape),),
        in_specs=[vmem()] * 4,
        out_specs=(vmem(),) * 3,
        cost_estimate=cost(200_000, 900_000),
        compiler_params=pltpu.CompilerParams(vmem_limit_bytes=LIMIT),
        name="finish",
    )(mine, z_swap(other), residual, summed[0])
    return (mixed, grad_queries, grad_keys, grad_values)


def solution(mesh):
    split = jax.sharding.Mesh(mesh.devices.reshape(4, 2, 4, -1), SEQ + ("tp",))
    rows = P(SEQ + ("tp",), None)
    strands = P(None, SEQ, "tp")
    return jax.shard_map(
        per_device,
        mesh=split,
        in_specs=(rows, strands, strands, strands, P("tp"), P("tp", None), rows, P(), P()),
        out_specs=(rows, strands, strands, strands),
        check_vma=False,
    )
```

```python
import jax
import jax.numpy as jnp
from jax import lax
from jax.experimental import pallas as pl
from jax.experimental.pallas import tpu as pltpu
from jax.sharding import PartitionSpec as P

HD = 64
BLK = 64
BAND = 2
STEP = 384
FAR_STEP = 256
LIMIT = 24 << 20

masked_value = -1e30
f32 = jnp.float32
bf16 = jnp.bfloat16

NT = (((1,), (1,)), ((), ()))
NN = (((1,), (0,)), ((), ()))
TN = (((0,), (0,)), ((), ()))


def dot(a, b, dims):
    return lax.dot_general(a, b, dims, preferred_element_type=f32)


def two_heads(x):
    first = lax.broadcasted_iota(jnp.int32, x.shape, 1) < HD
    zero = jnp.zeros_like(x)
    return jnp.concatenate([jnp.where(first, x, zero), jnp.where(first, zero, x)], axis=0)


def pick_heads(xt):
    rows = xt.shape[1] // 2
    own = jnp.concatenate([xt[:HD, :rows], xt[HD:, rows:]], axis=0)
    return own.T


def one_hot(n, at):
    r = lax.broadcasted_iota(jnp.int32, (n, n), 0)
    c = lax.broadcasted_iota(jnp.int32, (n, n), 1)
    return (c == at(r)).astype(bf16)


def flipped(x):
    n = x.shape[0]
    return dot(one_hot(n, lambda r: n - 1 - r), x, NN).astype(bf16)


SEQ = ("x", "zh", "y")


def place():
    x, zh, y = (lax.axis_index(a) for a in SEQ)
    nx, nz, ny = (lax.axis_size(a) for a in SEQ)
    return (x * nz + zh) * ny + y, nx * nz * ny, zh, y


def slot_of(owner, zh):
    nx, nz, ny = (lax.axis_size(a) for a in SEQ)
    xz, y = lax.div(owner, ny), lax.rem(owner, ny)
    x, z = lax.div(xz, nz), lax.rem(xz, nz)
    return jnp.where(z == zh, 0, nx * ny) + x * ny + y


def plane_readers(zh):
    nx, nz, ny = (lax.axis_size(a) for a in SEQ)
    return [(x * nz + zh) * ny + y for x in range(nx) for y in range(ny)]


def part(t, which):
    return slice((2 * t + which) * BLK, (2 * t + which + 1) * BLK)


def listed(fb_ref, t, shard, shards, zh, f):
    entry = fb_ref[shard if t == 0 else shards - 1 - shard, f]
    owner = lax.shift_right_arithmetic(entry, 1)
    owner = owner if t == 0 else shards - 1 - owner
    return entry >= 0, jnp.where(entry >= 0, slot_of(owner, zh), 0)


def asked_of(fb, t, shard, shards):
    mine = shard if t == 0 else shards - 1 - shard
    inner = fb & 1
    inner = inner + 1 if t == 0 else 2 - inner
    hit = jnp.where(lax.shift_right_arithmetic(fb, 1) == mine, inner, 0)
    return jnp.sum(hit, axis=1, keepdims=True)


def asked_rows(fb_ref, asked_buf, rel):
    shard, shards, zh, y = place()
    target = shard + rel * (1 - 2 * zh) * lax.axis_size("y")
    fb = fb_ref[...]
    for t in range(2):
        asked_buf[t] = jnp.broadcast_to(asked_of(fb, t, target, shards), asked_buf.shape[1:])


def asked_by(asked_buf, t, reader, rows):
    row = reader if t == 0 else asked_buf.shape[1] - 1 - reader
    return jnp.broadcast_to(asked_buf[t, pl.ds(row, 1)], (rows, 2 * HD))


def pack(fb_ref, kv_ref, out_ref, asked_buf, out_buf, sems, rel):
    shard, shards, zh, y = place()
    asked_rows(fb_ref, asked_buf, rel)
    copies = []
    for p, reader in enumerate(plane_readers(zh)):
        for t in range(2):
            second = asked_by(asked_buf, t, reader, BLK) == 2
            for which in range(2):
                out_buf[p, part(t, which)] = jnp.where(second, kv_ref[t, which, BLK:], kv_ref[t, which, :BLK])
        if p % 4 == 3:
            done = pl.ds(p - 3, 4)
            copies.append(pltpu.make_async_copy(out_buf.at[done], out_ref.at[done], sems.at[p // 4]))
            copies[-1].start()
    return copies


def pack_own_kernel(fb_ref, key_ref, value_ref, out_ref, kv_ref, asked_buf, out_buf, sems, in_sems):
    loads = [
        pltpu.make_async_copy(ref.at[t], kv_ref.at[t, which], in_sems.at[t, which])
        for t in range(2)
        for which, ref in ((0, key_ref), (1, value_ref))
    ]
    for copy in loads:
        copy.start()
    for copy in loads:
        copy.wait()
    for copy in pack(fb_ref, kv_ref, out_ref, asked_buf, out_buf, sems, 0):
        copy.wait()


def pack_partner_kernel(fb_ref, own_ref, partner_ref, out_ref, up_ref, down_ref, asked_buf, out_buf, sems):
    shard, shards, zh, y = place()
    copies = pack(fb_ref, partner_ref, out_ref, asked_buf, out_buf, sems, 1)
    up_ref[...] = jnp.where(y == lax.axis_size("y") - 1, partner_ref[...], own_ref[...])
    down_ref[...] = jnp.where(y == 0, partner_ref[...], own_ref[...])
    for copy in copies:
        copy.wait()


def stage(fb_ref, t, kv_ref, prev_ref, next_ref, far_refs, kbuf, vbuf):
    shard, shards, zh, y = place()
    plane = far_refs[0].shape[0]
    for which, buf in ((0, kbuf), (1, vbuf)):
        buf[0:128] = prev_ref[t, which]
        buf[128:256] = kv_ref[t, which]
        buf[256:384] = next_ref[t, which]
    for f in range(fb_ref.shape[1]):
        _, slot = listed(fb_ref, t, shard, shards, zh, f)
        rows = slice(STEP + f * BLK, STEP + (f + 1) * BLK)
        here = slot < plane
        at = jnp.where(here, slot, slot - plane)
        for which, buf in ((0, kbuf), (1, vbuf)):
            buf[rows] = jnp.where(here, *(ref[at, part(t, which)] for ref in far_refs))


def biased(fb_ref, t, slopes_ref, q2, kbuf, put):
    shard, shards, zh, y = place()
    cols = q2.shape[0]
    half = cols // 2
    head_col = lax.broadcasted_iota(jnp.int32, (1, cols), 1)
    slope = jnp.where(head_col < half, slopes_ref[0], slopes_ref[1])
    r = lax.broadcasted_iota(jnp.int32, (STEP, cols), 0)
    c = lax.broadcasted_iota(jnp.int32, (STEP, cols), 1)
    c = jnp.where(c < half, c, c - half)
    delta = r - 128 - c
    low = jnp.where(shard > 0, 0, 128)
    high = jnp.where(shard < shards - 1, STEP, 256)
    edge = jnp.where(c < BLK, 0, BLK)
    ok = (r >= jnp.maximum(edge, low)) & (r < jnp.minimum(edge + 320, high))
    scores = dot(kbuf[0:STEP], q2, NT) - slope * jnp.abs(delta).astype(f32)
    scores = jnp.where(ok, scores, masked_value)
    put(0, STEP, scores)
    top = jnp.max(scores, axis=0, keepdims=True)
    far_bias = slope * (-float((BAND + 1) * BLK))
    for lo in range(STEP, kbuf.shape[0], FAR_STEP):
        scores = dot(kbuf[lo : lo + FAR_STEP], q2, NT)
        parts = []
        for i in range(FAR_STEP // BLK):
            there, _ = listed(fb_ref, t, shard, shards, zh, (lo - STEP) // BLK + i)
            row = jnp.where(there, far_bias, masked_value)
            parts.append(scores[i * BLK : (i + 1) * BLK] + row)
        scores = jnp.concatenate(parts, axis=0)
        put(lo, lo + FAR_STEP, scores)
        top = jnp.maximum(top, jnp.max(scores, axis=0, keepdims=True))
    return top


def context_grad_kernel(ref0, ref2, ref4, ref6, odd_ref, weight_ref, out_ref, buf):
    count, rows, _ = buf.shape
    got = [x for k, ref in enumerate((ref0, ref2, ref4, ref6)) for x in (ref[...], odd_ref[k])]
    got = jnp.concatenate(got, axis=0)
    out = dot(got, weight_ref[...], NT).astype(bf16)
    for k in range(count):
        buf[k] = out[k * rows : (k + 1) * rows]
    at = lax.axis_index("tp")
    for k in range(count):
        out_ref[k * rows : (k + 1) * rows] = buf[lax.bitwise_xor(at, k)]


def attend_kernel(
    fb_ref, slopes_hbm, q_ref, kv_ref, prev_ref, next_ref, far_own, far_partner, grad_ref, mirrored_ref,
    ctx_ref, rev_ref, gq_ref, own_out, prev_out, next_out, partner_out, here_out,
    kbuf, vbuf, pbuf, dbuf, far_buf0, far_buf1, sems, slopes_ref, slopes_sem,
):
    shard, shards, zh, y = place()
    n = 2 * HD
    eye = one_hot(n, lambda r: r)
    total = kbuf.shape[0]
    slopes_copy = pltpu.make_async_copy(slopes_hbm, slopes_ref, slopes_sem)
    slopes_copy.start()
    copies = []
    for t in range(2):
        far_buf = (far_buf0, far_buf1)[t]
        spare = far_buf.shape[0] - 1
        to = [listed(fb_ref, t, shard, shards, zh, f) for f in range(fb_ref.shape[1])]
        to = [jnp.where(there, slot, spare) for there, slot in to]
        stage(fb_ref, t, kv_ref, prev_ref, next_ref, (far_own, far_partner), kbuf, vbuf)
        q2 = two_heads(q_ref[t] * HD ** (-0.5))
        if t == 0:
            slopes_copy.wait()
        g2 = two_heads(flipped(mirrored_ref[...]) if t == 1 else grad_ref[...])
        cols = q2.shape[0]

        def put(lo, hi, scores):
            pbuf[lo:hi] = scores

        top = biased(fb_ref, t, slopes_ref, q2, kbuf, put)
        norm = jnp.zeros((1, cols), f32)
        row_dot = jnp.zeros((1, cols), f32)
        for lo in range(0, total, FAR_STEP):
            w = jnp.exp(pbuf[lo : lo + FAR_STEP] - top)
            gp = dot(vbuf[lo : lo + FAR_STEP], g2, NT)
            pbuf[lo : lo + FAR_STEP] = w
            dbuf[lo : lo + FAR_STEP] = gp
            norm = norm + jnp.sum(w, axis=0, keepdims=True)
            row_dot = row_dot + jnp.sum(w * gp, axis=0, keepdims=True)
        inv = 1.0 / norm
        row_dot = row_dot * inv
        gq_acc = jnp.zeros((n, cols), f32)
        ctx_acc = jnp.zeros((n, cols), f32)
        for lo in range(0, total, STEP):
            p = pbuf[lo : lo + STEP] * inv
            low = p.astype(bf16)
            ds = (p * (dbuf[lo : lo + STEP] - row_dot)).astype(bf16)
            ctx_acc = ctx_acc + dot(vbuf[lo : lo + STEP], low, TN)
            gq_acc = gq_acc + dot(kbuf[lo : lo + STEP], ds, TN)
            for which, x in ((0, dot(ds, q2, NN)), (1, dot(low, g2, NN))):
                if lo == 0:
                    prev_out[t, which] = x[0:128].astype(bf16)
                    own_out[t, which] = x[128:256]
                    next_out[t, which] = x[256:384].astype(bf16)
                else:
                    x = x.astype(bf16)
                    for i in range(STEP // BLK):
                        far_buf[to[(lo - STEP) // BLK + i], which * BLK : (which + 1) * BLK] = x[i * BLK : (i + 1) * BLK]

        plane = far_own.shape[0]
        for k, (out, rows) in enumerate(((here_out, pl.ds(0, plane)), (partner_out, pl.ds(plane, plane)))):
            to = out.at[:, 2 * t * BLK : 2 * (t + 1) * BLK]
            copies.append(pltpu.make_async_copy(far_buf.at[rows], to, sems.at[t, k]))
            copies[-1].start()
        gq_ref[t] = (pick_heads(gq_acc) * HD ** (-0.5)).astype(bf16)
        ctx = pick_heads(ctx_acc).astype(bf16)
        if t == 1:
            rev_ref[...] = flipped(ctx)
        else:
            ctx_ref[...] = ctx
    for copy in copies:
        copy.wait()


def combine(fb_ref, far_ref, asked_buf, rel, put):
    shard, shards, zh, y = place()
    asked_rows(fb_ref, asked_buf, rel)
    rows = 32
    for t in range(2):
        for which in range(2):
            for lo in range(0, BLK, rows):
                first = jnp.zeros((rows, 2 * HD), f32)
                second = jnp.zeros((rows, 2 * HD), f32)
                at = part(t, which).start + lo
                for p, reader in enumerate(plane_readers(zh)):
                    block = asked_by(asked_buf, t, reader, rows)
                    x = far_ref[p, at : at + rows].astype(f32)
                    first = first + jnp.where(block == 1, x, 0.0)
                    second = second + jnp.where(block == 2, x, 0.0)
                put(t, which, slice(lo, lo + rows), first)
                put(t, which, slice(BLK + lo, BLK + lo + rows), second)


def combine_partner_kernel(fb_ref, prev_ref, next_ref, far_ref, out_ref, asked_buf):
    shard, shards, zh, y = place()
    last = lax.axis_size("y") - 1

    def put(t, which, rows, far):
        far = far + jnp.where(y == 0, prev_ref[t, which, rows].astype(f32), 0.0)
        far = far + jnp.where(y == last, next_ref[t, which, rows].astype(f32), 0.0)
        out_ref[t, which, rows] = far.astype(bf16)

    combine(fb_ref, far_ref, asked_buf, 1, put)


def combine_own_kernel(fb_ref, own_ref, prev_ref, next_ref, other_ref, far_ref, gk_ref, gv_ref, asked_buf):
    shard, shards, zh, y = place()
    last = lax.axis_size("y") - 1

    def put(t, which, rows, far):
        total = own_ref[t, which, rows] + jnp.where(y == 0, 0.0, prev_ref[t, which, rows].astype(f32))
        total = total + jnp.where(y == last, 0.0, next_ref[t, which, rows].astype(f32))
        total = total + other_ref[t, which, rows].astype(f32) + far
        (gk_ref, gv_ref)[which][t, rows] = total.astype(bf16)

    combine(fb_ref, far_ref, asked_buf, 0, put)


def project_kernel(ctx_ref, back_ref, weight_ref, even_ref, odd_ref, sum_buf):
    total = (ctx_ref[...].astype(f32) + back_ref[...].astype(f32)).astype(bf16)
    count, rows, _ = sum_buf.shape
    for k in range(count):
        sum_buf[k] = total[k * rows : (k + 1) * rows]
    at = lax.axis_index("tp")
    blocks = jnp.concatenate([sum_buf[lax.bitwise_xor(at, j)] for j in range(count)], axis=0)
    out = dot(blocks, weight_ref[...], NN)
    for j in range(count):
        ref = (even_ref, odd_ref)[j % 2]
        ref[j // 2] = out[j * rows : (j + 1) * rows].astype(ref.dtype)


def smem():
    return pl.BlockSpec(memory_space=pltpu.SMEM)


def vmem():
    return pl.BlockSpec(memory_space=pltpu.VMEM)


def hbm():
    return pl.BlockSpec(memory_space=pltpu.HBM)


def shape(dims, dtype=bf16):
    return jax.ShapeDtypeStruct(dims, dtype)


def cost(flops, nbytes, exps=0):
    return pl.CostEstimate(flops=flops, bytes_accessed=nbytes, transcendentals=exps)


def swap(x, bit):
    count = lax.axis_size("tp")
    return lax.ppermute(x, "tp", [(i, i ^ bit) for i in range(count)])


def per_device(
    residual, queries, keys, values, slopes, out_weight, cotangent, far_blocks, far_count
):
    nx, nz, ny = (lax.axis_size(a) for a in SEQ)
    seq_count = nx * nz * ny
    tp_count = lax.axis_size("tp")
    tok_rows, width = queries.shape[1:]
    total_keys = 3 * tok_rows + far_blocks.shape[1] * BLK
    model = out_weight.shape[1]
    cols = 2 * tok_rows
    both = (2, 2, tok_rows, width)
    pieces = (tp_count, tok_rows // tp_count, width)
    slots = (nx * ny, 4 * BLK, width)

    def plane_a2a(x):
        return lax.all_to_all(x, ("x", "y"), split_axis=0, concat_axis=0, tiled=True)

    def z_swap(x):
        return lax.ppermute(x, "zh", [(i, nz - 1 - i) for i in range(nz)])

    asked = pltpu.VMEM((2, seq_count, 2 * HD), jnp.int32)
    packed = [asked, pltpu.VMEM(slots, bf16), pltpu.SemaphoreType.DMA((nx * ny // 4,))]
    outgoing, key_value = pl.pallas_call(
        pack_own_kernel,
        out_shape=(pltpu.HBM(slots, bf16), shape(both)),
        in_specs=[vmem(), hbm(), hbm()],
        out_specs=(hbm(), vmem()),
        scratch_shapes=packed + [pltpu.SemaphoreType.DMA((2, 2))],
        cost_estimate=cost(500_000, 1_500_000),
        compiler_params=pltpu.CompilerParams(vmem_limit_bytes=LIMIT),
        name="pack_own",
    )(far_blocks, *(pltpu.with_memory_space_constraint(x, pltpu.HBM) for x in (keys, values)))
    far_own = plane_a2a(outgoing)
    partner = z_swap(key_value)
    outgoing, to_up, to_down = pl.pallas_call(
        pack_partner_kernel,
        out_shape=(pltpu.HBM(slots, bf16), shape(both), shape(both)),
        in_specs=[vmem()] * 3,
        out_specs=(hbm(), vmem(), vmem()),
        scratch_shapes=packed,
        cost_estimate=cost(500_000, 1_500_000),
        compiler_params=pltpu.CompilerParams(vmem_limit_bytes=LIMIT),
        name="pack_partner",
    )(far_blocks, key_value, partner)
    same_core = [cotangent] + [swap(cotangent, bit) for bit in (2, 4, 6)]
    other_core = swap(jnp.stack(same_core), 1)
    outgoing, other_core = lax.optimization_barrier((outgoing, other_core))
    far_partner = plane_a2a(outgoing)

    def flat(x, zh, y):
        return (x * nz + zh) * ny + y

    places = [(x, zh, y) for x in range(nx) for zh in range(nz) for y in range(ny)]
    up, down = [], []
    for x, zh, y in places:
        if y < ny - 1:
            up.append((flat(x, zh, y), flat(x, zh, y + 1)))
        elif zh == nz - 1:
            up.append((flat(x, zh, y), flat(x, zh, 0)))
        elif x < nx - 1:
            up.append((flat(x, zh, y), flat(x + 1, zh, 0)))
        if y > 0:
            down.append((flat(x, zh, y), flat(x, zh, y - 1)))
        elif zh == 0:
            down.append((flat(x, zh, y), flat(x, zh, ny - 1)))
        elif x > 0:
            down.append((flat(x, zh, y), flat(x - 1, zh, ny - 1)))
    mirror = [(i, seq_count - 1 - i) for i in range(seq_count)]
    from_prev = lax.ppermute(to_up, SEQ, up)
    from_next = lax.ppermute(to_down, SEQ, down)

    grad_context = pl.pallas_call(
        context_grad_kernel,
        out_shape=shape((tok_rows, width)),
        in_specs=[vmem()] * 6,
        out_specs=vmem(),
        scratch_shapes=[pltpu.VMEM(pieces, bf16)],
        cost_estimate=cost(34_000_000, 600_000),
        compiler_params=pltpu.CompilerParams(vmem_limit_bytes=LIMIT),
        name="context_grad",
    )(*same_core, other_core, out_weight)
    mirrored = lax.ppermute(grad_context, SEQ, mirror)

    square = shape((tok_rows, width))
    half = pltpu.VMEM((seq_count + 1, 2 * BLK, width), bf16)
    context_fwd, context_rev, grad_queries, own, before, after, partner_grads, here_grads = pl.pallas_call(
        attend_kernel,
        out_shape=(square, square, shape((2, tok_rows, width)), shape(both, f32), shape(both), shape(both))
        + (pltpu.HBM(slots, bf16),) * 2,
        in_specs=[smem(), hbm()] + [vmem()] * 8,
        out_specs=(vmem(),) * 6 + (hbm(),) * 2,
        scratch_shapes=[pltpu.VMEM((total_keys, width), bf16)] * 2
        + [pltpu.VMEM((total_keys, cols), f32)] * 2
        + [half, half, pltpu.SemaphoreType.DMA((2, 2)), pltpu.SMEM(slopes.shape, f32), pltpu.SemaphoreType.DMA(())],
        cost_estimate=cost(4_000_000_000, 8_000_000, 1_000_000),
        compiler_params=pltpu.CompilerParams(vmem_limit_bytes=LIMIT),
        name="attend",
    )(
        far_blocks, pltpu.with_memory_space_constraint(slopes, pltpu.HBM), queries, key_value, from_prev, from_next, far_own, far_partner, grad_context, mirrored)
    context_back = lax.ppermute(context_rev, SEQ, mirror)

    returned_partner = plane_a2a(partner_grads)
    from_prev_grad = lax.ppermute(after, SEQ, [(b, a) for a, b in down])
    from_next_grad = lax.ppermute(before, SEQ, [(b, a) for a, b in up])
    here_grads, returned_partner, context_back, from_prev_grad, from_next_grad = lax.optimization_barrier(
        (here_grads, returned_partner, context_back, from_prev_grad, from_next_grad)
    )
    returned_own = plane_a2a(here_grads)
    other = pl.pallas_call(
        combine_partner_kernel,
        out_shape=shape(both),
        in_specs=[vmem()] * 4,
        out_specs=vmem(),
        scratch_shapes=[asked],
        cost_estimate=cost(2_000_000, 1_500_000),
        compiler_params=pltpu.CompilerParams(vmem_limit_bytes=LIMIT),
        name="combine_partner",
    )(far_blocks, from_prev_grad, from_next_grad, returned_partner)
    other, context_back = lax.optimization_barrier((other, context_back))
    other = z_swap(other)

    even, odd = pl.pallas_call(
        project_kernel,
        out_shape=(
            shape((tp_count // 2, tok_rows // tp_count, model), f32),
            shape((tp_count // 2, tok_rows // tp_count, model)),
        ),
        in_specs=[vmem()] * 3,
        out_specs=(vmem(),) * 2,
        scratch_shapes=[pltpu.VMEM(pieces, bf16)],
        cost_estimate=cost(34_000_000, 1_000_000),
        compiler_params=pltpu.CompilerParams(vmem_limit_bytes=LIMIT),
        name="project",
    )(context_fwd, context_back, out_weight)
    held = even + swap(odd, 1).astype(f32)
    held, other = lax.optimization_barrier((held, other))
    parts = [swap(held[k].astype(bf16), 2 * k) for k in range(1, tp_count // 2)]
    grad_keys, grad_values = pl.pallas_call(
        combine_own_kernel,
        out_shape=(shape((2, tok_rows, width)),) * 2,
        in_specs=[vmem()] * 6,
        out_specs=(vmem(),) * 2,
        scratch_shapes=[asked],
        cost_estimate=cost(2_000_000, 1_500_000),
        compiler_params=pltpu.CompilerParams(vmem_limit_bytes=LIMIT),
        name="combine_own",
    )(far_blocks, own, from_prev_grad, from_next_grad, other, returned_own)
    grad_keys, grad_values, *parts = lax.optimization_barrier((grad_keys, grad_values, *parts))
    total = residual.astype(f32) + held[0]
    for part_here in parts:
        total = total + part_here.astype(f32)
    mixed = total.astype(bf16)
    return (mixed, grad_queries, grad_keys, grad_values)


def solution(mesh):
    split = jax.sharding.Mesh(mesh.devices.reshape(4, 2, 4, -1), SEQ + ("tp",))
    rows = P(SEQ + ("tp",), None)
    strands = P(None, SEQ, "tp")
    return jax.shard_map(
        per_device,
        mesh=split,
        in_specs=(rows, strands, strands, strands, P("tp"), P("tp", None), rows, P(), P()),
        out_specs=(rows, strands, strands, strands),
        check_vma=False,
    )
```

```python
import jax
import jax.numpy as jnp
from jax import lax
from jax.experimental import pallas as pl
from jax.experimental.pallas import tpu as pltpu
from jax.sharding import PartitionSpec as P

HD = 64
BLK = 64
BAND = 2
STEP = 384
FAR_STEP = 256
LIMIT = 24 << 20

masked_value = -1e30
f32 = jnp.float32
bf16 = jnp.bfloat16

NT = (((1,), (1,)), ((), ()))
NN = (((1,), (0,)), ((), ()))
TN = (((0,), (0,)), ((), ()))


def dot(a, b, dims):
    return lax.dot_general(a, b, dims, preferred_element_type=f32)


def two_heads(x):
    first = lax.broadcasted_iota(jnp.int32, x.shape, 1) < HD
    zero = jnp.zeros_like(x)
    return jnp.concatenate([jnp.where(first, x, zero), jnp.where(first, zero, x)], axis=0)


def pick_heads(xt):
    rows = xt.shape[1] // 2
    own = jnp.concatenate([xt[:HD, :rows], xt[HD:, rows:]], axis=0)
    return own.T


def one_hot(n, at):
    r = lax.broadcasted_iota(jnp.int32, (n, n), 0)
    c = lax.broadcasted_iota(jnp.int32, (n, n), 1)
    return (c == at(r)).astype(bf16)


def flipped(x):
    n = x.shape[0]
    return dot(one_hot(n, lambda r: n - 1 - r), x, NN).astype(bf16)


SEQ = ("x", "zh", "y")


def place():
    x, zh, y = (lax.axis_index(a) for a in SEQ)
    nx, nz, ny = (lax.axis_size(a) for a in SEQ)
    return (x * nz + zh) * ny + y, nx * nz * ny, zh, y


def slot_of(owner, zh):
    nx, nz, ny = (lax.axis_size(a) for a in SEQ)
    xz, y = lax.div(owner, ny), lax.rem(owner, ny)
    x, z = lax.div(xz, nz), lax.rem(xz, nz)
    return jnp.where(z == zh, 0, nx * ny) + x * ny + y


def plane_readers(zh):
    nx, nz, ny = (lax.axis_size(a) for a in SEQ)
    return [(x * nz + zh) * ny + y for x in range(nx) for y in range(ny)]


def part(t, which):
    return slice((2 * t + which) * BLK, (2 * t + which + 1) * BLK)


def listed(fb_ref, t, shard, shards, zh, f):
    entry = fb_ref[shard if t == 0 else shards - 1 - shard, f]
    owner = lax.shift_right_arithmetic(entry, 1)
    owner = owner if t == 0 else shards - 1 - owner
    return entry >= 0, jnp.where(entry >= 0, slot_of(owner, zh), 0)


def asked_of(fb, t, shard, shards):
    mine = shard if t == 0 else shards - 1 - shard
    inner = fb & 1
    inner = inner + 1 if t == 0 else 2 - inner
    hit = jnp.where(lax.shift_right_arithmetic(fb, 1) == mine, inner, 0)
    return jnp.sum(hit, axis=1, keepdims=True)


def asked_rows(fb_ref, asked_buf, rel):
    shard, shards, zh, y = place()
    target = shard + rel * (1 - 2 * zh) * lax.axis_size("y")
    fb = fb_ref[...]
    for t in range(2):
        asked_buf[t] = jnp.broadcast_to(asked_of(fb, t, target, shards), asked_buf.shape[1:])


def asked_by(asked_buf, t, reader, rows):
    row = reader if t == 0 else asked_buf.shape[1] - 1 - reader
    return jnp.broadcast_to(asked_buf[t, pl.ds(row, 1)], (rows, 2 * HD))


def pack(fb_ref, kv_ref, out_ref, asked_buf, out_buf, sems, rel):
    shard, shards, zh, y = place()
    asked_rows(fb_ref, asked_buf, rel)
    copies = []
    for p, reader in enumerate(plane_readers(zh)):
        for t in range(2):
            second = asked_by(asked_buf, t, reader, BLK) == 2
            for which in range(2):
                out_buf[p, part(t, which)] = jnp.where(second, kv_ref[t, which, BLK:], kv_ref[t, which, :BLK])
        if p % 4 == 3:
            done = pl.ds(p - 3, 4)
            copies.append(pltpu.make_async_copy(out_buf.at[done], out_ref.at[done], sems.at[p // 4]))
            copies[-1].start()
    return copies


def pack_own_kernel(fb_ref, key_ref, value_ref, out_ref, kv_ref, asked_buf, out_buf, sems, in_sems):
    loads = [
        pltpu.make_async_copy(ref.at[t], kv_ref.at[t, which], in_sems.at[t, which])
        for t in range(2)
        for which, ref in ((0, key_ref), (1, value_ref))
    ]
    for copy in loads:
        copy.start()
    for copy in loads:
        copy.wait()
    for copy in pack(fb_ref, kv_ref, out_ref, asked_buf, out_buf, sems, 0):
        copy.wait()


def pack_partner_kernel(fb_ref, own_ref, partner_ref, out_ref, up_ref, down_ref, asked_buf, out_buf, sems):
    shard, shards, zh, y = place()
    copies = pack(fb_ref, partner_ref, out_ref, asked_buf, out_buf, sems, 1)
    up_ref[...] = jnp.where(y == lax.axis_size("y") - 1, partner_ref[...], own_ref[...])
    down_ref[...] = jnp.where(y == 0, partner_ref[...], own_ref[...])
    for copy in copies:
        copy.wait()


def stage(fb_ref, t, kv_ref, prev_ref, next_ref, far_refs, kbuf, vbuf):
    shard, shards, zh, y = place()
    plane = far_refs[0].shape[0]
    for which, buf in ((0, kbuf), (1, vbuf)):
        buf[0:128] = prev_ref[t, which]
        buf[128:256] = kv_ref[t, which]
        buf[256:384] = next_ref[t, which]
    for f in range(fb_ref.shape[1]):
        _, slot = listed(fb_ref, t, shard, shards, zh, f)
        rows = slice(STEP + f * BLK, STEP + (f + 1) * BLK)
        here = slot < plane
        at = jnp.where(here, slot, slot - plane)
        for which, buf in ((0, kbuf), (1, vbuf)):
            buf[rows] = jnp.where(here, *(ref[at, part(t, which)] for ref in far_refs))


def biased(fb_ref, t, slopes_ref, q2, kbuf, put):
    shard, shards, zh, y = place()
    cols = q2.shape[0]
    half = cols // 2
    head_col = lax.broadcasted_iota(jnp.int32, (1, cols), 1)
    slope = jnp.where(head_col < half, slopes_ref[0], slopes_ref[1])
    r = lax.broadcasted_iota(jnp.int32, (STEP, cols), 0)
    c = lax.broadcasted_iota(jnp.int32, (STEP, cols), 1)
    c = jnp.where(c < half, c, c - half)
    delta = r - 128 - c
    low = jnp.where(shard > 0, 0, 128)
    high = jnp.where(shard < shards - 1, STEP, 256)
    edge = jnp.where(c < BLK, 0, BLK)
    ok = (r >= jnp.maximum(edge, low)) & (r < jnp.minimum(edge + 320, high))
    scores = dot(kbuf[0:STEP], q2, NT) - slope * jnp.abs(delta).astype(f32)
    scores = jnp.where(ok, scores, masked_value)
    put(0, STEP, scores)
    top = jnp.max(scores, axis=0, keepdims=True)
    far_bias = slope * (-float((BAND + 1) * BLK))
    for lo in range(STEP, kbuf.shape[0], FAR_STEP):
        scores = dot(kbuf[lo : lo + FAR_STEP], q2, NT)
        parts = []
        for i in range(FAR_STEP // BLK):
            there, _ = listed(fb_ref, t, shard, shards, zh, (lo - STEP) // BLK + i)
            row = jnp.where(there, far_bias, masked_value)
            parts.append(scores[i * BLK : (i + 1) * BLK] + row)
        scores = jnp.concatenate(parts, axis=0)
        put(lo, lo + FAR_STEP, scores)
        top = jnp.maximum(top, jnp.max(scores, axis=0, keepdims=True))
    return top


def context_grad_kernel(ref0, ref2, ref4, ref6, odd_ref, weight_ref, out_ref, buf):
    count, rows, _ = buf.shape
    got = [x for k, ref in enumerate((ref0, ref2, ref4, ref6)) for x in (ref[...], odd_ref[k])]
    got = jnp.concatenate(got, axis=0)
    out = dot(got, weight_ref[...], NT).astype(bf16)
    for k in range(count):
        buf[k] = out[k * rows : (k + 1) * rows]
    at = lax.axis_index("tp")
    for k in range(count):
        out_ref[k * rows : (k + 1) * rows] = buf[lax.bitwise_xor(at, k)]


def attend_kernel(
    fb_ref, slopes_hbm, q_ref, kv_ref, prev_ref, next_ref, far_own, far_partner, grad_ref, mirrored_ref,
    ctx_ref, rev_ref, gq_ref, own_out, prev_out, next_out, partner_out, here_out,
    kbuf, vbuf, pbuf, dbuf, far_buf0, far_buf1, sems, slopes_ref, slopes_sem,
):
    shard, shards, zh, y = place()
    n = 2 * HD
    eye = one_hot(n, lambda r: r)
    total = kbuf.shape[0]
    slopes_copy = pltpu.make_async_copy(slopes_hbm, slopes_ref, slopes_sem)
    slopes_copy.start()
    copies = []
    for t in range(2):
        far_buf = (far_buf0, far_buf1)[t]
        spare = far_buf.shape[0] - 1
        to = [listed(fb_ref, t, shard, shards, zh, f) for f in range(fb_ref.shape[1])]
        to = [jnp.where(there, slot, spare) for there, slot in to]
        stage(fb_ref, t, kv_ref, prev_ref, next_ref, (far_own, far_partner), kbuf, vbuf)
        q2 = two_heads(q_ref[t] * HD ** (-0.5))
        if t == 0:
            slopes_copy.wait()
        g2 = two_heads(flipped(mirrored_ref[...]) if t == 1 else grad_ref[...])
        cols = q2.shape[0]

        def put(lo, hi, scores):
            pbuf[lo:hi] = scores

        top = biased(fb_ref, t, slopes_ref, q2, kbuf, put)
        norm = jnp.zeros((1, cols), f32)
        row_dot = jnp.zeros((1, cols), f32)
        for lo in range(0, total, FAR_STEP):
            w = jnp.exp(pbuf[lo : lo + FAR_STEP] - top)
            gp = dot(vbuf[lo : lo + FAR_STEP], g2, NT)
            pbuf[lo : lo + FAR_STEP] = w
            dbuf[lo : lo + FAR_STEP] = gp
            norm = norm + jnp.sum(w, axis=0, keepdims=True)
            row_dot = row_dot + jnp.sum(w * gp, axis=0, keepdims=True)
        inv = 1.0 / norm
        row_dot = row_dot * inv
        gq_acc = jnp.zeros((n, cols), f32)
        ctx_acc = jnp.zeros((n, cols), f32)
        for lo in range(0, total, STEP):
            p = pbuf[lo : lo + STEP] * inv
            low = p.astype(bf16)
            ds = (p * (dbuf[lo : lo + STEP] - row_dot)).astype(bf16)
            ctx_acc = ctx_acc + dot(vbuf[lo : lo + STEP], low, TN)
            gq_acc = gq_acc + dot(kbuf[lo : lo + STEP], ds, TN)
            for which, x in ((0, dot(ds, q2, NN)), (1, dot(low, g2, NN))):
                if lo == 0:
                    prev_out[t, which] = x[0:128].astype(bf16)
                    own_out[t, which] = x[128:256]
                    next_out[t, which] = x[256:384].astype(bf16)
                else:
                    x = x.astype(bf16)
                    for i in range(STEP // BLK):
                        far_buf[to[(lo - STEP) // BLK + i], which * BLK : (which + 1) * BLK] = x[i * BLK : (i + 1) * BLK]

        plane = far_own.shape[0]
        for k, (out, rows) in enumerate(((here_out, pl.ds(0, plane)), (partner_out, pl.ds(plane, plane)))):
            to = out.at[:, 2 * t * BLK : 2 * (t + 1) * BLK]
            copies.append(pltpu.make_async_copy(far_buf.at[rows], to, sems.at[t, k]))
            copies[-1].start()
        gq_ref[t] = (pick_heads(gq_acc) * HD ** (-0.5)).astype(bf16)
        ctx = pick_heads(ctx_acc).astype(bf16)
        if t == 1:
            rev_ref[...] = flipped(ctx)
        else:
            ctx_ref[...] = ctx
    for copy in copies:
        copy.wait()


def combine(fb_ref, far_ref, asked_buf, rel, put):
    shard, shards, zh, y = place()
    asked_rows(fb_ref, asked_buf, rel)
    rows = 32
    for t in range(2):
        for which in range(2):
            for lo in range(0, BLK, rows):
                first = jnp.zeros((rows, 2 * HD), f32)
                second = jnp.zeros((rows, 2 * HD), f32)
                at = part(t, which).start + lo
                for p, reader in enumerate(plane_readers(zh)):
                    block = asked_by(asked_buf, t, reader, rows)
                    x = far_ref[p, at : at + rows].astype(f32)
                    first = first + jnp.where(block == 1, x, 0.0)
                    second = second + jnp.where(block == 2, x, 0.0)
                put(t, which, slice(lo, lo + rows), first)
                put(t, which, slice(BLK + lo, BLK + lo + rows), second)


def combine_partner_kernel(fb_ref, prev_ref, next_ref, far_ref, out_ref, asked_buf):
    shard, shards, zh, y = place()
    last = lax.axis_size("y") - 1

    def put(t, which, rows, far):
        far = far + jnp.where(y == 0, prev_ref[t, which, rows].astype(f32), 0.0)
        far = far + jnp.where(y == last, next_ref[t, which, rows].astype(f32), 0.0)
        out_ref[t, which, rows] = far.astype(bf16)

    combine(fb_ref, far_ref, asked_buf, 1, put)


def combine_own_kernel(fb_ref, own_ref, prev_ref, next_ref, other_ref, far_ref, gk_ref, gv_ref, asked_buf):
    shard, shards, zh, y = place()
    last = lax.axis_size("y") - 1

    def put(t, which, rows, far):
        total = own_ref[t, which, rows] + jnp.where(y == 0, 0.0, prev_ref[t, which, rows].astype(f32))
        total = total + jnp.where(y == last, 0.0, next_ref[t, which, rows].astype(f32))
        total = total + other_ref[t, which, rows].astype(f32) + far
        (gk_ref, gv_ref)[which][t, rows] = total.astype(bf16)

    combine(fb_ref, far_ref, asked_buf, 0, put)


def project_kernel(ctx_ref, back_ref, weight_ref, even_ref, odd_ref, sum_buf):
    total = (ctx_ref[...].astype(f32) + back_ref[...].astype(f32)).astype(bf16)
    count, rows, _ = sum_buf.shape
    for k in range(count):
        sum_buf[k] = total[k * rows : (k + 1) * rows]
    at = lax.axis_index("tp")
    blocks = jnp.concatenate([sum_buf[lax.bitwise_xor(at, j)] for j in range(count)], axis=0)
    out = dot(blocks, weight_ref[...], NN)
    for j in range(count):
        ref = (even_ref, odd_ref)[j % 2]
        ref[j // 2] = out[j * rows : (j + 1) * rows].astype(ref.dtype)


def smem():
    return pl.BlockSpec(memory_space=pltpu.SMEM)


def vmem():
    return pl.BlockSpec(memory_space=pltpu.VMEM)


def hbm():
    return pl.BlockSpec(memory_space=pltpu.HBM)


def shape(dims, dtype=bf16):
    return jax.ShapeDtypeStruct(dims, dtype)


def cost(flops, nbytes, exps=0):
    return pl.CostEstimate(flops=flops, bytes_accessed=nbytes, transcendentals=exps)


def swap(x, bit):
    count = lax.axis_size("tp")
    return lax.ppermute(x, "tp", [(i, i ^ bit) for i in range(count)])


def per_device(
    residual, queries, keys, values, slopes, out_weight, cotangent, far_blocks, far_count
):
    nx, nz, ny = (lax.axis_size(a) for a in SEQ)
    seq_count = nx * nz * ny
    tp_count = lax.axis_size("tp")
    tok_rows, width = queries.shape[1:]
    total_keys = 3 * tok_rows + far_blocks.shape[1] * BLK
    model = out_weight.shape[1]
    cols = 2 * tok_rows
    both = (2, 2, tok_rows, width)
    pieces = (tp_count, tok_rows // tp_count, width)
    slots = (nx * ny, 4 * BLK, width)

    def plane_a2a(x):
        return lax.all_to_all(x, ("x", "y"), split_axis=0, concat_axis=0, tiled=True)

    def z_swap(x):
        return lax.ppermute(x, "zh", [(i, nz - 1 - i) for i in range(nz)])

    asked = pltpu.VMEM((2, seq_count, 2 * HD), jnp.int32)
    packed = [asked, pltpu.VMEM(slots, bf16), pltpu.SemaphoreType.DMA((nx * ny // 4,))]
    outgoing, key_value = pl.pallas_call(
        pack_own_kernel,
        out_shape=(pltpu.HBM(slots, bf16), shape(both)),
        in_specs=[vmem(), hbm(), hbm()],
        out_specs=(hbm(), vmem()),
        scratch_shapes=packed + [pltpu.SemaphoreType.DMA((2, 2))],
        cost_estimate=cost(500_000, 1_500_000),
        compiler_params=pltpu.CompilerParams(vmem_limit_bytes=LIMIT),
        name="pack_own",
    )(far_blocks, *(pltpu.with_memory_space_constraint(x, pltpu.HBM) for x in (keys, values)))
    far_own = plane_a2a(outgoing)
    partner = z_swap(key_value)
    outgoing, to_up, to_down = pl.pallas_call(
        pack_partner_kernel,
        out_shape=(pltpu.HBM(slots, bf16), shape(both), shape(both)),
        in_specs=[vmem()] * 3,
        out_specs=(hbm(), vmem(), vmem()),
        scratch_shapes=packed,
        cost_estimate=cost(500_000, 1_500_000),
        compiler_params=pltpu.CompilerParams(vmem_limit_bytes=LIMIT),
        name="pack_partner",
    )(far_blocks, key_value, partner)
    same_core = [cotangent] + [swap(cotangent, bit) for bit in (2, 4, 6)]
    other_core = swap(jnp.stack(same_core), 1)
    outgoing, other_core = lax.optimization_barrier((outgoing, other_core))
    far_partner = plane_a2a(outgoing)

    def flat(x, zh, y):
        return (x * nz + zh) * ny + y

    places = [(x, zh, y) for x in range(nx) for zh in range(nz) for y in range(ny)]
    up, down = [], []
    for x, zh, y in places:
        if y < ny - 1:
            up.append((flat(x, zh, y), flat(x, zh, y + 1)))
        elif zh == nz - 1:
            up.append((flat(x, zh, y), flat(x, zh, 0)))
        elif x < nx - 1:
            up.append((flat(x, zh, y), flat(x + 1, zh, 0)))
        if y > 0:
            down.append((flat(x, zh, y), flat(x, zh, y - 1)))
        elif zh == 0:
            down.append((flat(x, zh, y), flat(x, zh, ny - 1)))
        elif x > 0:
            down.append((flat(x, zh, y), flat(x - 1, zh, ny - 1)))
    mirror = [(i, seq_count - 1 - i) for i in range(seq_count)]
    from_prev = lax.ppermute(to_up, SEQ, up)
    from_next = lax.ppermute(to_down, SEQ, down)

    grad_context = pl.pallas_call(
        context_grad_kernel,
        out_shape=shape((tok_rows, width)),
        in_specs=[vmem()] * 6,
        out_specs=vmem(),
        scratch_shapes=[pltpu.VMEM(pieces, bf16)],
        cost_estimate=cost(34_000_000, 600_000),
        compiler_params=pltpu.CompilerParams(vmem_limit_bytes=LIMIT),
        name="context_grad",
    )(*same_core, other_core, out_weight)
    mirrored = lax.ppermute(grad_context, SEQ, mirror)

    square = shape((tok_rows, width))
    half = pltpu.VMEM((seq_count + 1, 2 * BLK, width), bf16)
    context_fwd, context_rev, grad_queries, own, before, after, partner_grads, here_grads = pl.pallas_call(
        attend_kernel,
        out_shape=(square, square, shape((2, tok_rows, width)), shape(both, f32), shape(both), shape(both))
        + (pltpu.HBM(slots, bf16),) * 2,
        in_specs=[smem(), hbm()] + [vmem()] * 8,
        out_specs=(vmem(),) * 6 + (hbm(),) * 2,
        scratch_shapes=[pltpu.VMEM((total_keys, width), bf16)] * 2
        + [pltpu.VMEM((total_keys, cols), f32)] * 2
        + [half, half, pltpu.SemaphoreType.DMA((2, 2)), pltpu.SMEM(slopes.shape, f32), pltpu.SemaphoreType.DMA(())],
        cost_estimate=cost(4_000_000_000, 8_000_000, 1_000_000),
        compiler_params=pltpu.CompilerParams(vmem_limit_bytes=LIMIT),
        name="attend",
    )(
        far_blocks, pltpu.with_memory_space_constraint(slopes, pltpu.HBM), queries, key_value, from_prev, from_next, far_own, far_partner, grad_context, mirrored)
    context_back = lax.ppermute(context_rev, SEQ, mirror)

    returned_partner = plane_a2a(partner_grads)
    from_prev_grad = lax.ppermute(after, SEQ, [(b, a) for a, b in down])
    from_next_grad = lax.ppermute(before, SEQ, [(b, a) for a, b in up])
    here_grads, returned_partner, context_back = lax.optimization_barrier(
        (here_grads, returned_partner, context_back)
    )
    returned_own = plane_a2a(here_grads)
    other = pl.pallas_call(
        combine_partner_kernel,
        out_shape=shape(both),
        in_specs=[vmem()] * 4,
        out_specs=vmem(),
        scratch_shapes=[asked],
        cost_estimate=cost(2_000_000, 1_500_000),
        compiler_params=pltpu.CompilerParams(vmem_limit_bytes=LIMIT),
        name="combine_partner",
    )(far_blocks, from_prev_grad, from_next_grad, returned_partner)
    other, context_back = lax.optimization_barrier((other, context_back))
    other = z_swap(other)

    even, odd = pl.pallas_call(
        project_kernel,
        out_shape=(
            shape((tp_count // 2, tok_rows // tp_count, model), f32),
            shape((tp_count // 2, tok_rows // tp_count, model)),
        ),
        in_specs=[vmem()] * 3,
        out_specs=(vmem(),) * 2,
        scratch_shapes=[pltpu.VMEM(pieces, bf16)],
        cost_estimate=cost(34_000_000, 1_000_000),
        compiler_params=pltpu.CompilerParams(vmem_limit_bytes=LIMIT),
        name="project",
    )(context_fwd, context_back, out_weight)
    held = even + swap(odd, 1).astype(f32)
    parts = [swap(held[k].astype(bf16), 2 * k) for k in range(1, tp_count // 2)]
    total = residual.astype(f32) + held[0]
    for part_here in parts:
        total = total + part_here.astype(f32)
    mixed = total.astype(bf16)

    grad_keys, grad_values = pl.pallas_call(
        combine_own_kernel,
        out_shape=(shape((2, tok_rows, width)),) * 2,
        in_specs=[vmem()] * 6,
        out_specs=(vmem(),) * 2,
        scratch_shapes=[asked],
        cost_estimate=cost(2_000_000, 1_500_000),
        compiler_params=pltpu.CompilerParams(vmem_limit_bytes=LIMIT),
        name="combine_own",
    )(far_blocks, own, from_prev_grad, from_next_grad, other, returned_own)
    return (mixed, grad_queries, grad_keys, grad_values)


def solution(mesh):
    split = jax.sharding.Mesh(mesh.devices.reshape(4, 2, 4, -1), SEQ + ("tp",))
    rows = P(SEQ + ("tp",), None)
    strands = P(None, SEQ, "tp")
    return jax.shard_map(
        per_device,
        mesh=split,
        in_specs=(rows, strands, strands, strands, P("tp"), P("tp", None), rows, P(), P()),
        out_specs=(rows, strands, strands, strands),
        check_vma=False,
    )
```

```python
import jax
import jax.numpy as jnp
from jax import lax
from jax.experimental import pallas as pl
from jax.experimental.pallas import tpu as pltpu
from jax.sharding import PartitionSpec as P

HD = 64
BLK = 64
BAND = 2
STEP = 384
FAR_STEP = 256
LIMIT = 24 << 20

masked_value = -1e30
f32 = jnp.float32
bf16 = jnp.bfloat16

NT = (((1,), (1,)), ((), ()))
NN = (((1,), (0,)), ((), ()))
TN = (((0,), (0,)), ((), ()))


def dot(a, b, dims):
    return lax.dot_general(a, b, dims, preferred_element_type=f32)


def two_heads(x):
    first = lax.broadcasted_iota(jnp.int32, x.shape, 1) < HD
    zero = jnp.zeros_like(x)
    return jnp.concatenate([jnp.where(first, x, zero), jnp.where(first, zero, x)], axis=0)


def pick_heads(xt):
    rows = xt.shape[1] // 2
    own = jnp.concatenate([xt[:HD, :rows], xt[HD:, rows:]], axis=0)
    return own.T


def one_hot(n, at):
    r = lax.broadcasted_iota(jnp.int32, (n, n), 0)
    c = lax.broadcasted_iota(jnp.int32, (n, n), 1)
    return (c == at(r)).astype(bf16)


def flipped(x):
    n = x.shape[0]
    return dot(one_hot(n, lambda r: n - 1 - r), x, NN).astype(bf16)


SEQ = ("x", "zh", "y")


def place():
    x, zh, y = (lax.axis_index(a) for a in SEQ)
    nx, nz, ny = (lax.axis_size(a) for a in SEQ)
    return (x * nz + zh) * ny + y, nx * nz * ny, zh, y


def slot_of(owner, zh):
    nx, nz, ny = (lax.axis_size(a) for a in SEQ)
    xz, y = lax.div(owner, ny), lax.rem(owner, ny)
    x, z = lax.div(xz, nz), lax.rem(xz, nz)
    return jnp.where(z == zh, 0, nx * ny) + x * ny + y


def plane_readers(zh):
    nx, nz, ny = (lax.axis_size(a) for a in SEQ)
    return [(x * nz + zh) * ny + y for x in range(nx) for y in range(ny)]


def part(t, which):
    return slice((2 * t + which) * BLK, (2 * t + which + 1) * BLK)


def listed(fb_ref, t, shard, shards, zh, f):
    entry = fb_ref[shard if t == 0 else shards - 1 - shard, f]
    owner = lax.shift_right_arithmetic(entry, 1)
    owner = owner if t == 0 else shards - 1 - owner
    return entry >= 0, jnp.where(entry >= 0, slot_of(owner, zh), 0)


def asked_of(fb, t, shard, shards):
    mine = shard if t == 0 else shards - 1 - shard
    inner = fb & 1
    inner = inner + 1 if t == 0 else 2 - inner
    hit = jnp.where(lax.shift_right_arithmetic(fb, 1) == mine, inner, 0)
    return jnp.sum(hit, axis=1, keepdims=True)


def asked_rows(fb_ref, asked_buf, rel):
    shard, shards, zh, y = place()
    target = shard + rel * (1 - 2 * zh) * lax.axis_size("y")
    fb = fb_ref[...]
    for t in range(2):
        asked_buf[t] = jnp.broadcast_to(asked_of(fb, t, target, shards), asked_buf.shape[1:])


def asked_by(asked_buf, t, reader, rows):
    row = reader if t == 0 else asked_buf.shape[1] - 1 - reader
    return jnp.broadcast_to(asked_buf[t, pl.ds(row, 1)], (rows, 2 * HD))


def pack(fb_ref, kv_ref, out_ref, asked_buf, out_buf, sems, rel):
    shard, shards, zh, y = place()
    asked_rows(fb_ref, asked_buf, rel)
    copies = []
    for p, reader in enumerate(plane_readers(zh)):
        for t in range(2):
            second = asked_by(asked_buf, t, reader, BLK) == 2
            for which in range(2):
                out_buf[p, part(t, which)] = jnp.where(second, kv_ref[t, which, BLK:], kv_ref[t, which, :BLK])
        if p % 4 == 3:
            done = pl.ds(p - 3, 4)
            copies.append(pltpu.make_async_copy(out_buf.at[done], out_ref.at[done], sems.at[p // 4]))
            copies[-1].start()
    return copies


def pack_own_kernel(fb_ref, key_ref, value_ref, out_ref, kv_ref, asked_buf, out_buf, sems, in_sems):
    loads = [
        pltpu.make_async_copy(ref.at[t], kv_ref.at[t, which], in_sems.at[t, which])
        for t in range(2)
        for which, ref in ((0, key_ref), (1, value_ref))
    ]
    for copy in loads:
        copy.start()
    for copy in loads:
        copy.wait()
    for copy in pack(fb_ref, kv_ref, out_ref, asked_buf, out_buf, sems, 0):
        copy.wait()


def pack_partner_kernel(fb_ref, own_ref, partner_ref, out_ref, up_ref, down_ref, asked_buf, out_buf, sems):
    shard, shards, zh, y = place()
    copies = pack(fb_ref, partner_ref, out_ref, asked_buf, out_buf, sems, 1)
    up_ref[...] = jnp.where(y == lax.axis_size("y") - 1, partner_ref[...], own_ref[...])
    down_ref[...] = jnp.where(y == 0, partner_ref[...], own_ref[...])
    for copy in copies:
        copy.wait()


def stage(fb_ref, t, kv_ref, prev_ref, next_ref, far_refs, kbuf, vbuf):
    shard, shards, zh, y = place()
    plane = far_refs[0].shape[0]
    for which, buf in ((0, kbuf), (1, vbuf)):
        buf[0:128] = prev_ref[t, which]
        buf[128:256] = kv_ref[t, which]
        buf[256:384] = next_ref[t, which]
    for f in range(fb_ref.shape[1]):
        _, slot = listed(fb_ref, t, shard, shards, zh, f)
        rows = slice(STEP + f * BLK, STEP + (f + 1) * BLK)
        here = slot < plane
        at = jnp.where(here, slot, slot - plane)
        for which, buf in ((0, kbuf), (1, vbuf)):
            buf[rows] = jnp.where(here, *(ref[at, part(t, which)] for ref in far_refs))


def biased(fb_ref, t, slopes_ref, q2, kbuf, put):
    shard, shards, zh, y = place()
    cols = q2.shape[0]
    half = cols // 2
    head_col = lax.broadcasted_iota(jnp.int32, (1, cols), 1)
    slope = jnp.where(head_col < half, slopes_ref[0], slopes_ref[1])
    r = lax.broadcasted_iota(jnp.int32, (STEP, cols), 0)
    c = lax.broadcasted_iota(jnp.int32, (STEP, cols), 1)
    c = jnp.where(c < half, c, c - half)
    delta = r - 128 - c
    low = jnp.where(shard > 0, 0, 128)
    high = jnp.where(shard < shards - 1, STEP, 256)
    edge = jnp.where(c < BLK, 0, BLK)
    ok = (r >= jnp.maximum(edge, low)) & (r < jnp.minimum(edge + 320, high))
    scores = dot(kbuf[0:STEP], q2, NT) - slope * jnp.abs(delta).astype(f32)
    scores = jnp.where(ok, scores, masked_value)
    put(0, STEP, scores)
    top = jnp.max(scores, axis=0, keepdims=True)
    far_bias = slope * (-float((BAND + 1) * BLK))
    for lo in range(STEP, kbuf.shape[0], FAR_STEP):
        scores = dot(kbuf[lo : lo + FAR_STEP], q2, NT)
        parts = []
        for i in range(FAR_STEP // BLK):
            there, _ = listed(fb_ref, t, shard, shards, zh, (lo - STEP) // BLK + i)
            row = jnp.where(there, far_bias, masked_value)
            parts.append(scores[i * BLK : (i + 1) * BLK] + row)
        scores = jnp.concatenate(parts, axis=0)
        put(lo, lo + FAR_STEP, scores)
        top = jnp.maximum(top, jnp.max(scores, axis=0, keepdims=True))
    return top


def context_grad_kernel(ref0, ref2, ref4, ref6, odd_ref, weight_ref, out_ref, buf):
    count, rows, _ = buf.shape
    got = [x for k, ref in enumerate((ref0, ref2, ref4, ref6)) for x in (ref[...], odd_ref[k])]
    got = jnp.concatenate(got, axis=0)
    out = dot(got, weight_ref[...], NT).astype(bf16)
    for k in range(count):
        buf[k] = out[k * rows : (k + 1) * rows]
    at = lax.axis_index("tp")
    for k in range(count):
        out_ref[k * rows : (k + 1) * rows] = buf[lax.bitwise_xor(at, k)]


def attend_kernel(
    fb_ref, slopes_hbm, q_ref, kv_ref, prev_ref, next_ref, far_own, far_partner, grad_ref, mirrored_ref,
    ctx_ref, rev_ref, gq_ref, own_out, prev_out, next_out, partner_out, here_out,
    kbuf, vbuf, pbuf, dbuf, far_buf0, far_buf1, sems, slopes_ref, slopes_sem,
):
    shard, shards, zh, y = place()
    n = 2 * HD
    eye = one_hot(n, lambda r: r)
    total = kbuf.shape[0]
    slopes_copy = pltpu.make_async_copy(slopes_hbm, slopes_ref, slopes_sem)
    slopes_copy.start()
    copies = []
    for t in range(2):
        far_buf = (far_buf0, far_buf1)[t]
        spare = far_buf.shape[0] - 1
        to = [listed(fb_ref, t, shard, shards, zh, f) for f in range(fb_ref.shape[1])]
        to = [jnp.where(there, slot, spare) for there, slot in to]
        stage(fb_ref, t, kv_ref, prev_ref, next_ref, (far_own, far_partner), kbuf, vbuf)
        q2 = two_heads(q_ref[t] * HD ** (-0.5))
        if t == 0:
            slopes_copy.wait()
        g2 = two_heads(flipped(mirrored_ref[...]) if t == 1 else grad_ref[...])
        cols = q2.shape[0]

        def put(lo, hi, scores):
            pbuf[lo:hi] = scores

        top = biased(fb_ref, t, slopes_ref, q2, kbuf, put)
        norm = jnp.zeros((1, cols), f32)
        row_dot = jnp.zeros((1, cols), f32)
        for lo in range(0, total, FAR_STEP):
            w = jnp.exp(pbuf[lo : lo + FAR_STEP] - top)
            gp = dot(vbuf[lo : lo + FAR_STEP], g2, NT)
            pbuf[lo : lo + FAR_STEP] = w
            dbuf[lo : lo + FAR_STEP] = gp
            norm = norm + jnp.sum(w, axis=0, keepdims=True)
            row_dot = row_dot + jnp.sum(w * gp, axis=0, keepdims=True)
        inv = 1.0 / norm
        row_dot = row_dot * inv
        gq_acc = jnp.zeros((n, cols), f32)
        ctx_acc = jnp.zeros((n, cols), f32)
        for lo in range(0, total, STEP):
            p = pbuf[lo : lo + STEP] * inv
            low = p.astype(bf16)
            ds = (p * (dbuf[lo : lo + STEP] - row_dot)).astype(bf16)
            ctx_acc = ctx_acc + dot(vbuf[lo : lo + STEP], low, TN)
            gq_acc = gq_acc + dot(kbuf[lo : lo + STEP], ds, TN)
            for which, x in ((0, dot(ds, q2, NN)), (1, dot(low, g2, NN))):
                if lo == 0:
                    prev_out[t, which] = x[0:128].astype(bf16)
                    own_out[t, which] = x[128:256]
                    next_out[t, which] = x[256:384].astype(bf16)
                else:
                    x = x.astype(bf16)
                    for i in range(STEP // BLK):
                        far_buf[to[(lo - STEP) // BLK + i], which * BLK : (which + 1) * BLK] = x[i * BLK : (i + 1) * BLK]

        plane = far_own.shape[0]
        for k, (out, rows) in enumerate(((here_out, pl.ds(0, plane)), (partner_out, pl.ds(plane, plane)))):
            to = out.at[:, 2 * t * BLK : 2 * (t + 1) * BLK]
            copies.append(pltpu.make_async_copy(far_buf.at[rows], to, sems.at[t, k]))
            copies[-1].start()
        gq_ref[t] = (pick_heads(gq_acc) * HD ** (-0.5)).astype(bf16)
        ctx = pick_heads(ctx_acc).astype(bf16)
        if t == 1:
            rev_ref[...] = flipped(ctx)
        else:
            ctx_ref[...] = ctx
    for copy in copies:
        copy.wait()


def combine(fb_ref, far_ref, asked_buf, rel, put):
    shard, shards, zh, y = place()
    asked_rows(fb_ref, asked_buf, rel)
    rows = 32
    for t in range(2):
        for which in range(2):
            for lo in range(0, BLK, rows):
                first = jnp.zeros((rows, 2 * HD), f32)
                second = jnp.zeros((rows, 2 * HD), f32)
                at = part(t, which).start + lo
                for p, reader in enumerate(plane_readers(zh)):
                    block = asked_by(asked_buf, t, reader, rows)
                    x = far_ref[p, at : at + rows].astype(f32)
                    first = first + jnp.where(block == 1, x, 0.0)
                    second = second + jnp.where(block == 2, x, 0.0)
                put(t, which, slice(lo, lo + rows), first)
                put(t, which, slice(BLK + lo, BLK + lo + rows), second)


def combine_partner_kernel(fb_ref, prev_ref, next_ref, far_ref, out_ref, asked_buf):
    shard, shards, zh, y = place()
    last = lax.axis_size("y") - 1

    def put(t, which, rows, far):
        far = far + jnp.where(y == 0, prev_ref[t, which, rows].astype(f32), 0.0)
        far = far + jnp.where(y == last, next_ref[t, which, rows].astype(f32), 0.0)
        out_ref[t, which, rows] = far.astype(bf16)

    combine(fb_ref, far_ref, asked_buf, 1, put)


def combine_own_kernel(fb_ref, own_ref, prev_ref, next_ref, other_ref, far_ref, gk_ref, gv_ref, asked_buf):
    shard, shards, zh, y = place()
    last = lax.axis_size("y") - 1

    def put(t, which, rows, far):
        total = own_ref[t, which, rows] + jnp.where(y == 0, 0.0, prev_ref[t, which, rows].astype(f32))
        total = total + jnp.where(y == last, 0.0, next_ref[t, which, rows].astype(f32))
        total = total + other_ref[t, which, rows].astype(f32) + far
        (gk_ref, gv_ref)[which][t, rows] = total.astype(bf16)

    combine(fb_ref, far_ref, asked_buf, 0, put)


def project_kernel(ctx_ref, back_ref, weight_ref, even_ref, odd_ref, sum_buf):
    total = (ctx_ref[...].astype(f32) + back_ref[...].astype(f32)).astype(bf16)
    count, rows, _ = sum_buf.shape
    for k in range(count):
        sum_buf[k] = total[k * rows : (k + 1) * rows]
    at = lax.axis_index("tp")
    blocks = jnp.concatenate([sum_buf[lax.bitwise_xor(at, j)] for j in range(count)], axis=0)
    out = dot(blocks, weight_ref[...], NN)
    for j in range(count):
        ref = (even_ref, odd_ref)[j % 2]
        ref[j // 2] = out[j * rows : (j + 1) * rows].astype(ref.dtype)


def smem():
    return pl.BlockSpec(memory_space=pltpu.SMEM)


def vmem():
    return pl.BlockSpec(memory_space=pltpu.VMEM)


def hbm():
    return pl.BlockSpec(memory_space=pltpu.HBM)


def shape(dims, dtype=bf16):
    return jax.ShapeDtypeStruct(dims, dtype)


def cost(flops, nbytes, exps=0):
    return pl.CostEstimate(flops=flops, bytes_accessed=nbytes, transcendentals=exps)


def swap(x, bit):
    count = lax.axis_size("tp")
    return lax.ppermute(x, "tp", [(i, i ^ bit) for i in range(count)])


def per_device(
    residual, queries, keys, values, slopes, out_weight, cotangent, far_blocks, far_count
):
    nx, nz, ny = (lax.axis_size(a) for a in SEQ)
    seq_count = nx * nz * ny
    tp_count = lax.axis_size("tp")
    tok_rows, width = queries.shape[1:]
    total_keys = 3 * tok_rows + far_blocks.shape[1] * BLK
    model = out_weight.shape[1]
    cols = 2 * tok_rows
    both = (2, 2, tok_rows, width)
    pieces = (tp_count, tok_rows // tp_count, width)
    slots = (nx * ny, 4 * BLK, width)

    def plane_a2a(x):
        return lax.all_to_all(x, ("x", "y"), split_axis=0, concat_axis=0, tiled=True)

    def z_swap(x):
        return lax.ppermute(x, "zh", [(i, nz - 1 - i) for i in range(nz)])

    asked = pltpu.VMEM((2, seq_count, 2 * HD), jnp.int32)
    packed = [asked, pltpu.VMEM(slots, bf16), pltpu.SemaphoreType.DMA((nx * ny // 4,))]
    outgoing, key_value = pl.pallas_call(
        pack_own_kernel,
        out_shape=(pltpu.HBM(slots, bf16), shape(both)),
        in_specs=[vmem(), hbm(), hbm()],
        out_specs=(hbm(), vmem()),
        scratch_shapes=packed + [pltpu.SemaphoreType.DMA((2, 2))],
        cost_estimate=cost(500_000, 1_500_000),
        compiler_params=pltpu.CompilerParams(vmem_limit_bytes=LIMIT),
        name="pack_own",
    )(far_blocks, *(pltpu.with_memory_space_constraint(x, pltpu.HBM) for x in (keys, values)))
    far_own = plane_a2a(outgoing)
    partner = z_swap(key_value)
    outgoing, to_up, to_down = pl.pallas_call(
        pack_partner_kernel,
        out_shape=(pltpu.HBM(slots, bf16), shape(both), shape(both)),
        in_specs=[vmem()] * 3,
        out_specs=(hbm(), vmem(), vmem()),
        scratch_shapes=packed,
        cost_estimate=cost(500_000, 1_500_000),
        compiler_params=pltpu.CompilerParams(vmem_limit_bytes=LIMIT),
        name="pack_partner",
    )(far_blocks, key_value, partner)
    same_core = [cotangent] + [swap(cotangent, bit) for bit in (2, 4, 6)]
    other_core = swap(jnp.stack(same_core), 1)
    outgoing, other_core = lax.optimization_barrier((outgoing, other_core))
    far_partner = plane_a2a(outgoing)

    def flat(x, zh, y):
        return (x * nz + zh) * ny + y

    places = [(x, zh, y) for x in range(nx) for zh in range(nz) for y in range(ny)]
    up, down = [], []
    for x, zh, y in places:
        if y < ny - 1:
            up.append((flat(x, zh, y), flat(x, zh, y + 1)))
        elif zh == nz - 1:
            up.append((flat(x, zh, y), flat(x, zh, 0)))
        elif x < nx - 1:
            up.append((flat(x, zh, y), flat(x + 1, zh, 0)))
        if y > 0:
            down.append((flat(x, zh, y), flat(x, zh, y - 1)))
        elif zh == 0:
            down.append((flat(x, zh, y), flat(x, zh, ny - 1)))
        elif x > 0:
            down.append((flat(x, zh, y), flat(x - 1, zh, ny - 1)))
    mirror = [(i, seq_count - 1 - i) for i in range(seq_count)]
    from_prev = lax.ppermute(to_up, SEQ, up)
    from_next = lax.ppermute(to_down, SEQ, down)

    grad_context = pl.pallas_call(
        context_grad_kernel,
        out_shape=shape((tok_rows, width)),
        in_specs=[vmem()] * 6,
        out_specs=vmem(),
        scratch_shapes=[pltpu.VMEM(pieces, bf16)],
        cost_estimate=cost(34_000_000, 600_000),
        compiler_params=pltpu.CompilerParams(vmem_limit_bytes=LIMIT),
        name="context_grad",
    )(*same_core, other_core, out_weight)
    mirrored = lax.ppermute(grad_context, SEQ, mirror)

    square = shape((tok_rows, width))
    half = pltpu.VMEM((seq_count + 1, 2 * BLK, width), bf16)
    context_fwd, context_rev, grad_queries, own, before, after, partner_grads, here_grads = pl.pallas_call(
        attend_kernel,
        out_shape=(square, square, shape((2, tok_rows, width)), shape(both, f32), shape(both), shape(both))
        + (pltpu.HBM(slots, bf16),) * 2,
        in_specs=[smem(), hbm()] + [vmem()] * 8,
        out_specs=(vmem(),) * 6 + (hbm(),) * 2,
        scratch_shapes=[pltpu.VMEM((total_keys, width), bf16)] * 2
        + [pltpu.VMEM((total_keys, cols), f32)] * 2
        + [half, half, pltpu.SemaphoreType.DMA((2, 2)), pltpu.SMEM(slopes.shape, f32), pltpu.SemaphoreType.DMA(())],
        cost_estimate=cost(4_000_000_000, 8_000_000, 1_000_000),
        compiler_params=pltpu.CompilerParams(vmem_limit_bytes=LIMIT),
        name="attend",
    )(
        far_blocks, pltpu.with_memory_space_constraint(slopes, pltpu.HBM), queries, key_value, from_prev, from_next, far_own, far_partner, grad_context, mirrored)
    context_back = lax.ppermute(context_rev, SEQ, mirror)

    returned_partner = plane_a2a(partner_grads)
    from_prev_grad = lax.ppermute(after, SEQ, [(b, a) for a, b in down])
    from_next_grad = lax.ppermute(before, SEQ, [(b, a) for a, b in up])
    even, odd = pl.pallas_call(
        project_kernel,
        out_shape=(
            shape((tp_count // 2, tok_rows // tp_count, model), f32),
            shape((tp_count // 2, tok_rows // tp_count, model)),
        ),
        in_specs=[vmem()] * 3,
        out_specs=(vmem(),) * 2,
        scratch_shapes=[pltpu.VMEM(pieces, bf16)],
        cost_estimate=cost(34_000_000, 1_000_000),
        compiler_params=pltpu.CompilerParams(vmem_limit_bytes=LIMIT),
        name="project",
    )(context_fwd, context_back, out_weight)
    here_grads, returned_partner, even, odd = lax.optimization_barrier((here_grads, returned_partner, even, odd))
    returned_own = plane_a2a(here_grads)
    other = pl.pallas_call(
        combine_partner_kernel,
        out_shape=shape(both),
        in_specs=[vmem()] * 4,
        out_specs=vmem(),
        scratch_shapes=[asked],
        cost_estimate=cost(2_000_000, 1_500_000),
        compiler_params=pltpu.CompilerParams(vmem_limit_bytes=LIMIT),
        name="combine_partner",
    )(far_blocks, from_prev_grad, from_next_grad, returned_partner)
    other, odd = lax.optimization_barrier((other, odd))
    other = z_swap(other)

    held = even + swap(odd, 1).astype(f32)
    parts = [swap(held[k].astype(bf16), 2 * k) for k in range(1, tp_count // 2)]
    total = residual.astype(f32) + held[0]
    for part_here in parts:
        total = total + part_here.astype(f32)
    mixed = total.astype(bf16)

    grad_keys, grad_values = pl.pallas_call(
        combine_own_kernel,
        out_shape=(shape((2, tok_rows, width)),) * 2,
        in_specs=[vmem()] * 6,
        out_specs=(vmem(),) * 2,
        scratch_shapes=[asked],
        cost_estimate=cost(2_000_000, 1_500_000),
        compiler_params=pltpu.CompilerParams(vmem_limit_bytes=LIMIT),
        name="combine_own",
    )(far_blocks, own, from_prev_grad, from_next_grad, other, returned_own)
    return (mixed, grad_queries, grad_keys, grad_values)


def solution(mesh):
    split = jax.sharding.Mesh(mesh.devices.reshape(4, 2, 4, -1), SEQ + ("tp",))
    rows = P(SEQ + ("tp",), None)
    strands = P(None, SEQ, "tp")
    return jax.shard_map(
        per_device,
        mesh=split,
        in_specs=(rows, strands, strands, strands, P("tp"), P("tp", None), rows, P(), P()),
        out_specs=(rows, strands, strands, strands),
        check_vma=False,
    )
```

```python
import jax
import jax.numpy as jnp
from jax import lax
from jax.experimental import pallas as pl
from jax.experimental.pallas import tpu as pltpu
from jax.sharding import PartitionSpec as P

HD = 64
BLK = 64
BAND = 2
STEP = 384
FAR_STEP = 256
LIMIT = 24 << 20

masked_value = -1e30
f32 = jnp.float32
bf16 = jnp.bfloat16

NT = (((1,), (1,)), ((), ()))
NN = (((1,), (0,)), ((), ()))
TN = (((0,), (0,)), ((), ()))


def dot(a, b, dims):
    return lax.dot_general(a, b, dims, preferred_element_type=f32)


def two_heads(x):
    first = lax.broadcasted_iota(jnp.int32, x.shape, 1) < HD
    zero = jnp.zeros_like(x)
    return jnp.concatenate([jnp.where(first, x, zero), jnp.where(first, zero, x)], axis=0)


def pick_heads(xt):
    rows = xt.shape[1] // 2
    own = jnp.concatenate([xt[:HD, :rows], xt[HD:, rows:]], axis=0)
    return own.T


def one_hot(n, at):
    r = lax.broadcasted_iota(jnp.int32, (n, n), 0)
    c = lax.broadcasted_iota(jnp.int32, (n, n), 1)
    return (c == at(r)).astype(bf16)


def flipped(x):
    n = x.shape[0]
    return dot(one_hot(n, lambda r: n - 1 - r), x, NN).astype(bf16)


SEQ = ("x", "zh", "y")


def place():
    x, zh, y = (lax.axis_index(a) for a in SEQ)
    nx, nz, ny = (lax.axis_size(a) for a in SEQ)
    return (x * nz + zh) * ny + y, nx * nz * ny, zh, y


def slot_of(owner, zh):
    nx, nz, ny = (lax.axis_size(a) for a in SEQ)
    xz, y = lax.div(owner, ny), lax.rem(owner, ny)
    x, z = lax.div(xz, nz), lax.rem(xz, nz)
    return jnp.where(z == zh, 0, nx * ny) + x * ny + y


def plane_readers(zh):
    nx, nz, ny = (lax.axis_size(a) for a in SEQ)
    return [(x * nz + zh) * ny + y for x in range(nx) for y in range(ny)]


def part(t, which):
    return slice((2 * t + which) * BLK, (2 * t + which + 1) * BLK)


def listed(fb_ref, t, shard, shards, zh, f):
    entry = fb_ref[shard if t == 0 else shards - 1 - shard, f]
    owner = lax.shift_right_arithmetic(entry, 1)
    owner = owner if t == 0 else shards - 1 - owner
    return entry >= 0, jnp.where(entry >= 0, slot_of(owner, zh), 0)


def asked_of(fb, t, shard, shards):
    mine = shard if t == 0 else shards - 1 - shard
    inner = fb & 1
    inner = inner + 1 if t == 0 else 2 - inner
    hit = jnp.where(lax.shift_right_arithmetic(fb, 1) == mine, inner, 0)
    return jnp.sum(hit, axis=1, keepdims=True)


def asked_rows(fb_ref, asked_buf, rel):
    shard, shards, zh, y = place()
    target = shard + rel * (1 - 2 * zh) * lax.axis_size("y")
    fb = fb_ref[...]
    for t in range(2):
        asked_buf[t] = jnp.broadcast_to(asked_of(fb, t, target, shards), asked_buf.shape[1:])


def asked_by(asked_buf, t, reader, rows):
    row = reader if t == 0 else asked_buf.shape[1] - 1 - reader
    return jnp.broadcast_to(asked_buf[t, pl.ds(row, 1)], (rows, 2 * HD))


def pack(fb_ref, kv_ref, out_ref, asked_buf, out_buf, sems, rel):
    shard, shards, zh, y = place()
    asked_rows(fb_ref, asked_buf, rel)
    copies = []
    for p, reader in enumerate(plane_readers(zh)):
        for t in range(2):
            second = asked_by(asked_buf, t, reader, BLK) == 2
            for which in range(2):
                out_buf[p, part(t, which)] = jnp.where(second, kv_ref[t, which, BLK:], kv_ref[t, which, :BLK])
        if p % 4 == 3:
            done = pl.ds(p - 3, 4)
            copies.append(pltpu.make_async_copy(out_buf.at[done], out_ref.at[done], sems.at[p // 4]))
            copies[-1].start()
    return copies


def pack_own_kernel(fb_ref, key_ref, value_ref, out_ref, kv_ref, asked_buf, out_buf, sems, in_sems):
    loads = [
        pltpu.make_async_copy(ref.at[t], kv_ref.at[t, which], in_sems.at[t, which])
        for t in range(2)
        for which, ref in ((0, key_ref), (1, value_ref))
    ]
    for copy in loads:
        copy.start()
    for copy in loads:
        copy.wait()
    for copy in pack(fb_ref, kv_ref, out_ref, asked_buf, out_buf, sems, 0):
        copy.wait()


def pack_partner_kernel(fb_ref, own_ref, partner_ref, out_ref, up_ref, down_ref, asked_buf, out_buf, sems):
    shard, shards, zh, y = place()
    copies = pack(fb_ref, partner_ref, out_ref, asked_buf, out_buf, sems, 1)
    up_ref[...] = jnp.where(y == lax.axis_size("y") - 1, partner_ref[...], own_ref[...])
    down_ref[...] = jnp.where(y == 0, partner_ref[...], own_ref[...])
    for copy in copies:
        copy.wait()


def stage(fb_ref, t, kv_ref, prev_ref, next_ref, far_refs, kbuf, vbuf):
    shard, shards, zh, y = place()
    plane = far_refs[0].shape[0]
    for which, buf in ((0, kbuf), (1, vbuf)):
        buf[0:128] = prev_ref[t, which]
        buf[128:256] = kv_ref[t, which]
        buf[256:384] = next_ref[t, which]
    for f in range(fb_ref.shape[1]):
        _, slot = listed(fb_ref, t, shard, shards, zh, f)
        rows = slice(STEP + f * BLK, STEP + (f + 1) * BLK)
        here = slot < plane
        at = jnp.where(here, slot, slot - plane)
        for which, buf in ((0, kbuf), (1, vbuf)):
            buf[rows] = jnp.where(here, *(ref[at, part(t, which)] for ref in far_refs))


def biased(fb_ref, t, slopes_ref, q2, kbuf, put):
    shard, shards, zh, y = place()
    cols = q2.shape[0]
    half = cols // 2
    head_col = lax.broadcasted_iota(jnp.int32, (1, cols), 1)
    slope = jnp.where(head_col < half, slopes_ref[0], slopes_ref[1])
    r = lax.broadcasted_iota(jnp.int32, (STEP, cols), 0)
    c = lax.broadcasted_iota(jnp.int32, (STEP, cols), 1)
    c = jnp.where(c < half, c, c - half)
    delta = r - 128 - c
    low = jnp.where(shard > 0, 0, 128)
    high = jnp.where(shard < shards - 1, STEP, 256)
    edge = jnp.where(c < BLK, 0, BLK)
    ok = (r >= jnp.maximum(edge, low)) & (r < jnp.minimum(edge + 320, high))
    scores = dot(kbuf[0:STEP], q2, NT) - slope * jnp.abs(delta).astype(f32)
    scores = jnp.where(ok, scores, masked_value)
    put(0, STEP, scores)
    top = jnp.max(scores, axis=0, keepdims=True)
    far_bias = slope * (-float((BAND + 1) * BLK))
    for lo in range(STEP, kbuf.shape[0], FAR_STEP):
        scores = dot(kbuf[lo : lo + FAR_STEP], q2, NT)
        parts = []
        for i in range(FAR_STEP // BLK):
            there, _ = listed(fb_ref, t, shard, shards, zh, (lo - STEP) // BLK + i)
            row = jnp.where(there, far_bias, masked_value)
            parts.append(scores[i * BLK : (i + 1) * BLK] + row)
        scores = jnp.concatenate(parts, axis=0)
        put(lo, lo + FAR_STEP, scores)
        top = jnp.maximum(top, jnp.max(scores, axis=0, keepdims=True))
    return top


def context_grad_kernel(ref0, ref2, ref4, ref6, odd_ref, weight_ref, out_ref, buf):
    count, rows, _ = buf.shape
    got = [x for k, ref in enumerate((ref0, ref2, ref4, ref6)) for x in (ref[...], odd_ref[k])]
    got = jnp.concatenate(got, axis=0)
    out = dot(got, weight_ref[...], NT).astype(bf16)
    for k in range(count):
        buf[k] = out[k * rows : (k + 1) * rows]
    at = lax.axis_index("tp")
    for k in range(count):
        out_ref[k * rows : (k + 1) * rows] = buf[lax.bitwise_xor(at, k)]


def attend_kernel(
    fb_ref, slopes_hbm, q_ref, kv_ref, prev_ref, next_ref, far_own, far_partner, grad_ref, mirrored_ref,
    ctx_ref, rev_ref, gq_ref, own_out, prev_out, next_out, partner_out, here_out,
    kbuf, vbuf, pbuf, dbuf, far_buf0, far_buf1, sems, slopes_ref, slopes_sem,
):
    shard, shards, zh, y = place()
    n = 2 * HD
    eye = one_hot(n, lambda r: r)
    total = kbuf.shape[0]
    slopes_copy = pltpu.make_async_copy(slopes_hbm, slopes_ref, slopes_sem)
    slopes_copy.start()
    copies = []
    for t in range(2):
        far_buf = (far_buf0, far_buf1)[t]
        spare = far_buf.shape[0] - 1
        to = [listed(fb_ref, t, shard, shards, zh, f) for f in range(fb_ref.shape[1])]
        to = [jnp.where(there, slot, spare) for there, slot in to]
        stage(fb_ref, t, kv_ref, prev_ref, next_ref, (far_own, far_partner), kbuf, vbuf)
        q2 = two_heads(q_ref[t] * HD ** (-0.5))
        if t == 0:
            slopes_copy.wait()
        g2 = two_heads(flipped(mirrored_ref[...]) if t == 1 else grad_ref[...])
        cols = q2.shape[0]

        def put(lo, hi, scores):
            pbuf[lo:hi] = scores

        top = biased(fb_ref, t, slopes_ref, q2, kbuf, put)
        norm = jnp.zeros((1, cols), f32)
        row_dot = jnp.zeros((1, cols), f32)
        for lo in range(0, total, FAR_STEP):
            w = jnp.exp(pbuf[lo : lo + FAR_STEP] - top)
            gp = dot(vbuf[lo : lo + FAR_STEP], g2, NT)
            pbuf[lo : lo + FAR_STEP] = w
            dbuf[lo : lo + FAR_STEP] = gp
            norm = norm + jnp.sum(w, axis=0, keepdims=True)
            row_dot = row_dot + jnp.sum(w * gp, axis=0, keepdims=True)
        inv = 1.0 / norm
        row_dot = row_dot * inv
        gq_acc = jnp.zeros((n, cols), f32)
        ctx_acc = jnp.zeros((n, cols), f32)
        for lo in range(0, total, STEP):
            p = pbuf[lo : lo + STEP] * inv
            low = p.astype(bf16)
            ds = (p * (dbuf[lo : lo + STEP] - row_dot)).astype(bf16)
            ctx_acc = ctx_acc + dot(vbuf[lo : lo + STEP], low, TN)
            gq_acc = gq_acc + dot(kbuf[lo : lo + STEP], ds, TN)
            for which, x in ((0, dot(ds, q2, NN)), (1, dot(low, g2, NN))):
                if lo == 0:
                    prev_out[t, which] = x[0:128].astype(bf16)
                    own_out[t, which] = x[128:256]
                    next_out[t, which] = x[256:384].astype(bf16)
                else:
                    x = x.astype(bf16)
                    for i in range(STEP // BLK):
                        far_buf[to[(lo - STEP) // BLK + i], which * BLK : (which + 1) * BLK] = x[i * BLK : (i + 1) * BLK]

        plane = far_own.shape[0]
        for k, (out, rows) in enumerate(((here_out, pl.ds(0, plane)), (partner_out, pl.ds(plane, plane)))):
            to = out.at[:, 2 * t * BLK : 2 * (t + 1) * BLK]
            copies.append(pltpu.make_async_copy(far_buf.at[rows], to, sems.at[t, k]))
            copies[-1].start()
        gq_ref[t] = (pick_heads(gq_acc) * HD ** (-0.5)).astype(bf16)
        ctx = pick_heads(ctx_acc).astype(bf16)
        if t == 1:
            rev_ref[...] = flipped(ctx)
        else:
            ctx_ref[...] = ctx
    for copy in copies:
        copy.wait()


def combine(fb_ref, far_ref, asked_buf, rel, put):
    shard, shards, zh, y = place()
    asked_rows(fb_ref, asked_buf, rel)
    rows = 32
    for t in range(2):
        for which in range(2):
            for lo in range(0, BLK, rows):
                first = jnp.zeros((rows, 2 * HD), f32)
                second = jnp.zeros((rows, 2 * HD), f32)
                at = part(t, which).start + lo
                for p, reader in enumerate(plane_readers(zh)):
                    block = asked_by(asked_buf, t, reader, rows)
                    x = far_ref[p, at : at + rows].astype(f32)
                    first = first + jnp.where(block == 1, x, 0.0)
                    second = second + jnp.where(block == 2, x, 0.0)
                put(t, which, slice(lo, lo + rows), first)
                put(t, which, slice(BLK + lo, BLK + lo + rows), second)


def combine_partner_kernel(fb_ref, prev_ref, next_ref, far_ref, out_ref, asked_buf):
    shard, shards, zh, y = place()
    last = lax.axis_size("y") - 1

    def put(t, which, rows, far):
        far = far + jnp.where(y == 0, prev_ref[t, which, rows].astype(f32), 0.0)
        far = far + jnp.where(y == last, next_ref[t, which, rows].astype(f32), 0.0)
        out_ref[t, which, rows] = far.astype(bf16)

    combine(fb_ref, far_ref, asked_buf, 1, put)


def combine_own_kernel(fb_ref, own_ref, prev_ref, next_ref, other_ref, far_ref, gk_ref, gv_ref, asked_buf):
    shard, shards, zh, y = place()
    last = lax.axis_size("y") - 1

    def put(t, which, rows, far):
        total = own_ref[t, which, rows] + jnp.where(y == 0, 0.0, prev_ref[t, which, rows].astype(f32))
        total = total + jnp.where(y == last, 0.0, next_ref[t, which, rows].astype(f32))
        total = total + other_ref[t, which, rows].astype(f32) + far
        (gk_ref, gv_ref)[which][t, rows] = total.astype(bf16)

    combine(fb_ref, far_ref, asked_buf, 0, put)


def project_kernel(ctx_ref, back_ref, weight_ref, even_ref, odd_ref, sum_buf):
    total = (ctx_ref[...].astype(f32) + back_ref[...].astype(f32)).astype(bf16)
    count, rows, _ = sum_buf.shape
    for k in range(count):
        sum_buf[k] = total[k * rows : (k + 1) * rows]
    at = lax.axis_index("tp")
    blocks = jnp.concatenate([sum_buf[lax.bitwise_xor(at, j)] for j in range(count)], axis=0)
    out = dot(blocks, weight_ref[...], NN)
    for j in range(count):
        ref = (even_ref, odd_ref)[j % 2]
        ref[j // 2] = out[j * rows : (j + 1) * rows].astype(ref.dtype)


def smem():
    return pl.BlockSpec(memory_space=pltpu.SMEM)


def vmem():
    return pl.BlockSpec(memory_space=pltpu.VMEM)


def hbm():
    return pl.BlockSpec(memory_space=pltpu.HBM)


def shape(dims, dtype=bf16):
    return jax.ShapeDtypeStruct(dims, dtype)


def cost(flops, nbytes, exps=0):
    return pl.CostEstimate(flops=flops, bytes_accessed=nbytes, transcendentals=exps)


def swap(x, bit):
    count = lax.axis_size("tp")
    return lax.ppermute(x, "tp", [(i, i ^ bit) for i in range(count)])


def per_device(
    residual, queries, keys, values, slopes, out_weight, cotangent, far_blocks, far_count
):
    nx, nz, ny = (lax.axis_size(a) for a in SEQ)
    seq_count = nx * nz * ny
    tp_count = lax.axis_size("tp")
    tok_rows, width = queries.shape[1:]
    total_keys = 3 * tok_rows + far_blocks.shape[1] * BLK
    model = out_weight.shape[1]
    cols = 2 * tok_rows
    both = (2, 2, tok_rows, width)
    pieces = (tp_count, tok_rows // tp_count, width)
    slots = (nx * ny, 4 * BLK, width)

    def plane_a2a(x):
        return lax.all_to_all(x, ("x", "y"), split_axis=0, concat_axis=0, tiled=True)

    def z_swap(x):
        return lax.ppermute(x, "zh", [(i, nz - 1 - i) for i in range(nz)])

    asked = pltpu.VMEM((2, seq_count, 2 * HD), jnp.int32)
    packed = [asked, pltpu.VMEM(slots, bf16), pltpu.SemaphoreType.DMA((nx * ny // 4,))]
    outgoing, key_value = pl.pallas_call(
        pack_own_kernel,
        out_shape=(pltpu.HBM(slots, bf16), shape(both)),
        in_specs=[vmem(), hbm(), hbm()],
        out_specs=(hbm(), vmem()),
        scratch_shapes=packed + [pltpu.SemaphoreType.DMA((2, 2))],
        cost_estimate=cost(500_000, 1_500_000),
        compiler_params=pltpu.CompilerParams(vmem_limit_bytes=LIMIT),
        name="pack_own",
    )(far_blocks, *(pltpu.with_memory_space_constraint(x, pltpu.HBM) for x in (keys, values)))
    far_own = plane_a2a(outgoing)
    partner = z_swap(key_value)
    outgoing, to_up, to_down = pl.pallas_call(
        pack_partner_kernel,
        out_shape=(pltpu.HBM(slots, bf16), shape(both), shape(both)),
        in_specs=[vmem()] * 3,
        out_specs=(hbm(), vmem(), vmem()),
        scratch_shapes=packed,
        cost_estimate=cost(500_000, 1_500_000),
        compiler_params=pltpu.CompilerParams(vmem_limit_bytes=LIMIT),
        name="pack_partner",
    )(far_blocks, key_value, partner)
    same_core = [cotangent] + [swap(cotangent, bit) for bit in (2, 4, 6)]
    other_core = swap(jnp.stack(same_core), 1)
    outgoing, other_core = lax.optimization_barrier((outgoing, other_core))
    far_partner = plane_a2a(outgoing)

    def flat(x, zh, y):
        return (x * nz + zh) * ny + y

    places = [(x, zh, y) for x in range(nx) for zh in range(nz) for y in range(ny)]
    up, down = [], []
    for x, zh, y in places:
        if y < ny - 1:
            up.append((flat(x, zh, y), flat(x, zh, y + 1)))
        elif zh == nz - 1:
            up.append((flat(x, zh, y), flat(x, zh, 0)))
        elif x < nx - 1:
            up.append((flat(x, zh, y), flat(x + 1, zh, 0)))
        if y > 0:
            down.append((flat(x, zh, y), flat(x, zh, y - 1)))
        elif zh == 0:
            down.append((flat(x, zh, y), flat(x, zh, ny - 1)))
        elif x > 0:
            down.append((flat(x, zh, y), flat(x - 1, zh, ny - 1)))
    mirror = [(i, seq_count - 1 - i) for i in range(seq_count)]
    from_prev = lax.ppermute(to_up, SEQ, up)
    from_next = lax.ppermute(to_down, SEQ, down)

    grad_context = pl.pallas_call(
        context_grad_kernel,
        out_shape=shape((tok_rows, width)),
        in_specs=[vmem()] * 6,
        out_specs=vmem(),
        scratch_shapes=[pltpu.VMEM(pieces, bf16)],
        cost_estimate=cost(34_000_000, 600_000),
        compiler_params=pltpu.CompilerParams(vmem_limit_bytes=LIMIT),
        name="context_grad",
    )(*same_core, other_core, out_weight)
    mirrored = lax.ppermute(grad_context, SEQ, mirror)

    square = shape((tok_rows, width))
    half = pltpu.VMEM((seq_count + 1, 2 * BLK, width), bf16)
    context_fwd, context_rev, grad_queries, own, before, after, partner_grads, here_grads = pl.pallas_call(
        attend_kernel,
        out_shape=(square, square, shape((2, tok_rows, width)), shape(both, f32), shape(both), shape(both))
        + (pltpu.HBM(slots, bf16),) * 2,
        in_specs=[smem(), hbm()] + [vmem()] * 8,
        out_specs=(vmem(),) * 6 + (hbm(),) * 2,
        scratch_shapes=[pltpu.VMEM((total_keys, width), bf16)] * 2
        + [pltpu.VMEM((total_keys, cols), f32)] * 2
        + [half, half, pltpu.SemaphoreType.DMA((2, 2)), pltpu.SMEM(slopes.shape, f32), pltpu.SemaphoreType.DMA(())],
        cost_estimate=cost(4_000_000_000, 8_000_000, 1_000_000),
        compiler_params=pltpu.CompilerParams(vmem_limit_bytes=LIMIT),
        name="attend",
    )(
        far_blocks, pltpu.with_memory_space_constraint(slopes, pltpu.HBM), queries, key_value, from_prev, from_next, far_own, far_partner, grad_context, mirrored)
    context_back = lax.ppermute(context_rev, SEQ, mirror)

    returned_partner = plane_a2a(partner_grads)
    from_prev_grad = lax.ppermute(after, SEQ, [(b, a) for a, b in down])
    from_next_grad = lax.ppermute(before, SEQ, [(b, a) for a, b in up])
    even, odd = pl.pallas_call(
        project_kernel,
        out_shape=(
            shape((tp_count // 2, tok_rows // tp_count, model), f32),
            shape((tp_count // 2, tok_rows // tp_count, model)),
        ),
        in_specs=[vmem()] * 3,
        out_specs=(vmem(),) * 2,
        scratch_shapes=[pltpu.VMEM(pieces, bf16)],
        cost_estimate=cost(34_000_000, 1_000_000),
        compiler_params=pltpu.CompilerParams(vmem_limit_bytes=LIMIT),
        name="project",
    )(context_fwd, context_back, out_weight)
    here_grads, returned_partner, even, odd = lax.optimization_barrier((here_grads, returned_partner, even, odd))
    returned_own = plane_a2a(here_grads)
    other = pl.pallas_call(
        combine_partner_kernel,
        out_shape=shape(both),
        in_specs=[vmem()] * 4,
        out_specs=vmem(),
        scratch_shapes=[asked],
        cost_estimate=cost(2_000_000, 1_500_000),
        compiler_params=pltpu.CompilerParams(vmem_limit_bytes=LIMIT),
        name="combine_partner",
    )(far_blocks, from_prev_grad, from_next_grad, returned_partner)
    other, odd = lax.optimization_barrier((other, odd))
    other = z_swap(other)

    held = even + swap(odd, 1).astype(f32)
    pieces_out = [held[k].astype(bf16) for k in range(1, tp_count // 2)]
    pieces_out[0], other = lax.optimization_barrier((pieces_out[0], other))
    parts = [swap(here, 2 * k + 2) for k, here in enumerate(pieces_out)]
    total = residual.astype(f32) + held[0]
    for part_here in parts:
        total = total + part_here.astype(f32)
    mixed = total.astype(bf16)

    grad_keys, grad_values = pl.pallas_call(
        combine_own_kernel,
        out_shape=(shape((2, tok_rows, width)),) * 2,
        in_specs=[vmem()] * 6,
        out_specs=(vmem(),) * 2,
        scratch_shapes=[asked],
        cost_estimate=cost(2_000_000, 1_500_000),
        compiler_params=pltpu.CompilerParams(vmem_limit_bytes=LIMIT),
        name="combine_own",
    )(far_blocks, own, from_prev_grad, from_next_grad, other, returned_own)
    return (mixed, grad_queries, grad_keys, grad_values)


def solution(mesh):
    split = jax.sharding.Mesh(mesh.devices.reshape(4, 2, 4, -1), SEQ + ("tp",))
    rows = P(SEQ + ("tp",), None)
    strands = P(None, SEQ, "tp")
    return jax.shard_map(
        per_device,
        mesh=split,
        in_specs=(rows, strands, strands, strands, P("tp"), P("tp", None), rows, P(), P()),
        out_specs=(rows, strands, strands, strands),
        check_vma=False,
    )
```

```python
import jax
import jax.numpy as jnp
from jax import lax
from jax.experimental import pallas as pl
from jax.experimental.pallas import tpu as pltpu
from jax.sharding import PartitionSpec as P

HD = 64
BLK = 64
BAND = 2
STEP = 384
FAR_STEP = 256
LIMIT = 24 << 20

masked_value = -1e30
f32 = jnp.float32
bf16 = jnp.bfloat16

NT = (((1,), (1,)), ((), ()))
NN = (((1,), (0,)), ((), ()))
TN = (((0,), (0,)), ((), ()))


def dot(a, b, dims):
    return lax.dot_general(a, b, dims, preferred_element_type=f32)


def two_heads(x):
    first = lax.broadcasted_iota(jnp.int32, x.shape, 1) < HD
    zero = jnp.zeros_like(x)
    return jnp.concatenate([jnp.where(first, x, zero), jnp.where(first, zero, x)], axis=0)


def pick_heads(xt):
    rows = xt.shape[1] // 2
    own = jnp.concatenate([xt[:HD, :rows], xt[HD:, rows:]], axis=0)
    return own.T


def one_hot(n, at):
    r = lax.broadcasted_iota(jnp.int32, (n, n), 0)
    c = lax.broadcasted_iota(jnp.int32, (n, n), 1)
    return (c == at(r)).astype(bf16)


def flipped(x):
    n = x.shape[0]
    return dot(one_hot(n, lambda r: n - 1 - r), x, NN).astype(bf16)


SEQ = ("x", "zh", "y")


def place():
    x, zh, y = (lax.axis_index(a) for a in SEQ)
    nx, nz, ny = (lax.axis_size(a) for a in SEQ)
    return (x * nz + zh) * ny + y, nx * nz * ny, zh, y


def slot_of(owner, zh):
    nx, nz, ny = (lax.axis_size(a) for a in SEQ)
    xz, y = lax.div(owner, ny), lax.rem(owner, ny)
    x, z = lax.div(xz, nz), lax.rem(xz, nz)
    return jnp.where(z == zh, 0, nx * ny) + x * ny + y


def plane_readers(zh):
    nx, nz, ny = (lax.axis_size(a) for a in SEQ)
    return [(x * nz + zh) * ny + y for x in range(nx) for y in range(ny)]


def part(t, which):
    return slice((2 * t + which) * BLK, (2 * t + which + 1) * BLK)


def listed(fb_ref, t, shard, shards, zh, f):
    entry = fb_ref[f, shard if t == 0 else shards - 1 - shard]
    owner = lax.shift_right_arithmetic(entry, 1)
    owner = owner if t == 0 else shards - 1 - owner
    return entry >= 0, jnp.where(entry >= 0, slot_of(owner, zh), 0)


def asked_of(fb, t, shard, shards):
    mine = shard if t == 0 else shards - 1 - shard
    inner = fb & 1
    inner = inner + 1 if t == 0 else 2 - inner
    hit = jnp.where(lax.shift_right_arithmetic(fb, 1) == mine, inner, 0).astype(f32)
    return dot(hit, jnp.ones((fb.shape[0], 2 * HD), f32), TN).astype(jnp.int32)


def asked_rows(fb_ref, asked_buf, rel):
    shard, shards, zh, y = place()
    target = shard + rel * (1 - 2 * zh) * lax.axis_size("y")
    fb = fb_ref[...]
    for t in range(2):
        asked_buf[t] = asked_of(fb, t, target, shards)


def asked_by(asked_buf, t, reader, rows):
    row = reader if t == 0 else asked_buf.shape[1] - 1 - reader
    return jnp.broadcast_to(asked_buf[t, pl.ds(row, 1)], (rows, 2 * HD))


def pack(fb_ref, kv_ref, out_ref, asked_buf, out_buf, sems, rel):
    shard, shards, zh, y = place()
    asked_rows(fb_ref, asked_buf, rel)
    copies = []
    for p, reader in enumerate(plane_readers(zh)):
        for t in range(2):
            second = asked_by(asked_buf, t, reader, BLK) == 2
            for which in range(2):
                out_buf[p, part(t, which)] = jnp.where(second, kv_ref[t, which, BLK:], kv_ref[t, which, :BLK])
        if p % 4 == 3:
            done = pl.ds(p - 3, 4)
            copies.append(pltpu.make_async_copy(out_buf.at[done], out_ref.at[done], sems.at[p // 4]))
            copies[-1].start()
    return copies


def pack_own_kernel(fb_ref, key_ref, value_ref, out_ref, kv_ref, fb_buf, asked_buf, out_buf, sems, in_sems, fb_sem):
    loads = [pltpu.make_async_copy(fb_ref, fb_buf, fb_sem)]
    loads += [
        pltpu.make_async_copy(ref.at[t], kv_ref.at[t, which], in_sems.at[t, which])
        for t in range(2)
        for which, ref in ((0, key_ref), (1, value_ref))
    ]
    for copy in loads:
        copy.start()
    for copy in loads:
        copy.wait()
    for copy in pack(fb_buf, kv_ref, out_ref, asked_buf, out_buf, sems, 0):
        copy.wait()


def pack_partner_kernel(fb_ref, own_ref, partner_ref, out_ref, up_ref, down_ref, asked_buf, out_buf, sems):
    shard, shards, zh, y = place()
    copies = pack(fb_ref, partner_ref, out_ref, asked_buf, out_buf, sems, 1)
    up_ref[...] = jnp.where(y == lax.axis_size("y") - 1, partner_ref[...], own_ref[...])
    down_ref[...] = jnp.where(y == 0, partner_ref[...], own_ref[...])
    for copy in copies:
        copy.wait()


def stage(fb_ref, t, kv_ref, prev_ref, next_ref, far_refs, kbuf, vbuf):
    shard, shards, zh, y = place()
    plane = far_refs[0].shape[0]
    for which, buf in ((0, kbuf), (1, vbuf)):
        buf[0:128] = prev_ref[t, which]
        buf[128:256] = kv_ref[t, which]
        buf[256:384] = next_ref[t, which]
    for f in range(fb_ref.shape[0]):
        _, slot = listed(fb_ref, t, shard, shards, zh, f)
        rows = slice(STEP + f * BLK, STEP + (f + 1) * BLK)
        here = slot < plane
        at = jnp.where(here, slot, slot - plane)
        for which, buf in ((0, kbuf), (1, vbuf)):
            buf[rows] = jnp.where(here, *(ref[at, part(t, which)] for ref in far_refs))


def biased(fb_ref, t, slopes_ref, q2, kbuf, put):
    shard, shards, zh, y = place()
    cols = q2.shape[0]
    half = cols // 2
    head_col = lax.broadcasted_iota(jnp.int32, (1, cols), 1)
    slope = jnp.where(head_col < half, slopes_ref[0], slopes_ref[1])
    r = lax.broadcasted_iota(jnp.int32, (STEP, cols), 0)
    c = lax.broadcasted_iota(jnp.int32, (STEP, cols), 1)
    c = jnp.where(c < half, c, c - half)
    delta = r - 128 - c
    low = jnp.where(shard > 0, 0, 128)
    high = jnp.where(shard < shards - 1, STEP, 256)
    edge = jnp.where(c < BLK, 0, BLK)
    ok = (r >= jnp.maximum(edge, low)) & (r < jnp.minimum(edge + 320, high))
    scores = dot(kbuf[0:STEP], q2, NT) - slope * jnp.abs(delta).astype(f32)
    scores = jnp.where(ok, scores, masked_value)
    put(0, STEP, scores)
    top = jnp.max(scores, axis=0, keepdims=True)
    far_bias = slope * (-float((BAND + 1) * BLK))
    for lo in range(STEP, kbuf.shape[0], FAR_STEP):
        scores = dot(kbuf[lo : lo + FAR_STEP], q2, NT)
        parts = []
        for i in range(FAR_STEP // BLK):
            there, _ = listed(fb_ref, t, shard, shards, zh, (lo - STEP) // BLK + i)
            row = jnp.where(there, far_bias, masked_value)
            parts.append(scores[i * BLK : (i + 1) * BLK] + row)
        scores = jnp.concatenate(parts, axis=0)
        put(lo, lo + FAR_STEP, scores)
        top = jnp.maximum(top, jnp.max(scores, axis=0, keepdims=True))
    return top


def context_grad_kernel(ref0, ref2, ref4, ref6, odd_ref, weight_ref, out_ref, buf):
    count, rows, _ = buf.shape
    got = [x for k, ref in enumerate((ref0, ref2, ref4, ref6)) for x in (ref[...], odd_ref[k])]
    got = jnp.concatenate(got, axis=0)
    out = dot(got, weight_ref[...], NT).astype(bf16)
    for k in range(count):
        buf[k] = out[k * rows : (k + 1) * rows]
    at = lax.axis_index("tp")
    for k in range(count):
        out_ref[k * rows : (k + 1) * rows] = buf[lax.bitwise_xor(at, k)]


def attend_kernel(
    fb_ref, slopes_hbm, q_ref, kv_ref, prev_ref, next_ref, far_own, far_partner, grad_ref, mirrored_ref,
    ctx_ref, rev_ref, gq_ref, own_out, prev_out, next_out, partner_out, here_out,
    kbuf, vbuf, pbuf, dbuf, far_buf0, far_buf1, sems, slopes_ref, slopes_sem,
):
    shard, shards, zh, y = place()
    n = 2 * HD
    eye = one_hot(n, lambda r: r)
    total = kbuf.shape[0]
    slopes_copy = pltpu.make_async_copy(slopes_hbm, slopes_ref, slopes_sem)
    slopes_copy.start()
    copies = []
    for t in range(2):
        far_buf = (far_buf0, far_buf1)[t]
        spare = far_buf.shape[0] - 1
        to = [listed(fb_ref, t, shard, shards, zh, f) for f in range(fb_ref.shape[0])]
        to = [jnp.where(there, slot, spare) for there, slot in to]
        stage(fb_ref, t, kv_ref, prev_ref, next_ref, (far_own, far_partner), kbuf, vbuf)
        q2 = two_heads(q_ref[t] * HD ** (-0.5))
        if t == 0:
            slopes_copy.wait()
        g2 = two_heads(flipped(mirrored_ref[...]) if t == 1 else grad_ref[...])
        cols = q2.shape[0]

        def put(lo, hi, scores):
            pbuf[lo:hi] = scores

        top = biased(fb_ref, t, slopes_ref, q2, kbuf, put)
        norm = jnp.zeros((1, cols), f32)
        row_dot = jnp.zeros((1, cols), f32)
        for lo in range(0, total, FAR_STEP):
            w = jnp.exp(pbuf[lo : lo + FAR_STEP] - top)
            gp = dot(vbuf[lo : lo + FAR_STEP], g2, NT)
            pbuf[lo : lo + FAR_STEP] = w
            dbuf[lo : lo + FAR_STEP] = gp
            norm = norm + jnp.sum(w, axis=0, keepdims=True)
            row_dot = row_dot + jnp.sum(w * gp, axis=0, keepdims=True)
        inv = 1.0 / norm
        row_dot = row_dot * inv
        gq_acc = jnp.zeros((n, cols), f32)
        ctx_acc = jnp.zeros((n, cols), f32)
        for lo in range(0, total, STEP):
            p = pbuf[lo : lo + STEP] * inv
            low = p.astype(bf16)
            ds = (p * (dbuf[lo : lo + STEP] - row_dot)).astype(bf16)
            ctx_acc = ctx_acc + dot(vbuf[lo : lo + STEP], low, TN)
            gq_acc = gq_acc + dot(kbuf[lo : lo + STEP], ds, TN)
            for which, x in ((0, dot(ds, q2, NN)), (1, dot(low, g2, NN))):
                if lo == 0:
                    prev_out[t, which] = x[0:128].astype(bf16)
                    own_out[t, which] = x[128:256]
                    next_out[t, which] = x[256:384].astype(bf16)
                else:
                    x = x.astype(bf16)
                    for i in range(STEP // BLK):
                        far_buf[to[(lo - STEP) // BLK + i], which * BLK : (which + 1) * BLK] = x[i * BLK : (i + 1) * BLK]

        plane = far_own.shape[0]
        for k, (out, rows) in enumerate(((here_out, pl.ds(0, plane)), (partner_out, pl.ds(plane, plane)))):
            to = out.at[:, 2 * t * BLK : 2 * (t + 1) * BLK]
            copies.append(pltpu.make_async_copy(far_buf.at[rows], to, sems.at[t, k]))
            copies[-1].start()
        gq_ref[t] = (pick_heads(gq_acc) * HD ** (-0.5)).astype(bf16)
        ctx = pick_heads(ctx_acc).astype(bf16)
        if t == 1:
            rev_ref[...] = flipped(ctx)
        else:
            ctx_ref[...] = ctx
    for copy in copies:
        copy.wait()


def combine(fb_ref, far_ref, asked_buf, rel, put):
    shard, shards, zh, y = place()
    asked_rows(fb_ref, asked_buf, rel)
    rows = 32
    for t in range(2):
        for which in range(2):
            for lo in range(0, BLK, rows):
                first = jnp.zeros((rows, 2 * HD), f32)
                second = jnp.zeros((rows, 2 * HD), f32)
                at = part(t, which).start + lo
                for p, reader in enumerate(plane_readers(zh)):
                    block = asked_by(asked_buf, t, reader, rows)
                    x = far_ref[p, at : at + rows].astype(f32)
                    first = first + jnp.where(block == 1, x, 0.0)
                    second = second + jnp.where(block == 2, x, 0.0)
                put(t, which, slice(lo, lo + rows), first)
                put(t, which, slice(BLK + lo, BLK + lo + rows), second)


def combine_partner_kernel(fb_ref, prev_ref, next_ref, far_ref, out_ref, asked_buf):
    shard, shards, zh, y = place()
    last = lax.axis_size("y") - 1

    def put(t, which, rows, far):
        far = far + jnp.where(y == 0, prev_ref[t, which, rows].astype(f32), 0.0)
        far = far + jnp.where(y == last, next_ref[t, which, rows].astype(f32), 0.0)
        out_ref[t, which, rows] = far.astype(bf16)

    combine(fb_ref, far_ref, asked_buf, 1, put)


def combine_own_kernel(fb_ref, own_ref, prev_ref, next_ref, other_ref, far_ref, gk_ref, gv_ref, asked_buf):
    shard, shards, zh, y = place()
    last = lax.axis_size("y") - 1

    def put(t, which, rows, far):
        total = own_ref[t, which, rows] + jnp.where(y == 0, 0.0, prev_ref[t, which, rows].astype(f32))
        total = total + jnp.where(y == last, 0.0, next_ref[t, which, rows].astype(f32))
        total = total + other_ref[t, which, rows].astype(f32) + far
        (gk_ref, gv_ref)[which][t, rows] = total.astype(bf16)

    combine(fb_ref, far_ref, asked_buf, 0, put)


def project_kernel(ctx_ref, back_ref, weight_ref, even_ref, odd_ref, sum_buf):
    total = (ctx_ref[...].astype(f32) + back_ref[...].astype(f32)).astype(bf16)
    count, rows, _ = sum_buf.shape
    for k in range(count):
        sum_buf[k] = total[k * rows : (k + 1) * rows]
    at = lax.axis_index("tp")
    blocks = jnp.concatenate([sum_buf[lax.bitwise_xor(at, j)] for j in range(count)], axis=0)
    out = dot(blocks, weight_ref[...], NN)
    for j in range(count):
        ref = (even_ref, odd_ref)[j % 2]
        ref[j // 2] = out[j * rows : (j + 1) * rows].astype(ref.dtype)


def smem():
    return pl.BlockSpec(memory_space=pltpu.SMEM)


def vmem():
    return pl.BlockSpec(memory_space=pltpu.VMEM)


def hbm():
    return pl.BlockSpec(memory_space=pltpu.HBM)


def shape(dims, dtype=bf16):
    return jax.ShapeDtypeStruct(dims, dtype)


def cost(flops, nbytes, exps=0):
    return pl.CostEstimate(flops=flops, bytes_accessed=nbytes, transcendentals=exps)


def swap(x, bit):
    count = lax.axis_size("tp")
    return lax.ppermute(x, "tp", [(i, i ^ bit) for i in range(count)])


def per_device(
    residual, queries, keys, values, slopes, out_weight, cotangent, far_blocks, far_count
):
    nx, nz, ny = (lax.axis_size(a) for a in SEQ)
    seq_count = nx * nz * ny
    tp_count = lax.axis_size("tp")
    tok_rows, width = queries.shape[1:]
    total_keys = 3 * tok_rows + far_blocks.shape[1] * BLK
    model = out_weight.shape[1]
    cols = 2 * tok_rows
    both = (2, 2, tok_rows, width)
    pieces = (tp_count, tok_rows // tp_count, width)
    slots = (nx * ny, 4 * BLK, width)

    def plane_a2a(x):
        return lax.all_to_all(x, ("x", "y"), split_axis=0, concat_axis=0, tiled=True)

    def z_swap(x):
        return lax.ppermute(x, "zh", [(i, nz - 1 - i) for i in range(nz)])

    lists = far_blocks.T
    asked = pltpu.VMEM((2, seq_count, 2 * HD), jnp.int32)
    packed = [asked, pltpu.VMEM(slots, bf16), pltpu.SemaphoreType.DMA((nx * ny // 4,))]
    outgoing, key_value, near_lists = pl.pallas_call(
        pack_own_kernel,
        out_shape=(pltpu.HBM(slots, bf16), shape(both), shape(lists.shape, jnp.int32)),
        in_specs=[hbm()] * 3,
        out_specs=(hbm(), vmem(), vmem()),
        scratch_shapes=packed
        + [pltpu.SemaphoreType.DMA((2, 2)), pltpu.SemaphoreType.DMA(())],
        cost_estimate=cost(500_000, 1_500_000),
        compiler_params=pltpu.CompilerParams(vmem_limit_bytes=LIMIT),
        name="pack_own",
    )(*(pltpu.with_memory_space_constraint(x, pltpu.HBM) for x in (lists, keys, values)))
    far_own = plane_a2a(outgoing)
    partner = z_swap(key_value)
    outgoing, to_up, to_down = pl.pallas_call(
        pack_partner_kernel,
        out_shape=(pltpu.HBM(slots, bf16), shape(both), shape(both)),
        in_specs=[vmem()] * 3,
        out_specs=(hbm(), vmem(), vmem()),
        scratch_shapes=packed,
        cost_estimate=cost(500_000, 1_500_000),
        compiler_params=pltpu.CompilerParams(vmem_limit_bytes=LIMIT),
        name="pack_partner",
    )(near_lists, key_value, partner)
    same_core = [cotangent] + [swap(cotangent, bit) for bit in (2, 4, 6)]
    other_core = swap(jnp.stack(same_core), 1)
    outgoing, other_core = lax.optimization_barrier((outgoing, other_core))
    far_partner = plane_a2a(outgoing)

    def flat(x, zh, y):
        return (x * nz + zh) * ny + y

    places = [(x, zh, y) for x in range(nx) for zh in range(nz) for y in range(ny)]
    up, down = [], []
    for x, zh, y in places:
        if y < ny - 1:
            up.append((flat(x, zh, y), flat(x, zh, y + 1)))
        elif zh == nz - 1:
            up.append((flat(x, zh, y), flat(x, zh, 0)))
        elif x < nx - 1:
            up.append((flat(x, zh, y), flat(x + 1, zh, 0)))
        if y > 0:
            down.append((flat(x, zh, y), flat(x, zh, y - 1)))
        elif zh == 0:
            down.append((flat(x, zh, y), flat(x, zh, ny - 1)))
        elif x > 0:
            down.append((flat(x, zh, y), flat(x - 1, zh, ny - 1)))
    mirror = [(i, seq_count - 1 - i) for i in range(seq_count)]
    from_prev = lax.ppermute(to_up, SEQ, up)
    from_next = lax.ppermute(to_down, SEQ, down)

    grad_context = pl.pallas_call(
        context_grad_kernel,
        out_shape=shape((tok_rows, width)),
        in_specs=[vmem()] * 6,
        out_specs=vmem(),
        scratch_shapes=[pltpu.VMEM(pieces, bf16)],
        cost_estimate=cost(34_000_000, 600_000),
        compiler_params=pltpu.CompilerParams(vmem_limit_bytes=LIMIT),
        name="context_grad",
    )(*same_core, other_core, out_weight)
    mirrored = lax.ppermute(grad_context, SEQ, mirror)

    square = shape((tok_rows, width))
    half = pltpu.VMEM((seq_count + 1, 2 * BLK, width), bf16)
    context_fwd, context_rev, grad_queries, own, before, after, partner_grads, here_grads = pl.pallas_call(
        attend_kernel,
        out_shape=(square, square, shape((2, tok_rows, width)), shape(both, f32), shape(both), shape(both))
        + (pltpu.HBM(slots, bf16),) * 2,
        in_specs=[smem(), hbm()] + [vmem()] * 8,
        out_specs=(vmem(),) * 6 + (hbm(),) * 2,
        scratch_shapes=[pltpu.VMEM((total_keys, width), bf16)] * 2
        + [pltpu.VMEM((total_keys, cols), f32)] * 2
        + [half, half, pltpu.SemaphoreType.DMA((2, 2)), pltpu.SMEM(slopes.shape, f32), pltpu.SemaphoreType.DMA(())],
        cost_estimate=cost(4_000_000_000, 8_000_000, 1_000_000),
        compiler_params=pltpu.CompilerParams(vmem_limit_bytes=LIMIT),
        name="attend",
    )(
        near_lists, pltpu.with_memory_space_constraint(slopes, pltpu.HBM), queries, key_value, from_prev, from_next, far_own, far_partner, grad_context, mirrored)
    context_back = lax.ppermute(context_rev, SEQ, mirror)

    returned_partner = plane_a2a(partner_grads)
    from_prev_grad = lax.ppermute(after, SEQ, [(b, a) for a, b in down])
    from_next_grad = lax.ppermute(before, SEQ, [(b, a) for a, b in up])
    here_grads, returned_partner, context_back = lax.optimization_barrier(
        (here_grads, returned_partner, context_back)
    )
    returned_own = plane_a2a(here_grads)
    other = pl.pallas_call(
        combine_partner_kernel,
        out_shape=shape(both),
        in_specs=[vmem()] * 4,
        out_specs=vmem(),
        scratch_shapes=[asked],
        cost_estimate=cost(2_000_000, 1_500_000),
        compiler_params=pltpu.CompilerParams(vmem_limit_bytes=LIMIT),
        name="combine_partner",
    )(near_lists, from_prev_grad, from_next_grad, returned_partner)
    other, context_back = lax.optimization_barrier((other, context_back))
    other = z_swap(other)

    even, odd = pl.pallas_call(
        project_kernel,
        out_shape=(
            shape((tp_count // 2, tok_rows // tp_count, model), f32),
            shape((tp_count // 2, tok_rows // tp_count, model)),
        ),
        in_specs=[vmem()] * 3,
        out_specs=(vmem(),) * 2,
        scratch_shapes=[pltpu.VMEM(pieces, bf16)],
        cost_estimate=cost(34_000_000, 1_000_000),
        compiler_params=pltpu.CompilerParams(vmem_limit_bytes=LIMIT),
        name="project",
    )(context_fwd, context_back, out_weight)
    held = even + swap(odd, 1).astype(f32)
    parts = [swap(held[k].astype(bf16), 2 * k) for k in range(1, tp_count // 2)]
    total = residual.astype(f32) + held[0]
    for part_here in parts:
        total = total + part_here.astype(f32)
    mixed = total.astype(bf16)

    grad_keys, grad_values = pl.pallas_call(
        combine_own_kernel,
        out_shape=(shape((2, tok_rows, width)),) * 2,
        in_specs=[vmem()] * 6,
        out_specs=(vmem(),) * 2,
        scratch_shapes=[asked],
        cost_estimate=cost(2_000_000, 1_500_000),
        compiler_params=pltpu.CompilerParams(vmem_limit_bytes=LIMIT),
        name="combine_own",
    )(near_lists, own, from_prev_grad, from_next_grad, other, returned_own)
    return (mixed, grad_queries, grad_keys, grad_values)


def solution(mesh):
    split = jax.sharding.Mesh(mesh.devices.reshape(4, 2, 4, -1), SEQ + ("tp",))
    rows = P(SEQ + ("tp",), None)
    strands = P(None, SEQ, "tp")
    return jax.shard_map(
        per_device,
        mesh=split,
        in_specs=(rows, strands, strands, strands, P("tp"), P("tp", None), rows, P(), P()),
        out_specs=(rows, strands, strands, strands),
        check_vma=False,
    )
```

```python
import jax
import jax.numpy as jnp
from jax import lax
from jax.experimental import pallas as pl
from jax.experimental.pallas import tpu as pltpu
from jax.sharding import PartitionSpec as P

HD = 64
BLK = 64
BAND = 2
STEP = 384
FAR_STEP = 256
LIMIT = 24 << 20

masked_value = -1e30
f32 = jnp.float32
bf16 = jnp.bfloat16

NT = (((1,), (1,)), ((), ()))
NN = (((1,), (0,)), ((), ()))
TN = (((0,), (0,)), ((), ()))


def dot(a, b, dims):
    return lax.dot_general(a, b, dims, preferred_element_type=f32)


def two_heads(x):
    first = lax.broadcasted_iota(jnp.int32, x.shape, 1) < HD
    zero = jnp.zeros_like(x)
    return jnp.concatenate([jnp.where(first, x, zero), jnp.where(first, zero, x)], axis=0)


def pick_heads(xt):
    rows = xt.shape[1] // 2
    own = jnp.concatenate([xt[:HD, :rows], xt[HD:, rows:]], axis=0)
    return own.T


def one_hot(n, at):
    r = lax.broadcasted_iota(jnp.int32, (n, n), 0)
    c = lax.broadcasted_iota(jnp.int32, (n, n), 1)
    return (c == at(r)).astype(bf16)


def flipped(x):
    n = x.shape[0]
    return dot(one_hot(n, lambda r: n - 1 - r), x, NN).astype(bf16)


SEQ = ("x", "zh", "y")


def place():
    x, zh, y = (lax.axis_index(a) for a in SEQ)
    nx, nz, ny = (lax.axis_size(a) for a in SEQ)
    return (x * nz + zh) * ny + y, nx * nz * ny, zh, y


def slot_of(owner, zh):
    nx, nz, ny = (lax.axis_size(a) for a in SEQ)
    xz, y = lax.div(owner, ny), lax.rem(owner, ny)
    x, z = lax.div(xz, nz), lax.rem(xz, nz)
    return jnp.where(z == zh, 0, nx * ny) + x * ny + y


def plane_readers(zh):
    nx, nz, ny = (lax.axis_size(a) for a in SEQ)
    return [(x * nz + zh) * ny + y for x in range(nx) for y in range(ny)]


def part(t, which):
    return slice((2 * t + which) * BLK, (2 * t + which + 1) * BLK)


def listed(fb_ref, t, shard, shards, zh, f):
    entry = fb_ref[f, shard if t == 0 else shards - 1 - shard]
    owner = lax.shift_right_arithmetic(entry, 1)
    owner = owner if t == 0 else shards - 1 - owner
    return entry >= 0, jnp.where(entry >= 0, slot_of(owner, zh), 0)


def asked_of(fb, t, shard, shards):
    mine = shard if t == 0 else shards - 1 - shard
    inner = fb & 1
    inner = inner + 1 if t == 0 else 2 - inner
    hit = jnp.where(lax.shift_right_arithmetic(fb, 1) == mine, inner, 0).astype(f32)
    return dot(hit, jnp.ones((fb.shape[0], 2 * HD), f32), TN).astype(jnp.int32)


def asked_rows(fb_ref, asked_buf, rel):
    shard, shards, zh, y = place()
    target = shard + rel * (1 - 2 * zh) * lax.axis_size("y")
    fb = fb_ref[...]
    for t in range(2):
        asked_buf[t] = asked_of(fb, t, target, shards)


def asked_by(asked_buf, t, reader, rows):
    row = reader if t == 0 else asked_buf.shape[1] - 1 - reader
    return jnp.broadcast_to(asked_buf[t, pl.ds(row, 1)], (rows, 2 * HD))


def pack(fb_ref, kv_ref, out_ref, asked_buf, out_buf, sems, rel):
    shard, shards, zh, y = place()
    asked_rows(fb_ref, asked_buf, rel)
    copies = []
    for p, reader in enumerate(plane_readers(zh)):
        for t in range(2):
            second = asked_by(asked_buf, t, reader, BLK) == 2
            for which in range(2):
                out_buf[p, part(t, which)] = jnp.where(second, kv_ref[t, which, BLK:], kv_ref[t, which, :BLK])
        if p % 4 == 3:
            done = pl.ds(p - 3, 4)
            copies.append(pltpu.make_async_copy(out_buf.at[done], out_ref.at[done], sems.at[p // 4]))
            copies[-1].start()
    return copies


def pack_own_kernel(fb_ref, key_ref, value_ref, out_ref, kv_ref, fb_buf, asked_buf, out_buf, sems, in_sems, fb_sem):
    loads = [pltpu.make_async_copy(fb_ref, fb_buf, fb_sem)]
    loads += [
        pltpu.make_async_copy(ref.at[t], kv_ref.at[t, which], in_sems.at[t, which])
        for t in range(2)
        for which, ref in ((0, key_ref), (1, value_ref))
    ]
    for copy in loads:
        copy.start()
    for copy in loads:
        copy.wait()
    for copy in pack(fb_buf, kv_ref, out_ref, asked_buf, out_buf, sems, 0):
        copy.wait()


def pack_partner_kernel(fb_ref, own_ref, partner_ref, out_ref, up_ref, down_ref, asked_buf, out_buf, sems):
    shard, shards, zh, y = place()
    copies = pack(fb_ref, partner_ref, out_ref, asked_buf, out_buf, sems, 1)
    up_ref[...] = jnp.where(y == lax.axis_size("y") - 1, partner_ref[...], own_ref[...])
    down_ref[...] = jnp.where(y == 0, partner_ref[...], own_ref[...])
    for copy in copies:
        copy.wait()


def stage(fb_ref, t, kv_ref, prev_ref, next_ref, far_refs, kbuf, vbuf):
    shard, shards, zh, y = place()
    plane = far_refs[0].shape[0]
    for which, buf in ((0, kbuf), (1, vbuf)):
        buf[0:128] = prev_ref[t, which]
        buf[128:256] = kv_ref[t, which]
        buf[256:384] = next_ref[t, which]
    for f in range(fb_ref.shape[0]):
        _, slot = listed(fb_ref, t, shard, shards, zh, f)
        rows = slice(STEP + f * BLK, STEP + (f + 1) * BLK)
        here = slot < plane
        at = jnp.where(here, slot, slot - plane)
        for which, buf in ((0, kbuf), (1, vbuf)):
            buf[rows] = jnp.where(here, *(ref[at, part(t, which)] for ref in far_refs))


def biased(fb_ref, t, slopes_ref, q2, kbuf, put):
    shard, shards, zh, y = place()
    cols = q2.shape[0]
    half = cols // 2
    head_col = lax.broadcasted_iota(jnp.int32, (1, cols), 1)
    slope = jnp.where(head_col < half, slopes_ref[0], slopes_ref[1])
    r = lax.broadcasted_iota(jnp.int32, (STEP, cols), 0)
    c = lax.broadcasted_iota(jnp.int32, (STEP, cols), 1)
    c = jnp.where(c < half, c, c - half)
    delta = r - 128 - c
    low = jnp.where(shard > 0, 0, 128)
    high = jnp.where(shard < shards - 1, STEP, 256)
    edge = jnp.where(c < BLK, 0, BLK)
    ok = (r >= jnp.maximum(edge, low)) & (r < jnp.minimum(edge + 320, high))
    scores = dot(kbuf[0:STEP], q2, NT) - slope * jnp.abs(delta).astype(f32)
    scores = jnp.where(ok, scores, masked_value)
    put(0, STEP, scores)
    top = jnp.max(scores, axis=0, keepdims=True)
    far_bias = slope * (-float((BAND + 1) * BLK))
    for lo in range(STEP, kbuf.shape[0], FAR_STEP):
        scores = dot(kbuf[lo : lo + FAR_STEP], q2, NT)
        parts = []
        for i in range(FAR_STEP // BLK):
            there, _ = listed(fb_ref, t, shard, shards, zh, (lo - STEP) // BLK + i)
            row = jnp.where(there, far_bias, masked_value)
            parts.append(scores[i * BLK : (i + 1) * BLK] + row)
        scores = jnp.concatenate(parts, axis=0)
        put(lo, lo + FAR_STEP, scores)
        top = jnp.maximum(top, jnp.max(scores, axis=0, keepdims=True))
    return top


def context_grad_kernel(ref0, ref2, ref4, ref6, odd_ref, weight_ref, out_ref, buf):
    count, rows, _ = buf.shape
    got = [x for k, ref in enumerate((ref0, ref2, ref4, ref6)) for x in (ref[...], odd_ref[k])]
    got = jnp.concatenate(got, axis=0)
    out = dot(got, weight_ref[...], NT).astype(bf16)
    for k in range(count):
        buf[k] = out[k * rows : (k + 1) * rows]
    at = lax.axis_index("tp")
    for k in range(count):
        out_ref[k * rows : (k + 1) * rows] = buf[lax.bitwise_xor(at, k)]


def attend_kernel(
    fb_ref, slopes_hbm, q_ref, kv_ref, prev_ref, next_ref, far_own, far_partner, grad_ref, mirrored_ref,
    ctx_ref, rev_ref, gq_ref, own_out, prev_out, next_out, partner_out, here_out,
    kbuf, vbuf, pbuf, dbuf, far_buf0, far_buf1, sems, slopes_ref, slopes_sem,
):
    shard, shards, zh, y = place()
    n = 2 * HD
    eye = one_hot(n, lambda r: r)
    total = kbuf.shape[0]
    slopes_copy = pltpu.make_async_copy(slopes_hbm, slopes_ref, slopes_sem)
    slopes_copy.start()
    copies = []
    for t in range(2):
        far_buf = (far_buf0, far_buf1)[t]
        spare = far_buf.shape[0] - 1
        to = [listed(fb_ref, t, shard, shards, zh, f) for f in range(fb_ref.shape[0])]
        to = [jnp.where(there, slot, spare) for there, slot in to]
        stage(fb_ref, t, kv_ref, prev_ref, next_ref, (far_own, far_partner), kbuf, vbuf)
        q2 = two_heads(q_ref[t] * HD ** (-0.5))
        if t == 0:
            slopes_copy.wait()
        g2 = two_heads(flipped(mirrored_ref[...]) if t == 1 else grad_ref[...])
        cols = q2.shape[0]

        def put(lo, hi, scores):
            pbuf[lo:hi] = scores

        top = biased(fb_ref, t, slopes_ref, q2, kbuf, put)
        norm = jnp.zeros((1, cols), f32)
        row_dot = jnp.zeros((1, cols), f32)
        for lo in range(0, total, FAR_STEP):
            w = jnp.exp(pbuf[lo : lo + FAR_STEP] - top)
            gp = dot(vbuf[lo : lo + FAR_STEP], g2, NT)
            pbuf[lo : lo + FAR_STEP] = w
            dbuf[lo : lo + FAR_STEP] = gp
            norm = norm + jnp.sum(w, axis=0, keepdims=True)
            row_dot = row_dot + jnp.sum(w * gp, axis=0, keepdims=True)
        inv = 1.0 / norm
        row_dot = row_dot * inv
        gq_acc = jnp.zeros((n, cols), f32)
        ctx_acc = jnp.zeros((n, cols), f32)
        for lo in range(0, total, STEP):
            p = pbuf[lo : lo + STEP] * inv
            low = p.astype(bf16)
            ds = (p * (dbuf[lo : lo + STEP] - row_dot)).astype(bf16)
            ctx_acc = ctx_acc + dot(vbuf[lo : lo + STEP], low, TN)
            gq_acc = gq_acc + dot(kbuf[lo : lo + STEP], ds, TN)
            for which, x in ((0, dot(ds, q2, NN)), (1, dot(low, g2, NN))):
                if lo == 0:
                    prev_out[t, which] = x[0:128].astype(bf16)
                    own_out[t, which] = x[128:256]
                    next_out[t, which] = x[256:384].astype(bf16)
                else:
                    x = x.astype(bf16)
                    for i in range(STEP // BLK):
                        far_buf[to[(lo - STEP) // BLK + i], which * BLK : (which + 1) * BLK] = x[i * BLK : (i + 1) * BLK]

        plane = far_own.shape[0]
        for k, (out, rows) in enumerate(((here_out, pl.ds(0, plane)), (partner_out, pl.ds(plane, plane)))):
            to = out.at[:, 2 * t * BLK : 2 * (t + 1) * BLK]
            copies.append(pltpu.make_async_copy(far_buf.at[rows], to, sems.at[t, k]))
            copies[-1].start()
        gq_ref[t] = (pick_heads(gq_acc) * HD ** (-0.5)).astype(bf16)
        ctx = pick_heads(ctx_acc).astype(bf16)
        if t == 1:
            rev_ref[...] = flipped(ctx)
        else:
            ctx_ref[...] = ctx
    for copy in copies:
        copy.wait()


def combine(fb_ref, far_ref, asked_buf, rel, put):
    shard, shards, zh, y = place()
    asked_rows(fb_ref, asked_buf, rel)
    rows = 32
    for t in range(2):
        for which in range(2):
            for lo in range(0, BLK, rows):
                first = jnp.zeros((rows, 2 * HD), f32)
                second = jnp.zeros((rows, 2 * HD), f32)
                at = part(t, which).start + lo
                for p, reader in enumerate(plane_readers(zh)):
                    block = asked_by(asked_buf, t, reader, rows)
                    x = far_ref[p, at : at + rows].astype(f32)
                    first = first + jnp.where(block == 1, x, 0.0)
                    second = second + jnp.where(block == 2, x, 0.0)
                put(t, which, slice(lo, lo + rows), first)
                put(t, which, slice(BLK + lo, BLK + lo + rows), second)


def combine_partner_kernel(fb_ref, prev_ref, next_ref, far_ref, out_ref, asked_buf):
    shard, shards, zh, y = place()
    last = lax.axis_size("y") - 1

    def put(t, which, rows, far):
        far = far + jnp.where(y == 0, prev_ref[t, which, rows].astype(f32), 0.0)
        far = far + jnp.where(y == last, next_ref[t, which, rows].astype(f32), 0.0)
        out_ref[t, which, rows] = far.astype(bf16)

    combine(fb_ref, far_ref, asked_buf, 1, put)


def combine_own_kernel(fb_ref, own_ref, prev_ref, next_ref, other_ref, far_ref, gk_ref, gv_ref, asked_buf):
    shard, shards, zh, y = place()
    last = lax.axis_size("y") - 1

    def put(t, which, rows, far):
        total = own_ref[t, which, rows] + jnp.where(y == 0, 0.0, prev_ref[t, which, rows].astype(f32))
        total = total + jnp.where(y == last, 0.0, next_ref[t, which, rows].astype(f32))
        total = total + other_ref[t, which, rows].astype(f32) + far
        (gk_ref, gv_ref)[which][t, rows] = total.astype(bf16)

    combine(fb_ref, far_ref, asked_buf, 0, put)


def project_kernel(ctx_ref, back_ref, weight_ref, even_ref, odd_ref, sum_buf):
    total = (ctx_ref[...].astype(f32) + back_ref[...].astype(f32)).astype(bf16)
    count, rows, _ = sum_buf.shape
    for k in range(count):
        sum_buf[k] = total[k * rows : (k + 1) * rows]
    at = lax.axis_index("tp")
    blocks = jnp.concatenate([sum_buf[lax.bitwise_xor(at, j)] for j in range(count)], axis=0)
    out = dot(blocks, weight_ref[...], NN)
    for j in range(count):
        ref = (even_ref, odd_ref)[j % 2]
        ref[j // 2] = out[j * rows : (j + 1) * rows].astype(ref.dtype)


def smem():
    return pl.BlockSpec(memory_space=pltpu.SMEM)


def vmem():
    return pl.BlockSpec(memory_space=pltpu.VMEM)


def hbm():
    return pl.BlockSpec(memory_space=pltpu.HBM)


def shape(dims, dtype=bf16):
    return jax.ShapeDtypeStruct(dims, dtype)


def cost(flops, nbytes, exps=0):
    return pl.CostEstimate(flops=flops, bytes_accessed=nbytes, transcendentals=exps)


def swap(x, bit):
    count = lax.axis_size("tp")
    return lax.ppermute(x, "tp", [(i, i ^ bit) for i in range(count)])


def per_device(
    residual, queries, keys, values, slopes, out_weight, cotangent, far_blocks, far_count
):
    nx, nz, ny = (lax.axis_size(a) for a in SEQ)
    seq_count = nx * nz * ny
    tp_count = lax.axis_size("tp")
    tok_rows, width = queries.shape[1:]
    total_keys = 3 * tok_rows + far_blocks.shape[1] * BLK
    model = out_weight.shape[1]
    cols = 2 * tok_rows
    both = (2, 2, tok_rows, width)
    pieces = (tp_count, tok_rows // tp_count, width)
    slots = (nx * ny, 4 * BLK, width)

    def plane_a2a(x):
        return lax.all_to_all(x, ("x", "y"), split_axis=0, concat_axis=0, tiled=True)

    def z_swap(x):
        return lax.ppermute(x, "zh", [(i, nz - 1 - i) for i in range(nz)])

    lists = far_blocks.T
    asked = pltpu.VMEM((2, seq_count, 2 * HD), jnp.int32)
    packed = [asked, pltpu.VMEM(slots, bf16), pltpu.SemaphoreType.DMA((nx * ny // 4,))]
    outgoing, key_value, near_lists = pl.pallas_call(
        pack_own_kernel,
        out_shape=(pltpu.HBM(slots, bf16), shape(both), shape(lists.shape, jnp.int32)),
        in_specs=[hbm()] * 3,
        out_specs=(hbm(), vmem(), vmem()),
        scratch_shapes=packed
        + [pltpu.SemaphoreType.DMA((2, 2)), pltpu.SemaphoreType.DMA(())],
        cost_estimate=cost(500_000, 1_500_000),
        compiler_params=pltpu.CompilerParams(vmem_limit_bytes=LIMIT),
        name="pack_own",
    )(*(pltpu.with_memory_space_constraint(x, pltpu.HBM) for x in (lists, keys, values)))
    far_own = plane_a2a(outgoing)
    partner = z_swap(key_value)
    outgoing, to_up, to_down = pl.pallas_call(
        pack_partner_kernel,
        out_shape=(pltpu.HBM(slots, bf16), shape(both), shape(both)),
        in_specs=[vmem()] * 3,
        out_specs=(hbm(), vmem(), vmem()),
        scratch_shapes=packed,
        cost_estimate=cost(500_000, 1_500_000),
        compiler_params=pltpu.CompilerParams(vmem_limit_bytes=LIMIT),
        name="pack_partner",
    )(near_lists, key_value, partner)
    same_core = [cotangent] + [swap(cotangent, bit) for bit in (2, 4, 6)]
    other_core = swap(jnp.stack(same_core), 1)

    def flat(x, zh, y):
        return (x * nz + zh) * ny + y

    places = [(x, zh, y) for x in range(nx) for zh in range(nz) for y in range(ny)]
    up, down = [], []
    for x, zh, y in places:
        if y < ny - 1:
            up.append((flat(x, zh, y), flat(x, zh, y + 1)))
        elif zh == nz - 1:
            up.append((flat(x, zh, y), flat(x, zh, 0)))
        elif x < nx - 1:
            up.append((flat(x, zh, y), flat(x + 1, zh, 0)))
        if y > 0:
            down.append((flat(x, zh, y), flat(x, zh, y - 1)))
        elif zh == 0:
            down.append((flat(x, zh, y), flat(x, zh, ny - 1)))
        elif x > 0:
            down.append((flat(x, zh, y), flat(x - 1, zh, ny - 1)))
    mirror = [(i, seq_count - 1 - i) for i in range(seq_count)]
    from_prev = lax.ppermute(to_up, SEQ, up)
    from_next = lax.ppermute(to_down, SEQ, down)

    grad_context = pl.pallas_call(
        context_grad_kernel,
        out_shape=shape((tok_rows, width)),
        in_specs=[vmem()] * 6,
        out_specs=vmem(),
        scratch_shapes=[pltpu.VMEM(pieces, bf16)],
        cost_estimate=cost(34_000_000, 600_000),
        compiler_params=pltpu.CompilerParams(vmem_limit_bytes=LIMIT),
        name="context_grad",
    )(*same_core, other_core, out_weight)
    outgoing, grad_context = lax.optimization_barrier((outgoing, grad_context))
    far_partner = plane_a2a(outgoing)
    mirrored = lax.ppermute(grad_context, SEQ, mirror)

    square = shape((tok_rows, width))
    half = pltpu.VMEM((seq_count + 1, 2 * BLK, width), bf16)
    context_fwd, context_rev, grad_queries, own, before, after, partner_grads, here_grads = pl.pallas_call(
        attend_kernel,
        out_shape=(square, square, shape((2, tok_rows, width)), shape(both, f32), shape(both), shape(both))
        + (pltpu.HBM(slots, bf16),) * 2,
        in_specs=[smem(), hbm()] + [vmem()] * 8,
        out_specs=(vmem(),) * 6 + (hbm(),) * 2,
        scratch_shapes=[pltpu.VMEM((total_keys, width), bf16)] * 2
        + [pltpu.VMEM((total_keys, cols), f32)] * 2
        + [half, half, pltpu.SemaphoreType.DMA((2, 2)), pltpu.SMEM(slopes.shape, f32), pltpu.SemaphoreType.DMA(())],
        cost_estimate=cost(4_000_000_000, 8_000_000, 1_000_000),
        compiler_params=pltpu.CompilerParams(vmem_limit_bytes=LIMIT),
        name="attend",
    )(
        near_lists, pltpu.with_memory_space_constraint(slopes, pltpu.HBM), queries, key_value, from_prev, from_next, far_own, far_partner, grad_context, mirrored)
    context_back = lax.ppermute(context_rev, SEQ, mirror)

    returned_partner = plane_a2a(partner_grads)
    from_prev_grad = lax.ppermute(after, SEQ, [(b, a) for a, b in down])
    from_next_grad = lax.ppermute(before, SEQ, [(b, a) for a, b in up])
    here_grads, returned_partner, context_back = lax.optimization_barrier(
        (here_grads, returned_partner, context_back)
    )
    returned_own = plane_a2a(here_grads)
    other = pl.pallas_call(
        combine_partner_kernel,
        out_shape=shape(both),
        in_specs=[vmem()] * 4,
        out_specs=vmem(),
        scratch_shapes=[asked],
        cost_estimate=cost(2_000_000, 1_500_000),
        compiler_params=pltpu.CompilerParams(vmem_limit_bytes=LIMIT),
        name="combine_partner",
    )(near_lists, from_prev_grad, from_next_grad, returned_partner)
    other, context_back = lax.optimization_barrier((other, context_back))
    other = z_swap(other)

    even, odd = pl.pallas_call(
        project_kernel,
        out_shape=(
            shape((tp_count // 2, tok_rows // tp_count, model), f32),
            shape((tp_count // 2, tok_rows // tp_count, model)),
        ),
        in_specs=[vmem()] * 3,
        out_specs=(vmem(),) * 2,
        scratch_shapes=[pltpu.VMEM(pieces, bf16)],
        cost_estimate=cost(34_000_000, 1_000_000),
        compiler_params=pltpu.CompilerParams(vmem_limit_bytes=LIMIT),
        name="project",
    )(context_fwd, context_back, out_weight)
    held = even + swap(odd, 1).astype(f32)
    parts = [swap(held[k].astype(bf16), 2 * k) for k in range(1, tp_count // 2)]
    total = residual.astype(f32) + held[0]
    for part_here in parts:
        total = total + part_here.astype(f32)
    mixed = total.astype(bf16)

    grad_keys, grad_values = pl.pallas_call(
        combine_own_kernel,
        out_shape=(shape((2, tok_rows, width)),) * 2,
        in_specs=[vmem()] * 6,
        out_specs=(vmem(),) * 2,
        scratch_shapes=[asked],
        cost_estimate=cost(2_000_000, 1_500_000),
        compiler_params=pltpu.CompilerParams(vmem_limit_bytes=LIMIT),
        name="combine_own",
    )(near_lists, own, from_prev_grad, from_next_grad, other, returned_own)
    return (mixed, grad_queries, grad_keys, grad_values)


def solution(mesh):
    split = jax.sharding.Mesh(mesh.devices.reshape(4, 2, 4, -1), SEQ + ("tp",))
    rows = P(SEQ + ("tp",), None)
    strands = P(None, SEQ, "tp")
    return jax.shard_map(
        per_device,
        mesh=split,
        in_specs=(rows, strands, strands, strands, P("tp"), P("tp", None), rows, P(), P()),
        out_specs=(rows, strands, strands, strands),
        check_vma=False,
    )
```
